128 devices in a mesh: seq: 16 (over x_hi, y, core), tp: 8 (over x_lo, z).
Axes of the slice: x: 4 (x_hi: 2, x_lo: 2; x = x_hi * 2 + x_lo), y: 4, z: 4, core: 2. Of those that a mesh axis runs over, the one named last changes fastest.
Arguments:
- tokens: bfloat16 [8192, 1024], P('seq'), may hold values from -6 to 6
- segment_ids: int32 [8192], P('seq'), may hold values from 0 to 63, never falling along the last dimension, each value on 1 to 4608 neighbouring positions
- prefix_cache: bfloat16 [16384, 8, 128], P('seq', 'tp'), may hold values from -320 to 320
- norm1_gain: float32 [1024], replicated, may hold values from 0.5 to 1.5
- w_qkv: bfloat16 [1024, 8, 256], P(None, 'tp'), may hold values from -0.875 to 0.875
- w_out: bfloat16 [8, 128, 1024], P('tp'), may hold values from -0.1875 to 0.1875
- norm2_gain: float32 [1024], replicated, may hold values from 0.5 to 1.5
- expert_in: bfloat16 [32, 1024, 1024], P('seq'), may hold values from -0.1875 to 0.1875
- expert_out: bfloat16 [32, 512, 1024], P('seq'), may hold values from -0.25 to 0.25
- routes: int32 [8192, 8], P(('seq', 'tp')), may hold values from 0 to 31, all different within a row; in each aligned block of 64 rows (0 to 63, 64 to 127, ...) at most 32 rows name the same one
- route_weights: float32 [8192, 8], P(('seq', 'tp')), may hold values from 0.05 to 0.25
Outputs:
- hidden_out: bfloat16 [8192, 1024], P(('seq', 'tp'))
- new_cache: bfloat16 [8192, 8, 128], P('seq', 'tp')
The draws below stay inside these ranges and needn't reach their ends.
Inputs may be any that keep to these rules, and one draw needn't show every extreme that they name: `segment_ids`: 64 requests lie in order of their numbers, each on 1 to 4608 consecutive new tokens, one on exactly that many. `routes`: each row names 8 different experts; in the rows of one device (aligned blocks of 64 rows) no expert is named by more than 32 rows, a bound that some block reaches.
All inputs are finite; a program needn't handle non-finite values.
Results may differ from the reference program's by a relative error of at most 0.02.
The reference program's roundings to bfloat16 on the way (of `normed`, `queries`, `weights_b`, `attended`, `expert_input`, `expert_hidden` and `expert_output`) count: a program that leaves them out, or rounds other values in their place, can miss the bound.
Values may be sent and summed in bfloat16 or wider, within the bound.
No kernel may reach another device: no remote copies, remote signals or barrier semaphores. Data moves between devices by JAX's collectives and lax.ppermute only.
A program may use at most 128 MiB of HBM per device.

```python
import math
import jax
import jax.numpy as jnp
import numpy as np
from jax import lax

D = 1024
HEADS = 16
KV_HEADS = 8
HEAD_DIM = 64
FF = 512
EXPERTS = 32
TOPK = 8
TOK_DEV = 512
SEG_SPAN = 9
TOKENS = 8192
PREFIX = 16384
ROWS = 64
CAP = 32
REQUESTS = 64


def draw_prefix_cache(key, part):
    full_shape = (PREFIX, KV_HEADS, 2 * HEAD_DIM)
    normal_part = jax.random.normal(key, full_shape, jnp.float32) * 4.5
    return jnp.clip(normal_part, -27.0, 27.0).astype(jnp.bfloat16)


def level_of(rng, shape, split, low, top_value):
    def one(position, parts):
        draws = jax.random.uniform(jax.random.fold_in(jax.random.fold_in(rng, 6), position), (parts,), jnp.float32, low / len(split), top_value / len(split))
        return jnp.repeat(jnp.exp(draws), shape[position] // parts).reshape((-1,) + (1,) * (len(shape) - position - 1))

    level = one(*split[0])
    for cut in split[1:]:
        level = level * one(*cut)
    return level


def length_profile(amount, total, reach, lean):
    portions = [(1 << 20) // math.isqrt(grade ** lean) + 1 for grade in range(2, amount + 1)]
    rest, given = total - reach - (amount - 1), [1] * (amount - 1)
    while rest > 0:
        candidates = [i for i in range(amount - 1) if given[i] < reach]
        mass, left = sum([portions[i] for i in candidates]), rest
        for i in candidates:
            extra = min(reach - given[i], max(1, left * portions[i] // mass), rest)
            given[i] = given[i] + extra
            rest = rest - extra
    return np.array([reach] + given)


def uneven(key, count, total, most, skew):
    if count == 2:
        one = jax.random.randint(key, (), max(1, total - most), min(most, total - 1) + 1)
        return jnp.stack([one, total - one])
    lengths = jnp.asarray(length_profile(count, total, most, skew), jnp.int32)
    pairs = (count - 1) // 2
    giver, receiver = lengths[1:1 + 2 * pairs:2], lengths[2:2 + 2 * pairs:2]
    room = jnp.minimum(giver - 1, most - receiver)
    passed = jax.random.randint(jax.random.fold_in(key, 1), (pairs,), 0, 1 << 20) % (room + 1)
    lengths = lengths.at[1:1 + 2 * pairs:2].set(giver - passed).at[2:2 + 2 * pairs:2].set(receiver + passed)
    return lengths[jax.random.permutation(jax.random.fold_in(key, 2), count)]


def routed_block(own_key, own, number, rows, count, top, reach, slope):
    order = jax.random.permutation(own_key, count)
    packed, common = load_shares(count, rows * top, reach, slope, True), load_shares(count, rows * top, reach, slope, False)
    places = jnp.arange(count)

    def named(tallies, rotation):
        used = int((tallies > 0).sum())
        fixed = max(1, used // 4)
        passed = fixed + (places - fixed + rotation * (used - fixed)) % max(1, count - fixed)
        return jnp.zeros((count,), jnp.int32).at[order[jnp.where(places < fixed, places, passed)]].set(jnp.asarray(tallies, jnp.int32))

    tallies = jnp.where(number % 4 == 0, named(packed, number // 4), named(common, number - number // 4 - 1))
    mixed = jax.random.permutation(jax.random.fold_in(own, 3), count)
    donor, sink = mixed[0:count // 2 * 2:2], mixed[1:count // 2 * 2:2]
    margin = jnp.minimum(tallies[donor] - 1, reach - tallies[sink]) // 2
    margin = jnp.where((donor == order[0]) | (sink == order[0]) | (tallies[sink] == 0), 0, jnp.maximum(margin, 0))
    passed = jax.random.randint(jax.random.fold_in(own, 4), (count // 2,), 0, 1 << 20) % (margin + 1)
    tallies = tallies.at[donor].add(-passed).at[sink].add(passed)
    members = jnp.searchsorted(jnp.cumsum(tallies), jnp.arange(rows * top), side="right").astype(jnp.int32)
    grid = members.reshape(top, rows).T
    grid = grid[jax.random.permutation(jax.random.fold_in(own, 1), rows)]
    rotation = jax.random.randint(jax.random.fold_in(own, 2), (rows, 1), 0, top)
    return jnp.take_along_axis(grid, (jnp.arange(top)[None, :] + rotation) % top, axis=1)


def load_shares(amount, total, reach, slope, full):
    weights = [(1 << 20) // math.isqrt(standing ** slope) + 1 for standing in range(1, amount + 1)]
    largest = reach if full else min(reach, max(-(-total // amount), total * weights[0] // sum(weights)))
    least = 1 if total - largest >= amount - 1 else 0
    given, rest = [largest] + [least] * (amount - 1), total - largest - least * (amount - 1)
    while rest > 0:
        movable = [i for i in range(1, amount) if given[i] < largest] or [i for i in range(1, amount) if given[i] < reach]
        whole, left = sum([weights[i] for i in movable]), rest
        for i in movable:
            addition = min(reach - given[i], max(1, left * weights[i] // whole), rest)
            given[i] = given[i] + addition
            rest = rest - addition
    return np.array(given)


def scatter_about(key, shape, spread, reach, split=(), kind=jnp.bfloat16):
    factor_of = level_of(key, shape, split, -0.22, 0.18) if split else 1.0
    array = jax.random.normal(key, shape, jnp.float32) * spread * factor_of
    return jnp.minimum(jnp.maximum(array, -reach), reach).astype(kind)


def setup_inputs(seed: int = 0) -> dict:
    arg_keys = jax.random.split(jax.random.key(seed), 12)
    tokens = scatter_about(arg_keys[0], (TOKENS, D), 1.0, 6.0, ((0, 16),))
    segment_ids = jnp.searchsorted(jnp.cumsum(uneven(arg_keys[1], REQUESTS, TOKENS, SEG_SPAN * TOK_DEV, 2)), jnp.arange(TOKENS), side="right").astype(jnp.int32)
    prefix_cache = draw_prefix_cache(jax.random.fold_in(arg_keys[11], 71), 0)
    norm1_gain = jnp.clip(1.0 + 0.1 * jax.random.normal(arg_keys[3], (D,), jnp.float32), 0.5, 1.5)
    w_qkv = scatter_about(arg_keys[4], (D, KV_HEADS, (HEADS // KV_HEADS + 2) * HEAD_DIM), (D // 20) ** -0.5, 0.875, ((1, 8),))
    w_out = scatter_about(arg_keys[5], (KV_HEADS, (HEADS // KV_HEADS) * HEAD_DIM, D), (HEADS * HEAD_DIM) ** -0.5, 0.1875, ((0, 8),))
    norm2_gain = jnp.clip(1.0 + 0.1 * jax.random.normal(arg_keys[6], (D,), jnp.float32), 0.5, 1.5)
    expert_in = scatter_about(arg_keys[7], (EXPERTS, D, 2 * FF), D ** -0.5, 0.1875, ((0, 16),))
    expert_out = scatter_about(arg_keys[8], (EXPERTS, FF, D), FF ** -0.5, 0.25, ((0, 16),))
    routes_keys = jax.random.split(jax.random.fold_in(arg_keys[9], 1), TOKENS // ROWS)
    routes_turns = jax.random.permutation(jax.random.fold_in(arg_keys[9], 3), TOKENS // ROWS)
    routes = jax.vmap(lambda own, number: routed_block(jax.random.fold_in(arg_keys[9], 2), own, number, ROWS, EXPERTS, TOPK, CAP, 2))(routes_keys, routes_turns).reshape((TOKENS, TOPK))
    route_weights = jnp.clip(0.05 + 0.2 * jax.random.uniform(arg_keys[10], (TOKENS, TOPK), jnp.float32) ** level_of(arg_keys[10], (TOKENS, TOPK), ((0, 128),), -0.2, 0.2), 0.05, 0.25)
    return dict(tokens=tokens, segment_ids=segment_ids, prefix_cache=prefix_cache, norm1_gain=norm1_gain, w_qkv=w_qkv, w_out=w_out, norm2_gain=norm2_gain, expert_in=expert_in, expert_out=expert_out, routes=routes, route_weights=route_weights)


SCORE_SCALE = 0.015625
EPSILON = 1e-06

def normalize(inputs, norm_gain):
    widened = inputs.astype(jnp.float32)
    mean_square = lax.optimization_barrier(jnp.mean(widened * widened, axis=-1, keepdims=True))
    return widened * lax.rsqrt(mean_square + EPSILON) * norm_gain

def reference(tokens, segment_ids, prefix_cache, norm1_gain, w_qkv, w_out, norm2_gain, expert_in, expert_out, routes, route_weights):
    group_size = HEADS // KV_HEADS
    normed = normalize(tokens, norm1_gain).astype(jnp.bfloat16)
    projected = jnp.einsum('td,dkc->tkc', normed.astype(jnp.float32), w_qkv.astype(jnp.float32), precision=lax.Precision.HIGHEST)
    queries = projected[:, :, :group_size * HEAD_DIM].astype(jnp.bfloat16)
    new_cache = projected[:, :, group_size * HEAD_DIM:].astype(jnp.bfloat16)
    all_cache = jnp.concatenate([prefix_cache, new_cache], axis=0)
    block_len = math.gcd(TOKENS, 512)
    blocks = TOKENS // block_len
    positions = jnp.arange(TOKENS, dtype=jnp.int32)

    def per_head(member):
        query_head, cache_head = member
        key_head = cache_head[:, :HEAD_DIM].astype(jnp.float32)
        value_head = cache_head[:, HEAD_DIM:].astype(jnp.float32)

        def per_block(block):
            query_block, query_pos, query_seg = block
            query_wide = query_block.reshape(block_len, group_size, HEAD_DIM).astype(jnp.float32)
            scores = jnp.einsum('tgd,sd->tgs', query_wide, key_head, precision=lax.Precision.HIGHEST) * SCORE_SCALE
            suffix_ok = (segment_ids[None, :] == query_seg[:, None]) & (positions[None, :] <= query_pos[:, None])
            usable = jnp.concatenate([jnp.ones((block_len, PREFIX), dtype=bool), suffix_ok], axis=1)
            scores = jnp.where(usable[:, None, :], scores, -jnp.inf)
            row_max = lax.optimization_barrier(jnp.max(scores, axis=-1, keepdims=True))
            weights = jnp.exp(scores - row_max)
            denom = lax.optimization_barrier(jnp.sum(weights, axis=-1))
            weights_b = lax.optimization_barrier(weights.astype(jnp.bfloat16))
            mixed = jnp.einsum('tgs,sd->tgd', weights_b.astype(jnp.float32), value_head, precision=lax.Precision.HIGHEST)
            return (mixed / denom[..., None]).astype(jnp.bfloat16).reshape(block_len, group_size * HEAD_DIM)
        return lax.map(per_block, (query_head.reshape(blocks, block_len, group_size * HEAD_DIM), positions.reshape(blocks, block_len), segment_ids.reshape(blocks, block_len)))
    attended = lax.map(per_head, (jnp.transpose(queries, (1, 0, 2)), jnp.transpose(all_cache, (1, 0, 2))))
    attended = attended.reshape(KV_HEADS, TOKENS, group_size * HEAD_DIM)
    attended = jnp.transpose(attended, (1, 0, 2)).reshape(TOKENS, HEADS * HEAD_DIM)
    residual = tokens.astype(jnp.float32) + jnp.dot(attended, w_out.reshape(HEADS * HEAD_DIM, D), preferred_element_type=jnp.float32)
    expert_input = normalize(residual, norm2_gain).astype(jnp.bfloat16)
    padded = jnp.concatenate([expert_input, jnp.zeros((1, D), jnp.bfloat16)], axis=0)
    weight_pad = jnp.concatenate([route_weights, jnp.zeros((1, TOPK), jnp.float32)], axis=0)
    routes_pad = jnp.concatenate([routes, jnp.full((1, TOPK), -1, jnp.int32)], axis=0)

    def per_expert(total, expert_id):
        chosen = jnp.any(routes == expert_id, axis=1)
        row_index = jnp.nonzero(chosen, size=TOKENS // 2, fill_value=TOKENS)[0].astype(jnp.int32)
        chosen_rows = padded[row_index]
        joined = jnp.dot(chosen_rows, expert_in[expert_id], preferred_element_type=jnp.float32)
        expert_hidden = (jax.nn.silu(joined[:, :FF]) * joined[:, FF:]).astype(jnp.bfloat16)
        expert_output = jnp.dot(expert_hidden, expert_out[expert_id], preferred_element_type=jnp.float32).astype(jnp.bfloat16)
        gate_col = lax.optimization_barrier(jnp.sum(jnp.where(routes_pad[row_index] == expert_id, weight_pad[row_index], 0.0), axis=1))
        return (total.at[row_index].add(expert_output.astype(jnp.float32) * gate_col[:, None]), None)
    expert_sum, _ = lax.scan(per_expert, jnp.zeros((TOKENS + 1, D), jnp.float32), jnp.arange(EXPERTS, dtype=jnp.int32))
    hidden_out = (residual + expert_sum[:TOKENS]).astype(jnp.bfloat16)
    return (hidden_out, new_cache)
```

```python
import functools

import jax
import jax.numpy as jnp
from jax import lax
from jax.experimental import pallas as pl
from jax.experimental.pallas import tpu as pltpu
from jax.sharding import PartitionSpec as P

SCALE = 0.015625
EPS = 1e-06
HD = 64
NV = 80
TD = 512
PRE = 1024
ROWS = 64
TQ = 512
NQ = 2 * TD
SEG_AT = PRE + TD
GATE_AT = SEG_AT + 16
PAY = GATE_AT + ROWS
LIMIT = 60.0
NEG = -1e30
NT = (((1,), (1,)), ((), ()))
F32 = jnp.float32
BF = jnp.bfloat16


def seq_perm(move):
    return [
        (x * 8 + y * 2 + c, (lambda t: t[0] * 8 + t[1] * 2 + t[2])(move(x, y, c)))
        for x in range(2)
        for y in range(4)
        for c in range(2)
    ]


def tp_perm(move):
    return [(q * 4 + z, (lambda t: t[0] * 4 + t[1])(move(q, z))) for q in range(2) for z in range(4)]


CORE = seq_perm(lambda x, y, c: (x, y, 1 - c))
SHIFTS = [(0, 1), (0, 3), (1, 0), (0, 2), (1, 1), (1, 3), (1, 2)]
CHIP_GROUPS = [[x * 8 + y * 2 + c for x in range(2) for y in range(4)] for c in range(2)]


def rms(wide, gain):
    mean_square = jnp.mean(wide * wide, axis=-1, keepdims=True)
    return wide * lax.rsqrt(mean_square + EPS) * gain


def project_kernel(tok_ref, gain_ref, w_ref, pre_ref, seg_ref, gate_ref, pay_ref, q_ref, new_ref):
    normed = rms(tok_ref[...].astype(F32), gain_ref[...]).astype(BF)
    proj = jnp.dot(normed, w_ref[...], preferred_element_type=F32)
    pq = proj[:, :128].astype(BF).astype(F32) * SCALE
    low = lax.broadcasted_iota(jnp.int32, (TD, 128), 1) < HD
    q_ref[:TD, :] = jnp.where(low, pq, 0.0).astype(BF)
    q_ref[TD:, :] = jnp.where(low, pltpu.roll(pq, HD, 1), 0.0).astype(BF)
    new = proj[:, 128:].astype(BF)
    new_ref[...] = new
    pay_ref[:PRE, :] = pre_ref[...]
    pay_ref[PRE:SEG_AT, :] = new
    pay_ref[SEG_AT:GATE_AT, :] = seg_ref[...]
    pay_ref[GATE_AT:, :] = gate_ref[...]


def values_t(kv):
    row = lax.broadcasted_iota(jnp.int32, (NV, 128), 0)
    col = lax.broadcasted_iota(jnp.int32, (NV, 128), 1)
    pick = jnp.where((col == row + HD) & (row < HD), 1.0, 0.0).astype(BF)
    vt = lax.dot_general(pick, kv, NT, preferred_element_type=F32)
    ones = lax.broadcasted_iota(jnp.int32, vt.shape, 0) >= HD
    return jnp.where(ones, 1.0, vt).astype(BF)


def online_step(q, kv, o_ref, m_ref, cols, mask):
    s = lax.dot_general(kv, q, NT, preferred_element_type=F32)
    if mask is not None:
        s = jnp.where(mask, s, NEG)
    m0 = m_ref[0:1, cols]
    m1 = jnp.maximum(m0, jnp.max(s, axis=0, keepdims=True))
    p = jnp.exp(s - m1).astype(BF)
    o_ref[:, cols] = o_ref[:, cols] * jnp.exp(m0 - m1) + jnp.dot(
        values_t(kv), p, preferred_element_type=F32
    )
    m_ref[0:1, cols] = m1


def prefix_kernel(*refs, count, first):
    q_ref = refs[0]
    at = 1
    if not first:
        o_in, m_in = refs[1:3]
        at = 3
    pays = refs[at : at + count]
    o_ref, m_ref, buf, top, sem = refs[at + count :]
    for j in range(count):
        pltpu.make_async_copy(pays[j].at[pl.ds(0, PRE), :], buf.at[j], sem.at[j]).start()

    def wait(j):
        pltpu.make_async_copy(pays[0].at[pl.ds(0, PRE), :], buf.at[j], sem.at[j]).wait()

    def begin():
        if first:
            o_ref[...] = jnp.zeros_like(o_ref)
        else:
            o_ref[...] = o_in[...]
            m_ref[...] = m_in[...]

    begin()
    if first:
        wait(0)
        s = lax.dot_general(buf[0, :256, :], q_ref[...], NT, preferred_element_type=F32)
        m_ref[...] = jnp.broadcast_to(jnp.max(s, axis=0, keepdims=True), m_ref.shape)
    top[...] = jnp.full_like(top, NEG)

    def block(j, _):
        if first:
            pl.when(j > 0)(lambda: wait(j))
        else:
            wait(j)
        kv = buf[j]
        vt = values_t(kv)
        for t in range(NQ // TQ):
            cols = pl.ds(t * TQ, TQ)
            s = lax.dot_general(kv, q_ref[cols, :], NT, preferred_element_type=F32)
            top[0:1, cols] = jnp.maximum(top[0:1, cols], jnp.max(s, axis=0, keepdims=True))
            p = jnp.exp(s - m_ref[0:1, cols]).astype(BF)
            o_ref[:, cols] = o_ref[:, cols] + jnp.dot(vt, p, preferred_element_type=F32)
        return 0

    lax.fori_loop(0, count, block, 0)

    @pl.when(jnp.max(top[0:1, :] - m_ref[0:1, :]) > LIMIT)
    def _():
        begin()

        def again(i, _):
            kv = buf[i // 4, pl.ds(pl.multiple_of(i % 4 * 256, 256), 256), :]
            for t in range(NQ // 256):
                cols = pl.ds(t * 256, 256)
                online_step(q_ref[cols, :], kv, o_ref, m_ref, cols, None)
            return 0

        lax.fori_loop(0, count * 4, again, 0)


def prefix_call(q, state, pays):
    count = len(pays)
    first = state is None
    vm = pl.BlockSpec(memory_space=pltpu.VMEM)
    hbm = pl.BlockSpec(memory_space=pl.ANY)
    args = (q,) + (() if first else tuple(state)) + tuple(pays)
    return pl.pallas_call(
        functools.partial(prefix_kernel, count=count, first=first),
        in_specs=[vm] * (1 if first else 3) + [hbm] * count,
        out_specs=[vm, vm],
        out_shape=[jax.ShapeDtypeStruct((NV, NQ), F32), jax.ShapeDtypeStruct((8, NQ), F32)],
        scratch_shapes=[
            pltpu.VMEM((count, PRE, 128), BF),
            pltpu.VMEM((8, NQ), F32),
            pltpu.SemaphoreType.DMA((count,)),
        ],
        cost_estimate=pl.CostEstimate(
            flops=count * PRE * NQ * 2 * 600,
            bytes_accessed=count * PRE * 256 + NQ * 256 + NV * NQ * 8,
            transcendentals=count * PRE * NQ,
        ),
        name="prefix_attention",
    )(*args)


def suffix_kernel(src_ref, q_ref, o_in, m_in, qseg_ref, start_ref, *refs):
    pays = refs[:16]
    out_ref, o_ref, m_ref, buf, segs, top, sem = refs[16:]
    own = src_ref[0]
    for j in range(16):
        at = pl.multiple_of(src_ref[j] * TD, TD)
        pltpu.make_async_copy(pays[j].at[pl.ds(PRE, TD), :], buf.at[pl.ds(at, TD), :], sem.at[0, j]).start()
        pltpu.make_async_copy(pays[j].at[pl.ds(SEG_AT, 16), :], segs.at[j], sem.at[1, j]).start()
    for j in range(16):
        pltpu.make_async_copy(pays[j].at[pl.ds(SEG_AT, 16), :], segs.at[j], sem.at[1, j]).wait()
    mine = jnp.max(jnp.where(lax.broadcasted_iota(jnp.int32, (1, NQ), 1) == 0, qseg_ref[...], -1.0))
    count = jnp.zeros((16, 128), F32)
    for j in range(16):
        same = (segs[j].astype(F32) == mine) & (src_ref[j] < own)
        count = count + jnp.where(same, 1.0, 0.0)
    back = jnp.sum(count).astype(jnp.int32)
    begin_at = own * TD - back
    start = jnp.where(qseg_ref[...] == mine, begin_at, start_ref[...] + own * TD)
    for j in range(16):
        at = pl.multiple_of(src_ref[j] * TD, TD)
        pltpu.make_async_copy(pays[j].at[pl.ds(PRE, TD), :], buf.at[pl.ds(at, TD), :], sem.at[0, j]).wait()
    lane = lax.broadcasted_iota(jnp.int32, (1, NQ), 1)
    last = own * TD + jnp.where(lane >= TD, lane - TD, lane)
    o_ref[...] = o_in[...]
    m_ref[...] = m_in[...]
    top[...] = jnp.full_like(top, NEG)
    low = begin_at // TD

    def mask_of(at, size, cols, width):
        key = at + lax.broadcasted_iota(jnp.int32, (size, width), 0)
        return (key >= cols[0]) & (key <= cols[1])

    def block(b, _):
        at = pl.multiple_of(b * TD, TD)
        kv = buf[pl.ds(at, TD), :]
        vt = values_t(kv)
        for t in range(2):
            cols = pl.ds(t * TD, TD)
            s = lax.dot_general(kv, q_ref[cols, :], NT, preferred_element_type=F32)
            span = (start[:, t * TD : t * TD + TD], last[:, t * TD : t * TD + TD])
            s = jnp.where(mask_of(at, TD, span, TD), s, NEG)
            top[0:1, cols] = jnp.maximum(top[0:1, cols], jnp.max(s, axis=0, keepdims=True))
            p = jnp.exp(s - m_ref[0:1, cols]).astype(BF)
            o_ref[:, cols] = o_ref[:, cols] + jnp.dot(vt, p, preferred_element_type=F32)
        return 0

    lax.fori_loop(low, own + 1, block, 0)

    @pl.when(jnp.max(top[0:1, :] - m_ref[0:1, :]) > LIMIT)
    def _():
        o_ref[...] = o_in[...]
        m_ref[...] = m_in[...]

        def again(i, _):
            at = pl.multiple_of(i * 256, 256)
            kv = buf[pl.ds(at, 256), :]
            for t in range(4):
                cols = pl.ds(t * 256, 256)
                span = (start[:, t * 256 : t * 256 + 256], last[:, t * 256 : t * 256 + 256])
                online_step(q_ref[cols, :], kv, o_ref, m_ref, cols, mask_of(at, 256, span, 256))
            return 0

        lax.fori_loop(low * 2, own * 2 + 2, again, 0)

    total = o_ref[...]
    mixed = total[:HD, :] / total[HD : HD + 1, :]
    both = jnp.concatenate([mixed[:, :TD], mixed[:, TD:]], axis=0)
    out_ref[...] = jnp.transpose(both).astype(BF)


def suffix_call(src, q, state, qseg, start, pays):
    vm = pl.BlockSpec(memory_space=pltpu.VMEM)
    hbm = pl.BlockSpec(memory_space=pl.ANY)
    sm = pl.BlockSpec(memory_space=pltpu.SMEM)
    return pl.pallas_call(
        suffix_kernel,
        in_specs=[sm] + [vm] * 5 + [hbm] * 16,
        out_specs=vm,
        out_shape=jax.ShapeDtypeStruct((TD, 128), BF),
        scratch_shapes=[
            pltpu.VMEM((NV, NQ), F32),
            pltpu.VMEM((8, NQ), F32),
            pltpu.VMEM((16 * TD, 128), BF),
            pltpu.VMEM((16, 16, 128), BF),
            pltpu.VMEM((8, NQ), F32),
            pltpu.SemaphoreType.DMA((2, 16)),
        ],
        cost_estimate=pl.CostEstimate(
            flops=6 * TD * NQ * 2 * 600, bytes_accessed=16 * TD * 256, transcendentals=6 * TD * NQ
        ),
        name="suffix_attention",
    )(src, q, state[0], state[1], qseg, start, *pays)


def mix_kernel(order_ref, att_ref, tok_ref, gain_ref, w0, w1, w2, w3, w4, res_ref, xi_ref):
    total = tok_ref[...].astype(F32)
    parts = [w0.at[0], w1.at[0]] + [w.at[i] for w in (w2, w3, w4) for i in range(2)]
    acc = jnp.zeros((ROWS, 1024), F32)
    for j in range(8):
        acc = acc + jnp.dot(att_ref[order_ref[j + 1]], parts[j][...], preferred_element_type=F32)
    total = total + acc
    res_ref[...] = total
    xi_ref[...] = rms(total, gain_ref[...]).astype(BF)


def mix_call(order, att, tokens, gain, ws):
    def full(a):
        zeros = (0,) * a.ndim
        return pl.BlockSpec(a.shape, lambda i, o: zeros)

    out = pl.BlockSpec((ROWS, 1024), lambda i, o: (0, 0))
    return pl.pallas_call(
        mix_kernel,
        grid_spec=pltpu.PrefetchScalarGridSpec(
            num_scalar_prefetch=1,
            grid=(1,),
            in_specs=[full(att), pl.BlockSpec((ROWS, 1024), lambda i, o: (o[0], 0)), full(gain)]
            + [full(w) for w in ws],
            out_specs=[out, out],
        ),
        out_shape=[
            jax.ShapeDtypeStruct((ROWS, 1024), F32),
            jax.ShapeDtypeStruct((ROWS, 1024), BF),
        ],
        name="mix",
    )(order, att, tokens, gain, *ws)


def expert_kernel(num_ref, x_ref, wi_own, wi_peer, wo_own, wo_peer, *refs):
    gates = refs[:8]
    out_ref, acc, table = refs[8:]
    e = pl.program_id(0)

    @pl.when(e == 0)
    def _():
        for j in range(8):
            at = pl.multiple_of(num_ref[4 + j] * ROWS, ROWS)
            table[pl.ds(at, ROWS), :] = gates[j][...].astype(F32)

    def run(wi, wo, add):
        x = x_ref[...]
        joined = jnp.dot(x, wi[0], preferred_element_type=F32)
        g = joined[:, :512]
        hidden = (g / (1.0 + jnp.exp(-g)) * joined[:, 512:]).astype(BF)
        o = jnp.dot(hidden, wo[0], preferred_element_type=F32).astype(BF).astype(F32)
        lane = lax.broadcasted_iota(jnp.int32, (512, 128), 1)
        number = num_ref[e]
        hit = (lane == number) | (lane == number + 32)
        gate = jnp.sum(jnp.where(hit, table[...], 0.0), axis=1, keepdims=True)
        o = o * gate
        if add:
            acc[...] = acc[...] + o
        else:
            acc[...] = o

    pl.when(e == 0)(lambda: run(wi_own, wo_own, False))
    pl.when(e == 1)(lambda: run(wi_own, wo_own, True))
    pl.when(e >= 2)(lambda: run(wi_peer, wo_peer, True))

    @pl.when(e == 3)
    def _():
        out_ref[...] = acc[...].astype(BF)


def expert_call(numbers, x, wi_own, wi_peer, wo_own, wo_peer, pays):
    own = lambda e, n: (jnp.minimum(e, 1), 0, 0)
    peer = lambda e, n: (jnp.maximum(e - 2, 0), 0, 0)
    fixed = lambda e, n: (0, 0)
    return pl.pallas_call(
        expert_kernel,
        grid_spec=pltpu.PrefetchScalarGridSpec(
            num_scalar_prefetch=1,
            grid=(4,),
            in_specs=[
                pl.BlockSpec((512, 1024), fixed),
                pl.BlockSpec((1, 1024, 1024), own),
                pl.BlockSpec((1, 1024, 1024), peer),
                pl.BlockSpec((1, 512, 1024), own),
                pl.BlockSpec((1, 512, 1024), peer),
            ]
            + [pl.BlockSpec((ROWS, 128), fixed)] * 8,
            out_specs=pl.BlockSpec((512, 1024), fixed),
            scratch_shapes=[pltpu.VMEM((512, 1024), F32), pltpu.VMEM((512, 128), F32)],
        ),
        out_shape=jax.ShapeDtypeStruct((512, 1024), BF),
        name="experts",
    )(numbers, x, wi_own, wi_peer, wo_own, wo_peer, *pays)


def body(
    tokens,
    segment_ids,
    prefix_cache,
    norm1_gain,
    w_qkv,
    w_out,
    norm2_gain,
    expert_in,
    expert_out,
    routes,
    route_weights,
):
    seq = lax.axis_index("seq")
    tp = lax.axis_index("tp")
    x, y, c = seq // 8, seq // 2 % 4, seq % 2
    q4, z = tp // 4, tp % 4

    segf = segment_ids.astype(F32)
    seg_rows = jnp.concatenate([segf.reshape(4, 128), jnp.full((12, 128), -1.0, F32)]).astype(BF)
    local = jnp.sum((segment_ids[:, None] < segment_ids[None, :]).astype(jnp.int32), axis=0)
    start = jnp.concatenate([local, local])[None, :]
    qseg = jnp.concatenate([segf, segf])[None, :]
    dense = jnp.sum(
        jnp.where(
            routes[:, :, None] == jnp.arange(32, dtype=jnp.int32), route_weights[:, :, None], 0.0
        ),
        axis=1,
    )
    high = lax.reduce_precision(dense, 8, 7)
    gates = jnp.concatenate([high, dense - high, jnp.zeros((ROWS, 64), F32)], axis=1).astype(BF)

    pay, q, new = pl.pallas_call(
        project_kernel,
        out_shape=[
            jax.ShapeDtypeStruct((PAY, 128), BF),
            jax.ShapeDtypeStruct((NQ, 128), BF),
            jax.ShapeDtypeStruct((TD, 128), BF),
        ],
        name="project",
    )(
        tokens,
        norm1_gain[None, :],
        w_qkv.reshape(1024, 256),
        prefix_cache.reshape(PRE, 128),
        seg_rows,
        gates,
    )

    far = [
        lax.ppermute(
            pay, "seq", seq_perm(lambda a, b, d, i=i, j=j: ((a + i) % 2, (b + j) % 4, d))
        )
        for i, j in SHIFTS
    ]
    wi_peer = lax.ppermute(expert_in, "seq", CORE)
    wo_peer = lax.ppermute(expert_out, "seq", CORE)
    near = [lax.ppermute(p, "seq", CORE) for p in [pay] + far]
    wx = lax.ppermute(w_out, "tp", tp_perm(lambda a, b: (1 - a, b)))
    wpair = jnp.concatenate([w_out, wx])
    wz = [lax.ppermute(wpair, "tp", tp_perm(lambda a, b, k=k: (a, (b + k) % 4))) for k in (1, 3, 2)]

    state = prefix_call(q, None, [pay, near[0]])
    state = prefix_call(q, state, [p for k in range(3) for p in (far[k], near[k + 1])])
    state = prefix_call(q, state, [p for k in range(3, 7) for p in (far[k], near[k + 1])])
    chips = [(x, y)] + [((x - i) % 2, (y - j) % 4) for i, j in SHIFTS]
    same = [a * 8 + b * 2 + c for a, b in chips]
    other = [a * 8 + b * 2 + (1 - c) for a, b in chips]
    src = jnp.stack([v for pair in zip(same, other) for v in pair]).astype(jnp.int32)
    pays = [v for pair in zip([pay] + far, near) for v in pair]
    attended = suffix_call(src, q, state, qseg, start, pays)

    spread = lax.all_to_all(attended.reshape(8, ROWS, 128), "tp", 0, 0, tiled=True)
    heads = [q4 * 4 + z, (1 - q4) * 4 + z]
    for k in (1, 3, 2):
        heads += [q4 * 4 + (z - k) % 4, (1 - q4) * 4 + (z - k) % 4]
    order = jnp.stack([tp] + heads).astype(jnp.int32)
    residual, xi = mix_call(order, spread, tokens, norm2_gain[None, :], [w_out, wx] + wz)

    everyone = lax.all_to_all(
        jnp.broadcast_to(xi[None], (8, ROWS, 1024)),
        "seq",
        0,
        0,
        axis_index_groups=CHIP_GROUPS,
        tiled=True,
    )
    peer = x * 8 + y * 2 + (1 - c)
    numbers = jnp.stack(
        [seq * 2, seq * 2 + 1, peer * 2, peer * 2 + 1] + [a * 4 + b for a, b in chips]
    ).astype(jnp.int32)
    gate_parts = [p[GATE_AT:] for p in [pay] + far]
    partial = expert_call(
        numbers, everyone.reshape(512, 1024), expert_in, wi_peer, expert_out, wo_peer, gate_parts
    )
    returned = lax.all_to_all(
        partial.reshape(8, ROWS, 1024), "seq", 0, 0, axis_index_groups=CHIP_GROUPS, tiled=True
    )
    hidden = (residual + jnp.sum(returned.astype(F32), axis=0)).astype(BF)
    return hidden, new.reshape(TD, 1, 128)


def solution(mesh):
    in_specs = (
        P("seq", None),
        P("seq"),
        P("seq", "tp", None),
        P(),
        P(None, "tp", None),
        P("tp", None, None),
        P(),
        P("seq", None, None),
        P("seq", None, None),
        P(("seq", "tp"), None),
        P(("seq", "tp"), None),
    )
    out_specs = (P(("seq", "tp"), None), P("seq", "tp", None))
    return jax.shard_map(body, mesh=mesh, in_specs=in_specs, out_specs=out_specs, check_vma=False)
```

```python
import functools

import jax
import jax.numpy as jnp
from jax import lax
from jax.experimental import pallas as pl
from jax.experimental.pallas import tpu as pltpu
from jax.sharding import PartitionSpec as P

SCALE = 0.015625
EPS = 1e-06
HD = 64
NV = 80
TD = 512
PRE = 1024
ROWS = 64
TQ = 512
NQ = 2 * TD
GATE_AT = PRE + TD
SEG_AT = GATE_AT + ROWS
PAY = SEG_AT + 16
LIMIT = 1e26
NEG = -1e30
NT = (((1,), (1,)), ((), ()))
F32 = jnp.float32
BF = jnp.bfloat16


def seq_perm(move):
    return [
        (x * 8 + y * 2 + c, (lambda t: t[0] * 8 + t[1] * 2 + t[2])(move(x, y, c)))
        for x in range(2)
        for y in range(4)
        for c in range(2)
    ]


def tp_perm(move):
    return [(q * 4 + z, (lambda t: t[0] * 4 + t[1])(move(q, z))) for q in range(2) for z in range(4)]


CORE = seq_perm(lambda x, y, c: (x, y, 1 - c))
SHIFTS = [((0, 1), (0, 3)), ((1, 0), (0, 2)), ((1, 1), (1, 3)), ((1, 2), (1, 2))]
CHIP_GROUPS = [[x * 8 + y * 2 + c for x in range(2) for y in range(4)] for c in range(2)]


def rms(wide, gain):
    mean_square = jnp.mean(wide * wide, axis=-1, keepdims=True)
    return wide * lax.rsqrt(mean_square + EPS) * gain


def project_kernel(
    tok_ref, gain_ref, w_ref, pre_ref, seg_ref, route_ref, weight_ref, pay_ref, q_ref, new_ref
):
    normed = rms(tok_ref[...].astype(F32), gain_ref[...]).astype(BF)
    proj = jnp.dot(normed, w_ref[...], preferred_element_type=F32)
    pq = proj[:, :128].astype(BF).astype(F32) * SCALE
    low = lax.broadcasted_iota(jnp.int32, (TD, 128), 1) < HD
    q_ref[:TD, :] = jnp.where(low, pq, 0.0).astype(BF)
    q_ref[TD:, :] = jnp.where(low, pltpu.roll(pq, HD, 1), 0.0).astype(BF)
    new = proj[:, 128:].astype(BF)
    new_ref[...] = new
    pay_ref[:PRE, :] = pre_ref[...]
    pay_ref[PRE:GATE_AT, :] = new
    lane = lax.broadcasted_iota(jnp.int32, (ROWS, 128), 1)
    table = jnp.zeros((ROWS, 128), F32)
    for k in range(8):
        expert = route_ref[:, k : k + 1]
        weight = weight_ref[:, k : k + 1]
        high = weight.astype(BF).astype(F32)
        table = table + jnp.where(lane == expert, high, 0.0)
        table = table + jnp.where(lane == expert + 32, weight - high, 0.0)
    pay_ref[GATE_AT:SEG_AT, :] = table.astype(BF)
    segs = jnp.concatenate([seg_ref[...].astype(F32), jnp.full((12, 128), -1.0, F32)], axis=0)
    pay_ref[SEG_AT:, :] = segs.astype(BF)


def values_t(kv):
    row = lax.broadcasted_iota(jnp.int32, (NV, 128), 0)
    col = lax.broadcasted_iota(jnp.int32, (NV, 128), 1)
    pick = jnp.where((col == row + HD) & (row < HD), 1.0, 0.0).astype(BF)
    vt = lax.dot_general(pick, kv, NT, preferred_element_type=F32)
    ones = lax.broadcasted_iota(jnp.int32, vt.shape, 0) >= HD
    return jnp.where(ones, 1.0, vt).astype(BF)


def online_step(q, kv, o_ref, m_ref, cols, mask):
    s = lax.dot_general(kv, q, NT, preferred_element_type=F32)
    if mask is not None:
        s = jnp.where(mask, s, NEG)
    m0 = m_ref[0:1, cols]
    m1 = jnp.maximum(m0, jnp.max(s, axis=0, keepdims=True))
    p = jnp.exp(s - m1).astype(BF)
    o_ref[:, cols] = o_ref[:, cols] * jnp.exp(m0 - m1) + jnp.dot(
        values_t(kv), p, preferred_element_type=F32
    )
    m_ref[0:1, cols] = m1


def pieces(ref, which, rows):
    if len(ref.shape) == 2:
        return [ref.at[rows, :]]
    return [ref.at[i, rows, :] for i in which]


def prefix_kernel(*refs, shapes, first):
    q_ref = refs[0]
    at = 1
    if not first:
        o_in, m_in = refs[1:3]
        at = 3
    pays = refs[at : at + len(shapes)]
    o_ref, m_ref, buf, sem = refs[at + len(shapes) :]
    parts = [v for p in pays for v in pieces(p, (0, 1), pl.ds(0, PRE))]
    count = len(parts)
    for j in range(count):
        pltpu.make_async_copy(parts[j], buf.at[j], sem.at[j]).start()

    def wait(j):
        pltpu.make_async_copy(parts[0], buf.at[j], sem.at[j]).wait()

    def begin():
        if first:
            o_ref[...] = jnp.zeros_like(o_ref)
        else:
            o_ref[...] = o_in[...]
            m_ref[...] = m_in[...]

    begin()
    if first:
        wait(0)
        s = lax.dot_general(buf[0, :256, :], q_ref[...], NT, preferred_element_type=F32)
        m_ref[...] = jnp.broadcast_to(jnp.max(s, axis=0, keepdims=True), m_ref.shape)

    def block(j, _):
        if first:
            pl.when(j > 0)(lambda: wait(j))
        else:
            wait(j)
        kv = buf[j]
        vt = values_t(kv)
        for t in range(NQ // TQ):
            cols = pl.ds(t * TQ, TQ)
            s = lax.dot_general(kv, q_ref[cols, :], NT, preferred_element_type=F32)
            p = jnp.exp(s - m_ref[0:1, cols]).astype(BF)
            o_ref[:, cols] = o_ref[:, cols] + jnp.dot(vt, p, preferred_element_type=F32)
        return 0

    lax.fori_loop(0, count, block, 0)

    @pl.when(jnp.logical_not(jnp.max(o_ref[HD : HD + 1, :]) < LIMIT))
    def _():
        begin()
        if first:
            m_ref[...] = jnp.full_like(m_ref, NEG)

        def again(i, _):
            kv = buf[i // 4, pl.ds(pl.multiple_of(i % 4 * 256, 256), 256), :]
            for t in range(NQ // 256):
                cols = pl.ds(t * 256, 256)
                online_step(q_ref[cols, :], kv, o_ref, m_ref, cols, None)
            return 0

        lax.fori_loop(0, count * 4, again, 0)


def prefix_call(q, state, pays):
    shapes = [p.shape for p in pays]
    count = sum(1 if len(v) == 2 else 2 for v in shapes)
    first = state is None
    vm = pl.BlockSpec(memory_space=pltpu.VMEM)
    hbm = pl.BlockSpec(memory_space=pl.ANY)
    args = (q,) + (() if first else tuple(state)) + tuple(pays)
    return pl.pallas_call(
        functools.partial(prefix_kernel, shapes=shapes, first=first),
        in_specs=[vm] * (1 if first else 3) + [hbm] * len(shapes),
        out_specs=[vm, vm],
        out_shape=[jax.ShapeDtypeStruct((NV, NQ), F32), jax.ShapeDtypeStruct((8, NQ), F32)],
        scratch_shapes=[pltpu.VMEM((count, PRE, 128), BF), pltpu.SemaphoreType.DMA((count,))],
        cost_estimate=pl.CostEstimate(
            flops=count * PRE * NQ * 2 * 600,
            bytes_accessed=count * PRE * 256 + NQ * 256 + NV * NQ * 8,
            transcendentals=count * PRE * NQ,
        ),
        name="prefix_attention",
    )(*args)


def place():
    seq = lax.axis_index("seq")
    return seq // 8, lax.rem(seq // 2, 4), lax.rem(seq, 2)


def behind(x, y, c, k):
    a, b = SHIFTS[k]
    i = jnp.where(c == 0, a[0], b[0])
    j = jnp.where(c == 0, a[1], b[1])
    return lax.rem(x - i + 2, 2), lax.rem(y - j + 4, 4)


def sources():
    x, y, c = place()
    d = 1 - c
    out = [x * 8 + y * 2 + c, x * 8 + y * 2 + d]
    for k in range(4):
        a, b = behind(x, y, c, k)
        e, f = behind(x, y, d, k)
        far, near = a * 8 + b * 2, e * 8 + f * 2
        out += [far + c, far + d, near + d, near + c] if k < 3 else [far + c, near + d]
    return out


def suffix_kernel(q_ref, o_in, m_in, qseg_ref, start_ref, *refs):
    out_ref, o_ref, m_ref, buf, segs, sem = refs[10:]
    src = sources()
    own = src[0]
    news = [v for p in refs[:10] for v in pieces(p, (0, 1), pl.ds(PRE, TD))]
    marks = [v for p in refs[:10] for v in pieces(p, (0, 1), pl.ds(SEG_AT, 16))]
    copies = []
    for j in range(16):
        at = pl.multiple_of(src[j] * TD, TD)
        copies.append(pltpu.make_async_copy(marks[j], segs.at[j], sem.at[1, j]))
        copies.append(pltpu.make_async_copy(news[j], buf.at[pl.ds(at, TD), :], sem.at[0, j]))
    for v in copies:
        v.start()
    for v in copies[::2]:
        v.wait()
    mine = jnp.max(jnp.where(lax.broadcasted_iota(jnp.int32, (1, NQ), 1) == 0, qseg_ref[...], -1.0))
    count = jnp.zeros((16, 128), F32)
    for j in range(16):
        same = (segs[j].astype(F32) == mine) & (src[j] < own)
        count = count + jnp.where(same, 1.0, 0.0)
    back = jnp.sum(count).astype(jnp.int32)
    begin_at = own * TD - back
    start = jnp.where(qseg_ref[...] == mine, begin_at, start_ref[...] + own * TD)
    for v in copies[1::2]:
        v.wait()
    lane = lax.broadcasted_iota(jnp.int32, (1, NQ), 1)
    last = own * TD + jnp.where(lane >= TD, lane - TD, lane)
    o_ref[...] = o_in[...]
    m_ref[...] = m_in[...]
    low = begin_at // TD
    latest = jnp.max(start)

    def mask_of(at, size, cols, width):
        key = at + lax.broadcasted_iota(jnp.int32, (size, width), 0)
        return (key >= cols[0]) & (key <= cols[1])

    def block(b, masked):
        at = pl.multiple_of(b * TD, TD)
        kv = buf[pl.ds(at, TD), :]
        vt = values_t(kv)
        for t in range(2):
            cols = pl.ds(t * TD, TD)
            s = lax.dot_general(kv, q_ref[cols, :], NT, preferred_element_type=F32)
            if masked:
                span = (start[:, t * TD : t * TD + TD], last[:, t * TD : t * TD + TD])
                s = jnp.where(mask_of(at, TD, span, TD), s, NEG)
            p = jnp.exp(s - m_ref[0:1, cols]).astype(BF)
            o_ref[:, cols] = o_ref[:, cols] + jnp.dot(vt, p, preferred_element_type=F32)

    def step(b, _):
        whole = (latest <= b * TD) & (b < own)
        pl.when(whole)(lambda: block(b, False))
        pl.when(jnp.logical_not(whole))(lambda: block(b, True))
        return 0

    lax.fori_loop(low, own + 1, step, 0)

    @pl.when(jnp.logical_not(jnp.max(o_ref[HD : HD + 1, :]) < LIMIT))
    def _():
        o_ref[...] = o_in[...]
        m_ref[...] = m_in[...]

        def again(i, _):
            at = pl.multiple_of(i * 256, 256)
            kv = buf[pl.ds(at, 256), :]
            for t in range(4):
                cols = pl.ds(t * 256, 256)
                span = (start[:, t * 256 : t * 256 + 256], last[:, t * 256 : t * 256 + 256])
                online_step(q_ref[cols, :], kv, o_ref, m_ref, cols, mask_of(at, 256, span, 256))
            return 0

        lax.fori_loop(low * 2, own * 2 + 2, again, 0)

    total = o_ref[...]
    mixed = total[:HD, :] / total[HD : HD + 1, :]
    both = jnp.concatenate([mixed[:, :TD], mixed[:, TD:]], axis=0)
    out_ref[...] = jnp.transpose(both).astype(BF)


def suffix_call(q, state, qseg, start, pays):
    vm = pl.BlockSpec(memory_space=pltpu.VMEM)
    hbm = pl.BlockSpec(memory_space=pl.ANY)
    return pl.pallas_call(
        suffix_kernel,
        in_specs=[vm] * 5 + [hbm] * 10,
        out_specs=vm,
        out_shape=jax.ShapeDtypeStruct((TD, 128), BF),
        scratch_shapes=[
            pltpu.VMEM((NV, NQ), F32),
            pltpu.VMEM((8, NQ), F32),
            pltpu.VMEM((16 * TD, 128), BF),
            pltpu.VMEM((16, 16, 128), BF),
            pltpu.SemaphoreType.DMA((2, 16)),
        ],
        cost_estimate=pl.CostEstimate(
            flops=6 * TD * NQ * 2 * 600, bytes_accessed=16 * TD * 256, transcendentals=6 * TD * NQ
        ),
        name="suffix_attention",
    )(q, state[0], state[1], qseg, start, *pays)


def mix_kernel(att_ref, tok_hbm, gain_ref, w0, w1, w2, w3, w4, res_ref, xi_ref, tok, sem):
    tp = lax.axis_index("tp")
    fetch = pltpu.make_async_copy(
        tok_hbm.at[pl.ds(pl.multiple_of(tp * ROWS, ROWS), ROWS), :], tok, sem
    )
    fetch.start()
    q, z = tp // 4, lax.rem(tp, 4)
    parts = [w0.at[0], w1.at[0]] + [w.at[i] for w in (w2, w3, w4) for i in range(2)]
    total = jnp.zeros((ROWS, 1024), F32)
    for j in range(8):
        head = (q if j % 2 == 0 else 1 - q) * 4 + lax.rem(z - (0, 1, 3, 2)[j // 2] + 4, 4)
        total = total + jnp.dot(att_ref[head], parts[j][...], preferred_element_type=F32)
    fetch.wait()
    total = tok[...].astype(F32) + total
    res_ref[...] = total
    xi = rms(total, gain_ref[...]).astype(BF)
    for j in range(8):
        xi_ref[j] = xi


def mix_call(att, tokens, gain, ws):
    vm = pl.BlockSpec(memory_space=pltpu.VMEM)
    return pl.pallas_call(
        mix_kernel,
        in_specs=[vm, pl.BlockSpec(memory_space=pl.ANY), vm] + [vm] * 5,
        out_specs=[vm, vm],
        out_shape=[
            jax.ShapeDtypeStruct((ROWS, 1024), F32),
            jax.ShapeDtypeStruct((8, ROWS, 1024), BF),
        ],
        scratch_shapes=[pltpu.VMEM((ROWS, 1024), BF), pltpu.SemaphoreType.DMA],
        name="mix",
    )(att, tokens, gain, *ws)


def expert_kernel(x_ref, wi_own, wi_peer, wo_own, wo_peer, *refs):
    gates = refs[:8]
    out_ref, acc, table = refs[8:]
    e = pl.program_id(0)
    x, y, c = place()

    @pl.when(e == 0)
    def _():
        chips = [(x, y)]
        for k in range(4):
            chips += [behind(x, y, c, k), behind(x, y, 1 - c, k)]
        for j in range(8):
            at = pl.multiple_of((chips[j][0] * 4 + chips[j][1]) * ROWS, ROWS)
            part = gates[j][...] if len(gates[j].shape) == 2 else gates[j][0]
            table[pl.ds(at, ROWS), :] = part.astype(F32)

    def run(wi, wo, add):
        joined = jnp.dot(x_ref[...], wi[0], preferred_element_type=F32)
        g = joined[:, :512]
        hidden = (g / (1.0 + jnp.exp(-g)) * joined[:, 512:]).astype(BF)
        o = jnp.dot(hidden, wo[0], preferred_element_type=F32).astype(BF).astype(F32)
        lane = lax.broadcasted_iota(jnp.int32, (512, 128), 1)
        side = jnp.where(e < 2, c, 1 - c)
        number = (x * 8 + y * 2 + side) * 2 + lax.rem(e, 2)
        hit = (lane == number) | (lane == number + 32)
        gate = jnp.sum(jnp.where(hit, table[...], 0.0), axis=1, keepdims=True)
        o = o * gate
        if add:
            acc[...] = acc[...] + o
        else:
            acc[...] = o

    pl.when(e == 0)(lambda: run(wi_own, wo_own, False))
    pl.when(e == 1)(lambda: run(wi_own, wo_own, True))
    pl.when(e >= 2)(lambda: run(wi_peer, wo_peer, True))

    @pl.when(e == 3)
    def _():
        out_ref[...] = acc[...].astype(BF)


def expert_call(x, wi_own, wi_peer, wo_own, wo_peer, pays):
    own = lambda e: (jnp.minimum(e, 1), 0, 0)
    peer = lambda e: (jnp.maximum(e - 2, 0), 0, 0)
    flat = pl.BlockSpec((ROWS, 128), lambda e: (GATE_AT // ROWS, 0))

    def pair(i):
        return pl.BlockSpec((1, ROWS, 128), lambda e: (i, GATE_AT // ROWS, 0))

    return pl.pallas_call(
        expert_kernel,
        grid=(4,),
        in_specs=[
            pl.BlockSpec((512, 1024), lambda e: (0, 0)),
            pl.BlockSpec((1, 1024, 1024), own),
            pl.BlockSpec((1, 1024, 1024), peer),
            pl.BlockSpec((1, 512, 1024), own),
            pl.BlockSpec((1, 512, 1024), peer),
            flat,
        ]
        + [pair(i) for _ in range(3) for i in range(2)]
        + [flat],
        out_specs=pl.BlockSpec((512, 1024), lambda e: (0, 0)),
        scratch_shapes=[pltpu.VMEM((512, 1024), F32), pltpu.VMEM((512, 128), F32)],
        out_shape=jax.ShapeDtypeStruct((512, 1024), BF),
        name="experts",
    )(x, wi_own, wi_peer, wo_own, wo_peer, *pays)


def body(
    tokens,
    segment_ids,
    prefix_cache,
    norm1_gain,
    w_qkv,
    w_out,
    norm2_gain,
    expert_in,
    expert_out,
    routes,
    route_weights,
):
    pay, q, new = pl.pallas_call(
        project_kernel,
        out_shape=[
            jax.ShapeDtypeStruct((PAY, 128), BF),
            jax.ShapeDtypeStruct((NQ, 128), BF),
            jax.ShapeDtypeStruct((TD, 128), BF),
        ],
        name="project",
    )(
        tokens,
        norm1_gain[None, :],
        w_qkv.reshape(1024, 256),
        prefix_cache.reshape(PRE, 128),
        segment_ids.reshape(4, 128),
        routes,
        route_weights,
    )
    tie = lax.optimization_barrier

    wx = lax.ppermute(w_out, "tp", tp_perm(lambda a, b: (1 - a, b)))
    near0 = lax.ppermute(pay, "seq", CORE)
    state = prefix_call(q, None, [pay])
    near0, wx, state = tie((near0, wx, state))
    pair = jnp.stack([pay, near0])

    def ahead(k):
        return seq_perm(
            lambda a, b, d: ((a + SHIFTS[k][d][0]) % 2, (b + SHIFTS[k][d][1]) % 4, d)
        )

    far = [lax.ppermute(pair, "seq", ahead(k)) for k in range(3)]
    far.append(lax.ppermute(pay, "seq", ahead(3)))
    segment_ids, state = tie((segment_ids, state))
    segf = segment_ids.astype(F32)
    local = jnp.sum((segment_ids[:, None] < segment_ids[None, :]).astype(jnp.int32), axis=0)
    start = jnp.concatenate([local, local])[None, :]
    qseg = jnp.concatenate([segf, segf])[None, :]
    state = prefix_call(q, state, [near0])

    far[0], far[1], state = tie((far[0], far[1], state))
    near = [lax.ppermute(far[k], "seq", CORE) for k in range(2)]
    wpair = jnp.concatenate([w_out, wx])
    wz = [lax.ppermute(wpair, "tp", tp_perm(lambda a, b, k=k: (a, (b + k) % 4))) for k in (1, 3, 2)]
    state = prefix_call(q, state, [far[0], far[1]])
    near[0], near[1], far[2], far[3], state = tie((near[0], near[1], far[2], far[3], state))
    near += [lax.ppermute(far[k], "seq", CORE) for k in range(2, 4)]
    state = prefix_call(q, state, [near[0], near[1], far[2], far[3]])
    expert_in, expert_out, state = tie((expert_in, expert_out, state))
    wi_peer = lax.ppermute(expert_in, "seq", CORE)
    wo_peer = lax.ppermute(expert_out, "seq", CORE)
    state = prefix_call(q, state, [near[2], near[3]])
    pays = [pay, near0] + [v for k in range(4) for v in (far[k], near[k])]
    attended = suffix_call(q, state, qseg, start, pays)

    spread = lax.all_to_all(attended.reshape(8, ROWS, 128), "tp", 0, 0, tiled=True)
    residual, copies = mix_call(spread, tokens, norm2_gain[None, :], [w_out, wx] + wz)
    everyone = lax.all_to_all(copies, "seq", 0, 0, axis_index_groups=CHIP_GROUPS, tiled=True)
    partial = expert_call(
        everyone.reshape(512, 1024),
        expert_in,
        wi_peer,
        expert_out,
        wo_peer,
        [pay, far[0], near[0], far[1], near[1], far[2], near[2], far[3]],
    )
    returned = lax.all_to_all(
        partial.reshape(8, ROWS, 1024), "seq", 0, 0, axis_index_groups=CHIP_GROUPS, tiled=True
    )
    hidden = (residual + jnp.sum(returned.astype(F32), axis=0)).astype(BF)
    return hidden, new.reshape(TD, 1, 128)


def solution(mesh):
    in_specs = (
        P("seq", None),
        P("seq"),
        P("seq", "tp", None),
        P(),
        P(None, "tp", None),
        P("tp", None, None),
        P(),
        P("seq", None, None),
        P("seq", None, None),
        P(("seq", "tp"), None),
        P(("seq", "tp"), None),
    )
    out_specs = (P(("seq", "tp"), None), P("seq", "tp", None))
    return jax.shard_map(body, mesh=mesh, in_specs=in_specs, out_specs=out_specs, check_vma=False)
```

```python
import functools

import jax
import jax.numpy as jnp
from jax import lax
from jax.experimental import pallas as pl
from jax.experimental.pallas import tpu as pltpu
from jax.sharding import PartitionSpec as P

SCALE = 0.015625
EPS = 1e-06
HD = 64
NV = 80
TD = 512
PRE = 1024
ROWS = 64
TQ = 512
NQ = 2 * TD
SEG_AT = TD
PAY = SEG_AT + 16
MSG = 72
LIMIT = 1e26
NEG = -1e30
NT = (((1,), (1,)), ((), ()))
F32 = jnp.float32
BF = jnp.bfloat16


def seq_perm(move):
    return [
        (x * 8 + y * 2 + c, (lambda t: t[0] * 8 + t[1] * 2 + t[2])(move(x, y, c)))
        for x in range(2)
        for y in range(4)
        for c in range(2)
    ]


def tp_perm(move):
    return [(q * 4 + z, (lambda t: t[0] * 4 + t[1])(move(q, z))) for q in range(2) for z in range(4)]


CORE = seq_perm(lambda x, y, c: (x, y, 1 - c))
ACROSS = seq_perm(lambda x, y, c: (1 - x, y, c))
TURNS = (1, 3, 2)
SIDES = [
    (s * 8 + q * 4 + z, s * 8 + q * 4 + (z + (1 if s % 2 == 0 else 3)) % 4)
    for s in range(16)
    for q in range(2)
    for z in range(4)
]
CHIP_GROUPS = [[x * 8 + y * 2 + c for x in range(2) for y in range(4)] for c in range(2)]


def rms(wide, gain):
    mean_square = jnp.mean(wide * wide, axis=-1, keepdims=True)
    return wide * lax.rsqrt(mean_square + EPS) * gain


def project_kernel(tok_ref, gain_ref, w_ref, seg_ref, pay_ref, ask_ref, row_ref, new_ref):
    normed = rms(tok_ref[...].astype(F32), gain_ref[...]).astype(BF)
    proj = jnp.dot(normed, w_ref[...], preferred_element_type=F32)
    ask_ref[:TD, :] = (proj[:, :128].astype(BF).astype(F32) * SCALE).astype(BF)
    new = proj[:, 128:].astype(BF)
    new_ref[...] = new
    pay_ref[:TD, :] = new
    seg = seg_ref[...].astype(F32)
    segs = jnp.concatenate([seg, jnp.full((12, 128), -1.0, F32)], axis=0).astype(BF)
    pay_ref[SEG_AT:, :] = segs
    ask_ref[SEG_AT:, :] = segs
    row = jnp.concatenate([seg[k : k + 1, :] for k in range(4)], axis=1)
    col = jnp.transpose(jnp.broadcast_to(row, (8, TD)))[:, 0:1]
    below = jnp.sum(jnp.where(col < row, 1.0, 0.0), axis=0, keepdims=True)
    row_ref[0:1, :] = jnp.concatenate([below, below], axis=1)
    row_ref[1:2, :] = jnp.concatenate([row, row], axis=1)


def values_t(kv):
    row = lax.broadcasted_iota(jnp.int32, (NV, 128), 0)
    col = lax.broadcasted_iota(jnp.int32, (NV, 128), 1)
    pick = jnp.where((col == row + HD) & (row < HD), 1.0, 0.0).astype(BF)
    vt = lax.dot_general(pick, kv, NT, preferred_element_type=F32)
    ones = lax.broadcasted_iota(jnp.int32, vt.shape, 0) >= HD
    return jnp.where(ones, 1.0, vt).astype(BF)


def online_step(q, kv, o_ref, m_ref, cols, mask):
    s = lax.dot_general(kv, q, NT, preferred_element_type=F32)
    if mask is not None:
        s = jnp.where(mask, s, NEG)
    m0 = m_ref[0:1, cols]
    m1 = jnp.maximum(m0, jnp.max(s, axis=0, keepdims=True))
    p = jnp.exp(s - m1).astype(BF)
    o_ref[:, cols] = o_ref[:, cols] * jnp.exp(m0 - m1) + jnp.dot(
        values_t(kv), p, preferred_element_type=F32
    )
    m_ref[0:1, cols] = m1


def spread_heads(stage, q_ref):
    wide = stage[...].astype(F32)
    low = lax.broadcasted_iota(jnp.int32, (TD, 128), 1) < HD
    q_ref[:TD, :] = jnp.where(low, wide, 0.0).astype(BF)
    q_ref[TD:, :] = jnp.where(low, pltpu.roll(wide, HD, 1), 0.0).astype(BF)


def fetch_all(pairs, sem):
    copies = [pltpu.make_async_copy(a, b, sem.at[i]) for i, (a, b) in enumerate(pairs)]
    for v in copies:
        v.start()
    return copies


def add_block(kv, q_ref, o_ref, m_ref, mask):
    vt = values_t(kv)
    for t in range(NQ // TQ):
        cols = pl.ds(t * TQ, TQ)
        s = lax.dot_general(kv, q_ref[cols, :], NT, preferred_element_type=F32)
        if mask is not None:
            s = jnp.where(mask(t * TQ, TQ), s, NEG)
        p = jnp.exp(s - m_ref[0:1, cols]).astype(BF)
        o_ref[:, cols] = o_ref[:, cols] + jnp.dot(vt, p, preferred_element_type=F32)


def too_large(o_ref):
    return jnp.logical_not(jnp.max(o_ref[HD : HD + 1, :]) < LIMIT)


def add_prefix(count, buf, sem, q_ref, o_ref, m_ref, head):
    def wait(j):
        pltpu.make_async_copy(buf.at[0], buf.at[j], sem.at[j]).wait()

    def block(j, _):
        if head:
            pl.when(j > 0)(lambda: wait(j))
        else:
            wait(j)
        add_block(buf[j], q_ref, o_ref, m_ref, None)
        return 0

    lax.fori_loop(0, count, block, 0)


def again_prefix(count, buf, q_ref, o_ref, m_ref):
    def again(i, _):
        kv = buf[i // 4, pl.ds(pl.multiple_of(i % 4 * 256, 256), 256), :]
        for t in range(NQ // 256):
            cols = pl.ds(t * 256, 256)
            online_step(q_ref[cols, :], kv, o_ref, m_ref, cols, None)
        return 0

    lax.fori_loop(0, count * 4, again, 0)


def masker(start, last, at, size):
    def mask(t, width):
        key = at + lax.broadcasted_iota(jnp.int32, (size, width), 0)
        return (key >= start[:, t : t + width]) & (key <= last[:, t : t + width])

    return mask


def add_suffix(low, whole, end, diagonal, start, last, buf, q_ref, o_ref, m_ref):
    def block(at, size, masked):
        at = pl.multiple_of(at, TD)
        mask = masker(start, last, at, size) if masked else None
        add_block(buf[pl.ds(at, size), :], q_ref, o_ref, m_ref, mask)

    ahead = end - whole
    split = lax.rem(ahead, 2)

    def partly(b, _):
        block(jnp.where(b < whole, b, end) * TD, TD, True)
        return 0

    lax.fori_loop(low, whole + (1 if diagonal else 0), partly, 0)
    pl.when(split == 1)(lambda: block(whole * TD, TD, False))

    def fully(b, _):
        block((whole + split + 2 * b) * TD, 2 * TD, False)
        return 0

    lax.fori_loop(0, ahead // 2, fully, 0)


def again_suffix(low, end, start, last, buf, q_ref, o_ref, m_ref):
    def again(i, _):
        at = pl.multiple_of(i * 256, 256)
        kv = buf[pl.ds(at, 256), :]
        mask = masker(start, last, at, 256)
        for t in range(4):
            online_step(
                q_ref[pl.ds(t * 256, 256), :], kv, o_ref, m_ref, pl.ds(t * 256, 256), mask(t * 256, 256)
            )
        return 0

    lax.fori_loop(low * 2, end * 2, again, 0)


def place():
    seq = lax.axis_index("seq")
    return seq // 8, lax.rem(seq // 2, 4), lax.rem(seq, 2)


def half_sources():
    x, y, c = place()
    rows = [y] + [lax.rem(y - k + 4, 4) for k in TURNS]
    return [r * 2 + d for r in rows for d in (c, 1 - c)]


def news_pairs(pays, buf, segs):
    src = half_sources()
    out = [(pays[j].at[pl.ds(SEG_AT, 16), :], segs.at[j]) for j in range(8)]
    for j in range(8):
        at = pl.multiple_of(src[j] * TD, TD)
        out.append((pays[j].at[pl.ds(0, TD), :], buf.at[pl.ds(at, TD), :]))
    return out


def count_same(segs, number, keep):
    total = jnp.zeros((16, 128), F32)
    for j in range(8):
        hit = (segs[j].astype(F32) == number) & keep[j]
        total = total + jnp.where(hit, 1.0, 0.0)
    return jnp.sum(total).astype(jnp.int32)


def begin_kernel(ask_hbm, *refs, count):
    parts = refs[:count]
    o_ref, m_ref, stage, q_ref, buf, sem = refs[count:]
    copies = fetch_all(
        [(parts[j], buf.at[j]) for j in range(count)] + [(ask_hbm.at[pl.ds(0, TD), :], stage)], sem
    )
    o_ref[...] = jnp.zeros_like(o_ref)
    copies[count].wait()
    spread_heads(stage, q_ref)
    copies[0].wait()
    s = lax.dot_general(buf[0, :256, :], q_ref[...], NT, preferred_element_type=F32)
    m_ref[...] = jnp.broadcast_to(jnp.max(s, axis=0, keepdims=True), m_ref.shape)
    add_prefix(count, buf, sem, q_ref, o_ref, m_ref, True)

    @pl.when(too_large(o_ref))
    def _():
        o_ref[...] = jnp.zeros_like(o_ref)
        m_ref[...] = jnp.full_like(m_ref, NEG)
        again_prefix(count, buf, q_ref, o_ref, m_ref)


VM = pl.BlockSpec(memory_space=pltpu.VMEM)
HBM = pl.BlockSpec(memory_space=pl.ANY)
STATE = [jax.ShapeDtypeStruct((NV, NQ), F32), jax.ShapeDtypeStruct((8, NQ), F32)]
ASK = [pltpu.VMEM((TD, 128), BF), pltpu.VMEM((NQ, 128), BF)]


def price(keys):
    return pl.CostEstimate(
        flops=keys * NQ * 2 * 600, bytes_accessed=keys * 256, transcendentals=keys * NQ
    )


def begin_call(ask, parts):
    count = len(parts)
    return pl.pallas_call(
        functools.partial(begin_kernel, count=count),
        in_specs=[HBM] * (1 + count),
        out_specs=[VM, VM],
        out_shape=STATE,
        scratch_shapes=ASK
        + [pltpu.VMEM((count, PRE, 128), BF), pltpu.SemaphoreType.DMA((count + 1,))],
        cost_estimate=price(count * PRE),
        name="attend_prefix",
    )(ask, *parts)


def partner_kernel(ask_hbm, o_in, m_in, *refs):
    pays = refs[:8]
    out_ref, stage, marks, q_ref, o_ref, m_ref, buf, segs, sem = refs[8:]
    x, y, c = place()
    copies = fetch_all(
        news_pairs(pays, buf, segs)
        + [
            (ask_hbm.at[pl.ds(0, TD), :], stage),
            (ask_hbm.at[pl.ds(SEG_AT, 16), :], marks),
        ],
        sem,
    )
    o_ref[...] = o_in[...]
    m_ref[...] = m_in[...]
    for v in copies[:8] + copies[16:]:
        v.wait()
    spread_heads(stage, q_ref)
    newest = segs[0].astype(F32)
    for j in range(1, 8):
        newest = jnp.maximum(newest, segs[j].astype(F32))
    newest = jnp.max(newest)
    early = x == 0
    begin = 8 * TD - count_same(segs, newest, [early] * 8)
    seg = marks[...].astype(F32)
    row = jnp.concatenate([seg[k : k + 1, :] for k in range(4)], axis=1)
    row = jnp.concatenate([row, row], axis=1)
    start = jnp.where((row == newest) & early, begin, 8 * TD)
    last = jnp.full((1, NQ), 8 * TD, jnp.int32)
    low = jnp.min(start) // TD
    whole = jnp.minimum((jnp.max(start) + TD - 1) // TD, 8)
    for v in copies[8:16]:
        v.wait()
    add_suffix(low, whole, 8, False, start, last, buf, q_ref, o_ref, m_ref)

    @pl.when(too_large(o_ref))
    def _():
        o_ref[...] = o_in[...]
        m_ref[...] = m_in[...]
        again_suffix(low, 8, start, last, buf, q_ref, o_ref, m_ref)

    out_ref[:HD, :] = o_ref[:HD, :]
    first = lax.broadcasted_iota(jnp.int32, (8, NQ), 0) == 0
    out_ref[HD:, :] = jnp.where(first, o_ref[HD : HD + 1, :], m_ref[0:1, :])


def partner_call(ask, state, pays):
    return pl.pallas_call(
        partner_kernel,
        in_specs=[HBM, VM, VM] + [HBM] * 8,
        out_specs=VM,
        out_shape=jax.ShapeDtypeStruct((MSG, NQ), F32),
        scratch_shapes=[
            ASK[0],
            pltpu.VMEM((16, 128), BF),
            ASK[1],
            pltpu.VMEM((NV, NQ), F32),
            pltpu.VMEM((8, NQ), F32),
            pltpu.VMEM((8 * TD, 128), BF),
            pltpu.VMEM((8, 16, 128), BF),
            pltpu.SemaphoreType.DMA((18,)),
        ],
        cost_estimate=price(3 * TD),
        name="attend_partner",
    )(ask, state[0], state[1], *pays)


def own_kernel(ask_hbm, row_ref, o_in, m_in, *refs):
    parts = refs[:6]
    pays = refs[6:14]
    out_ref, top_ref, stage, q_ref, o_ref, m_ref, pre, buf, segs, sem, pre_sem = refs[14:]
    x, y, c = place()
    asked = pltpu.make_async_copy(ask_hbm.at[pl.ds(0, TD), :], stage, sem.at[16])
    asked.start()
    fetch_all([(parts[j], pre.at[j]) for j in range(6)], pre_sem)
    copies = fetch_all(news_pairs(pays, buf, segs), sem)
    o_ref[...] = o_in[...]
    m_ref[...] = m_in[...]
    asked.wait()
    spread_heads(stage, q_ref)
    add_prefix(6, pre, pre_sem, q_ref, o_ref, m_ref, False)
    for v in copies:
        v.wait()
    own = y * 2 + c
    row = row_ref[1:2, :]
    mine = jnp.max(jnp.where(lax.broadcasted_iota(jnp.int32, (1, NQ), 1) == 0, row, -1.0))
    src = half_sources()
    begin = own * TD - count_same(segs, mine, [v < own for v in src])
    start = jnp.where(row == mine, begin, row_ref[0:1, :].astype(jnp.int32) + own * TD)
    lane = lax.broadcasted_iota(jnp.int32, (1, NQ), 1)
    last = own * TD + jnp.where(lane >= TD, lane - TD, lane)
    low = begin // TD
    whole = jnp.minimum((jnp.max(start) + TD - 1) // TD, own)
    add_suffix(low, whole, own, True, start, last, buf, q_ref, o_ref, m_ref)

    @pl.when(too_large(o_ref))
    def _():
        o_ref[...] = o_in[...]
        m_ref[...] = m_in[...]
        again_prefix(6, pre, q_ref, o_ref, m_ref)
        again_suffix(low, own + 1, start, last, buf, q_ref, o_ref, m_ref)

    out_ref[...] = o_ref[...]
    top_ref[...] = m_ref[...]


def own_call(ask, rows, state, parts, pays):
    return pl.pallas_call(
        own_kernel,
        in_specs=[HBM, VM, VM, VM] + [HBM] * 14,
        out_specs=[VM, VM],
        out_shape=STATE,
        scratch_shapes=ASK
        + [
            pltpu.VMEM((NV, NQ), F32),
            pltpu.VMEM((8, NQ), F32),
            pltpu.VMEM((6, PRE, 128), BF),
            pltpu.VMEM((8 * TD, 128), BF),
            pltpu.VMEM((8, 16, 128), BF),
            pltpu.SemaphoreType.DMA((17,)),
            pltpu.SemaphoreType.DMA((6,)),
        ],
        cost_estimate=price(9 * PRE),
        name="attend_own",
    )(ask, rows, state[0], state[1], *parts, *pays)


def join_kernel(o_ref, m_ref, msg_ref, out_ref):
    far = msg_ref[HD + 1 : HD + 2, :]
    near = m_ref[0:1, :]
    top = jnp.maximum(near, far)
    wa, wb = jnp.exp(near - top), jnp.exp(far - top)
    total = o_ref[: HD + 8, :] * wa + msg_ref[...] * wb
    mixed = total[:HD, :] / total[HD : HD + 1, :]
    both = jnp.concatenate([mixed[:, :TD], mixed[:, TD:]], axis=0)
    out_ref[...] = jnp.transpose(both).astype(BF)


def mix_kernel(
    att_ref, tok_hbm, gain_ref, route_ref, weight_ref, w0, w1, w2, w3, w4, res_ref, xi_ref, tok, sem
):
    tp = lax.axis_index("tp")
    fetch = pltpu.make_async_copy(
        tok_hbm.at[pl.ds(pl.multiple_of(tp * ROWS, ROWS), ROWS), :], tok, sem
    )
    fetch.start()
    q, z = tp // 4, lax.rem(tp, 4)
    side = 1 + 2 * place()[2]
    back = [0, side, 4 - side, 2]
    parts = [w0.at[0], w1.at[0]] + [w.at[i] for w in (w2, w3, w4) for i in range(2)]
    total = jnp.zeros((ROWS, 1024), F32)
    for j in range(8):
        head = (q if j % 2 == 0 else 1 - q) * 4 + lax.rem(z - back[j // 2] + 4, 4)
        total = total + jnp.dot(att_ref[head], parts[j][...], preferred_element_type=F32)
    line = lax.broadcasted_iota(jnp.int32, (128, ROWS), 0)
    table = jnp.zeros((128, ROWS), F32)
    for k in range(8):
        expert = route_ref[k : k + 1, :]
        weight = weight_ref[k : k + 1, :]
        high = weight.astype(BF).astype(F32)
        table = table + jnp.where(line == expert, high, 0.0)
        table = table + jnp.where(line == expert + 32, weight - high, 0.0)
    gates = jnp.transpose(table).astype(BF)
    fetch.wait()
    total = tok[...].astype(F32) + total
    res_ref[...] = total
    xi = rms(total, gain_ref[...]).astype(BF)
    for j in range(8):
        xi_ref[j, :, :1024] = xi
        xi_ref[j, :, 1024:] = gates


def mix_call(att, tokens, gain, routes, weights, ws):
    return pl.pallas_call(
        mix_kernel,
        in_specs=[VM, HBM] + [VM] * 8,
        out_specs=[VM, VM],
        out_shape=[
            jax.ShapeDtypeStruct((ROWS, 1024), F32),
            jax.ShapeDtypeStruct((8, ROWS, 1152), BF),
        ],
        scratch_shapes=[pltpu.VMEM((ROWS, 1024), BF), pltpu.SemaphoreType.DMA],
        name="mix",
    )(att, tokens, gain, routes, weights, *ws)


def expert_kernel(x_ref, wi_own, wi_peer, wo_own, wo_peer, out_ref, acc):
    e = pl.program_id(0)
    x, y, c = place()

    def run(wi, wo, add):
        joined = jnp.dot(x_ref[:, :1024], wi[0], preferred_element_type=F32)
        g = joined[:, :512]
        hidden = (g / (1.0 + jnp.exp(-g)) * joined[:, 512:]).astype(BF)
        o = jnp.dot(hidden, wo[0], preferred_element_type=F32).astype(BF).astype(F32)
        lane = lax.broadcasted_iota(jnp.int32, (512, 128), 1)
        side = jnp.where(e < 2, c, 1 - c)
        number = (x * 8 + y * 2 + side) * 2 + lax.rem(e, 2)
        hit = (lane == number) | (lane == number + 32)
        table = x_ref[:, 1024:].astype(F32)
        gate = jnp.sum(jnp.where(hit, table, 0.0), axis=1, keepdims=True)
        o = o * gate
        if add:
            acc[...] = acc[...] + o
        else:
            acc[...] = o

    pl.when(e == 0)(lambda: run(wi_own, wo_own, False))
    pl.when(e == 1)(lambda: run(wi_own, wo_own, True))
    pl.when(e >= 2)(lambda: run(wi_peer, wo_peer, True))

    @pl.when(e == 3)
    def _():
        out_ref[...] = acc[...].astype(BF)


def expert_call(x, wi_own, wi_peer, wo_own, wo_peer):
    own = lambda e: (jnp.minimum(e, 1), 0, 0)
    peer = lambda e: (jnp.maximum(e - 2, 0), 0, 0)
    return pl.pallas_call(
        expert_kernel,
        grid=(4,),
        in_specs=[
            pl.BlockSpec((512, 1152), lambda e: (0, 0)),
            pl.BlockSpec((1, 1024, 1024), own),
            pl.BlockSpec((1, 1024, 1024), peer),
            pl.BlockSpec((1, 512, 1024), own),
            pl.BlockSpec((1, 512, 1024), peer),
        ],
        out_specs=pl.BlockSpec((512, 1024), lambda e: (0, 0)),
        scratch_shapes=[pltpu.VMEM((512, 1024), F32)],
        out_shape=jax.ShapeDtypeStruct((512, 1024), BF),
        name="experts",
    )(x, wi_own, wi_peer, wo_own, wo_peer)


def body(
    tokens,
    segment_ids,
    prefix_cache,
    norm1_gain,
    w_qkv,
    w_out,
    norm2_gain,
    expert_in,
    expert_out,
    routes,
    route_weights,
):
    tie = lax.optimization_barrier

    def swap(v):
        return lax.ppermute(v, "seq", CORE)

    def across(v):
        return lax.ppermute(v, "seq", ACROSS)

    def round_y(v):
        return [
            lax.ppermute(v, "seq", seq_perm(lambda a, b, d, k=k: (a, (b + k) % 4, d)))
            for k in TURNS
        ]

    pre = prefix_cache.reshape(PRE, 128)
    far_pre = round_y(pre)
    near_pre = [swap(pre)]
    pay, ask, rows, new = pl.pallas_call(
        project_kernel,
        out_shape=[
            jax.ShapeDtypeStruct((PAY, 128), BF),
            jax.ShapeDtypeStruct((PAY, 128), BF),
            jax.ShapeDtypeStruct((8, NQ), F32),
            jax.ShapeDtypeStruct((TD, 128), BF),
        ],
        cost_estimate=pl.CostEstimate(flops=2 * TD * 1024 * 256, bytes_accessed=2 << 20, transcendentals=TD),
        name="project",
    )(tokens, norm1_gain[None, :], w_qkv.reshape(1024, 256), segment_ids.reshape(4, 128))
    asked = across(ask)
    pay, w_out_in = tie((pay, w_out))
    wx = lax.ppermute(w_out_in, "tp", tp_perm(lambda a, b: (1 - a, b)))
    first = begin_call(ask, [pre, near_pre[0]])

    far_pre, asked, wx, first, pay = tie((far_pre, asked, wx, first, pay))
    near_pre += [swap(v) for v in far_pre]
    near_new = [swap(pay)]
    near_new, pay = tie((near_new, pay))
    far_new = round_y(pay)
    wpair = jnp.concatenate([w_out, wx])
    side = lax.ppermute(wpair, ("seq", "tp"), SIDES)
    opposite = lax.ppermute(wpair, "tp", tp_perm(lambda a, b: (a, (b + 2) % 4)))
    shards = [v for p in zip([pre] + far_pre, near_pre) for v in p]
    second = begin_call(asked, shards)

    far_new, side, opposite, second = tie((far_new, side, opposite, second))
    near_new += [swap(v) for v in far_new]
    wz = [side, swap(side), opposite]
    pays = [v for p in zip([pay] + far_new, near_new) for v in p]
    message = partner_call(asked, second, pays)

    wz, near_new, message, expert_in_t, expert_out_t = tie(
        (wz, near_new, message, expert_in, expert_out)
    )
    returned = across(message)
    wi_peer = swap(expert_in_t)
    wo_peer = swap(expert_out_t)
    o, m = own_call(ask, rows, first, shards[2:], pays)
    attended = pl.pallas_call(
        join_kernel, out_shape=jax.ShapeDtypeStruct((TD, 128), BF), name="join"
    )(o, m, returned)

    spread = lax.all_to_all(attended.reshape(8, ROWS, 128), "tp", 0, 0, tiled=True)
    residual, copies = mix_call(
        spread,
        tokens,
        norm2_gain[None, :],
        jnp.transpose(routes),
        jnp.transpose(route_weights),
        [w_out, wx] + wz,
    )
    everyone = lax.all_to_all(copies, "seq", 0, 0, axis_index_groups=CHIP_GROUPS, tiled=True)
    partial = expert_call(
        everyone.reshape(512, 1152), expert_in, wi_peer, expert_out, wo_peer
    )
    back = lax.all_to_all(
        partial.reshape(8, ROWS, 1024), "seq", 0, 0, axis_index_groups=CHIP_GROUPS, tiled=True
    )
    hidden = (residual + jnp.sum(back.astype(F32), axis=0)).astype(BF)
    return hidden, new.reshape(TD, 1, 128)


def solution(mesh):
    in_specs = (
        P("seq", None),
        P("seq"),
        P("seq", "tp", None),
        P(),
        P(None, "tp", None),
        P("tp", None, None),
        P(),
        P("seq", None, None),
        P("seq", None, None),
        P(("seq", "tp"), None),
        P(("seq", "tp"), None),
    )
    out_specs = (P(("seq", "tp"), None), P("seq", "tp", None))
    return jax.shard_map(body, mesh=mesh, in_specs=in_specs, out_specs=out_specs, check_vma=False)
```

```python
import functools

import jax
import jax.numpy as jnp
from jax import lax
from jax.experimental import pallas as pl
from jax.experimental.pallas import tpu as pltpu
from jax.sharding import PartitionSpec as P

SCALE = 0.015625
EPS = 1e-06
HD = 64
NV = 80
TD = 512
PRE = 1024
ROWS = 64
TQ = 512
NQ = 2 * TD
SEG_AT = TD
PAY = SEG_AT + 16
MSG = 72
LIMIT = 1e26
NEG = -1e30
NT = (((1,), (1,)), ((), ()))
F32 = jnp.float32
BF = jnp.bfloat16


def seq_perm(move):
    return [
        (x * 8 + y * 2 + c, (lambda t: t[0] * 8 + t[1] * 2 + t[2])(move(x, y, c)))
        for x in range(2)
        for y in range(4)
        for c in range(2)
    ]


def tp_perm(move):
    return [(q * 4 + z, (lambda t: t[0] * 4 + t[1])(move(q, z))) for q in range(2) for z in range(4)]


CORE = seq_perm(lambda x, y, c: (x, y, 1 - c))
ACROSS = seq_perm(lambda x, y, c: (1 - x, y, c))
TURNS = (1, 3, 2)
SIDES = [
    (s * 8 + q * 4 + z, s * 8 + q * 4 + (z + (1 if s % 2 == 0 else 3)) % 4)
    for s in range(16)
    for q in range(2)
    for z in range(4)
]
CHIP_GROUPS = [[x * 8 + y * 2 + c for x in range(2) for y in range(4)] for c in range(2)]


def room(mib):
    return pltpu.CompilerParams(vmem_limit_bytes=mib << 20)


def rms(wide, gain):
    mean_square = jnp.mean(wide * wide, axis=-1, keepdims=True)
    return wide * lax.rsqrt(mean_square + EPS) * gain


def project_kernel(tok_ref, gain_ref, w_ref, seg_ref, pay_ref, ask_ref, row_ref, new_ref):
    normed = rms(tok_ref[...].astype(F32), gain_ref[...]).astype(BF)
    proj = jnp.dot(normed, w_ref[...], preferred_element_type=F32)
    ask_ref[:TD, :] = (proj[:, :128].astype(BF).astype(F32) * SCALE).astype(BF)
    new = proj[:, 128:].astype(BF)
    new_ref[...] = new
    pay_ref[:TD, :] = new
    seg = seg_ref[...].astype(F32)
    segs = jnp.concatenate([seg, jnp.full((12, 128), -1.0, F32)], axis=0).astype(BF)
    pay_ref[SEG_AT:, :] = segs
    ask_ref[SEG_AT:, :] = segs
    row = jnp.concatenate([seg[k : k + 1, :] for k in range(4)], axis=1)
    col = jnp.transpose(jnp.broadcast_to(row, (8, TD)))[:, 0:1]
    below = jnp.sum(jnp.where(col < row, 1.0, 0.0), axis=0, keepdims=True)
    row_ref[0:1, :] = jnp.concatenate([below, below], axis=1)
    row_ref[1:2, :] = jnp.concatenate([row, row], axis=1)


def values_t(kv):
    row = lax.broadcasted_iota(jnp.int32, (NV, 128), 0)
    col = lax.broadcasted_iota(jnp.int32, (NV, 128), 1)
    pick = jnp.where((col == row + HD) & (row < HD), 1.0, 0.0).astype(BF)
    vt = lax.dot_general(pick, kv, NT, preferred_element_type=F32)
    ones = lax.broadcasted_iota(jnp.int32, vt.shape, 0) >= HD
    return jnp.where(ones, 1.0, vt).astype(BF)


def online_step(q, kv, o_ref, m_ref, cols, mask):
    s = lax.dot_general(kv, q, NT, preferred_element_type=F32)
    if mask is not None:
        s = jnp.where(mask, s, NEG)
    m0 = m_ref[0:1, cols]
    m1 = jnp.maximum(m0, jnp.max(s, axis=0, keepdims=True))
    p = jnp.exp(s - m1).astype(BF)
    o_ref[:, cols] = o_ref[:, cols] * jnp.exp(m0 - m1) + jnp.dot(
        values_t(kv), p, preferred_element_type=F32
    )
    m_ref[0:1, cols] = m1


def spread_heads(stage, q_ref):
    wide = stage[...].astype(F32)
    low = lax.broadcasted_iota(jnp.int32, (TD, 128), 1) < HD
    q_ref[:TD, :] = jnp.where(low, wide, 0.0).astype(BF)
    q_ref[TD:, :] = jnp.where(low, pltpu.roll(wide, HD, 1), 0.0).astype(BF)


def fetch_all(pairs, sem):
    copies = [pltpu.make_async_copy(a, b, sem.at[i]) for i, (a, b) in enumerate(pairs)]
    for v in copies:
        v.start()
    return copies


def add_block(kv, q_ref, o_ref, m_ref, mask):
    vt = values_t(kv)
    for t in range(NQ // TQ):
        cols = pl.ds(t * TQ, TQ)
        s = lax.dot_general(kv, q_ref[cols, :], NT, preferred_element_type=F32)
        if mask is not None:
            s = jnp.where(mask(t * TQ, TQ), s, NEG)
        p = jnp.exp(s - m_ref[0:1, cols]).astype(BF)
        o_ref[:, cols] = o_ref[:, cols] + jnp.dot(vt, p, preferred_element_type=F32)


def too_large(o_ref):
    return jnp.logical_not(jnp.max(o_ref[HD : HD + 1, :]) < LIMIT)


def add_prefix(count, buf, sem, q_ref, o_ref, m_ref, head):
    def wait(j):
        pltpu.make_async_copy(buf.at[0], buf.at[j], sem.at[j]).wait()

    def block(j, _):
        if head:
            pl.when(j > 0)(lambda: wait(j))
        else:
            wait(j)
        add_block(buf[j], q_ref, o_ref, m_ref, None)
        return 0

    lax.fori_loop(0, count, block, 0, unroll=2)


def again_prefix(count, buf, q_ref, o_ref, m_ref):
    def again(i, _):
        kv = buf[i // 4, pl.ds(pl.multiple_of(i % 4 * 256, 256), 256), :]
        for t in range(NQ // 256):
            cols = pl.ds(t * 256, 256)
            online_step(q_ref[cols, :], kv, o_ref, m_ref, cols, None)
        return 0

    lax.fori_loop(0, count * 4, again, 0)


def masker(start, last, at, size):
    def mask(t, width):
        key = at + lax.broadcasted_iota(jnp.int32, (size, width), 0)
        ok = key >= start[:, t : t + width]
        return ok if last is None else ok & (key <= last[:, t : t + width])

    return mask


def add_suffix(low, whole, end, diagonal, start, last, buf, q_ref, o_ref, m_ref):
    def block(at, size, masked):
        at = pl.multiple_of(at, TD)
        bound = last if masked == "both" else None
        mask = masker(start, bound, at, size) if masked else None
        add_block(buf[pl.ds(at, size), :], q_ref, o_ref, m_ref, mask)

    ahead = end - whole
    split = lax.rem(ahead, 2)

    def partly(b, _):
        block(b * TD, TD, "start")
        return 0

    lax.fori_loop(low, whole, partly, 0)
    if diagonal:
        block(end * TD, TD, "both")
    pl.when(split == 1)(lambda: block(whole * TD, TD, None))

    def fully(b, _):
        block((whole + split + 2 * b) * TD, 2 * TD, None)
        return 0

    lax.fori_loop(0, ahead // 2, fully, 0)


def again_suffix(low, end, start, last, buf, q_ref, o_ref, m_ref):
    def again(i, _):
        at = pl.multiple_of(i * 256, 256)
        kv = buf[pl.ds(at, 256), :]
        mask = masker(start, last, at, 256)
        for t in range(4):
            online_step(
                q_ref[pl.ds(t * 256, 256), :], kv, o_ref, m_ref, pl.ds(t * 256, 256), mask(t * 256, 256)
            )
        return 0

    lax.fori_loop(low * 2, end * 2, again, 0)


def place():
    seq = lax.axis_index("seq")
    return seq // 8, lax.rem(seq // 2, 4), lax.rem(seq, 2)


def half_sources():
    x, y, c = place()
    rows = [y] + [lax.rem(y - k + 4, 4) for k in TURNS]
    return [r * 2 + d for r in rows for d in (c, 1 - c)]


def news_pairs(pays, buf, segs):
    src = half_sources()
    out = [(pays[j].at[pl.ds(SEG_AT, 16), :], segs.at[j]) for j in range(8)]
    for j in range(8):
        at = pl.multiple_of(src[j] * TD, TD)
        out.append((pays[j].at[pl.ds(0, TD), :], buf.at[pl.ds(at, TD), :]))
    return out


def count_same(segs, number, keep):
    total = jnp.zeros((16, 128), F32)
    for j in range(8):
        hit = segs[j].astype(F32) == jnp.where(keep[j], number, -2.0)
        total = total + jnp.where(hit, 1.0, 0.0)
    return jnp.sum(total).astype(jnp.int32)


def begin_kernel(ask_hbm, *refs, count):
    parts = refs[:count]
    o_ref, m_ref, stage, q_ref, buf, sem = refs[count:]
    copies = fetch_all(
        [(parts[j], buf.at[j]) for j in range(count)] + [(ask_hbm.at[pl.ds(0, TD), :], stage)], sem
    )
    o_ref[...] = jnp.zeros_like(o_ref)
    copies[count].wait()
    spread_heads(stage, q_ref)
    copies[0].wait()
    s = lax.dot_general(buf[0, :256, :], q_ref[...], NT, preferred_element_type=F32)
    m_ref[...] = jnp.broadcast_to(jnp.max(s, axis=0, keepdims=True), m_ref.shape)
    add_prefix(count, buf, sem, q_ref, o_ref, m_ref, True)

    @pl.when(too_large(o_ref))
    def _():
        o_ref[...] = jnp.zeros_like(o_ref)
        m_ref[...] = jnp.full_like(m_ref, NEG)
        again_prefix(count, buf, q_ref, o_ref, m_ref)


VM = pl.BlockSpec(memory_space=pltpu.VMEM)
HBM = pl.BlockSpec(memory_space=pl.ANY)
STATE = [jax.ShapeDtypeStruct((NV, NQ), F32), jax.ShapeDtypeStruct((8, NQ), F32)]
ASK = [pltpu.VMEM((TD, 128), BF), pltpu.VMEM((NQ, 128), BF)]


def price(keys):
    return pl.CostEstimate(
        flops=keys * NQ * 2 * 600, bytes_accessed=keys * 256, transcendentals=keys * NQ
    )


def begin_call(ask, parts):
    count = len(parts)
    return pl.pallas_call(
        functools.partial(begin_kernel, count=count),
        in_specs=[HBM] * (1 + count),
        out_specs=[VM, VM],
        out_shape=STATE,
        scratch_shapes=ASK
        + [pltpu.VMEM((count, PRE, 128), BF), pltpu.SemaphoreType.DMA((count + 1,))],
        cost_estimate=price(count * PRE),
        compiler_params=room(20),
        name="attend_prefix",
    )(ask, *parts)


def partner_kernel(ask_hbm, o_in, m_in, *refs):
    pays = refs[:8]
    out_ref, stage, marks, q_ref, o_ref, m_ref, buf, segs, sem = refs[8:]
    o_ref[...] = o_in[...]
    m_ref[...] = m_in[...]

    @pl.when(place()[0] == 0)
    def _():
        copies = fetch_all(
            news_pairs(pays, buf, segs)
            + [
                (ask_hbm.at[pl.ds(0, TD), :], stage),
                (ask_hbm.at[pl.ds(SEG_AT, 16), :], marks),
            ],
            sem,
        )
        for v in copies[:8] + copies[16:]:
            v.wait()
        spread_heads(stage, q_ref)
        newest = segs[0].astype(F32)
        for j in range(1, 8):
            newest = jnp.maximum(newest, segs[j].astype(F32))
        newest = jnp.max(newest)
        begin = 8 * TD - count_same(segs, newest, [True] * 8)
        seg = marks[...].astype(F32)
        row = jnp.concatenate([seg[k : k + 1, :] for k in range(4)], axis=1)
        row = jnp.concatenate([row, row], axis=1)
        start = jnp.where(row == newest, begin, 8 * TD)
        last = jnp.full((1, NQ), 8 * TD, jnp.int32)
        low = jnp.min(start) // TD
        whole = jnp.minimum((jnp.max(start) + TD - 1) // TD, 8)
        for v in copies[8:16]:
            v.wait()
        add_suffix(low, whole, 8, False, start, last, buf, q_ref, o_ref, m_ref)

        @pl.when(too_large(o_ref))
        def _():
            o_ref[...] = o_in[...]
            m_ref[...] = m_in[...]
            again_suffix(low, 8, start, last, buf, q_ref, o_ref, m_ref)

    out_ref[:HD, :] = o_ref[:HD, :]
    first = lax.broadcasted_iota(jnp.int32, (8, NQ), 0) == 0
    out_ref[HD:, :] = jnp.where(first, o_ref[HD : HD + 1, :], m_ref[0:1, :])


def partner_call(ask, state, pays):
    return pl.pallas_call(
        partner_kernel,
        in_specs=[HBM, VM, VM] + [HBM] * 8,
        out_specs=VM,
        out_shape=jax.ShapeDtypeStruct((MSG, NQ), F32),
        scratch_shapes=[
            ASK[0],
            pltpu.VMEM((16, 128), BF),
            ASK[1],
            pltpu.VMEM((NV, NQ), F32),
            pltpu.VMEM((8, NQ), F32),
            pltpu.VMEM((8 * TD, 128), BF),
            pltpu.VMEM((8, 16, 128), BF),
            pltpu.SemaphoreType.DMA((18,)),
        ],
        cost_estimate=price(3 * TD),
        compiler_params=room(20),
        name="attend_partner",
    )(ask, state[0], state[1], *pays)


def own_kernel(ask_hbm, row_ref, o_in, m_in, *refs):
    parts = refs[:6]
    pays = refs[6:14]
    out_ref, top_ref, stage, q_ref, o_ref, m_ref, pre, buf, segs, sem, pre_sem = refs[14:]
    x, y, c = place()
    asked = pltpu.make_async_copy(ask_hbm.at[pl.ds(0, TD), :], stage, sem.at[16])
    asked.start()
    fetch_all([(parts[j], pre.at[j]) for j in range(6)], pre_sem)
    copies = fetch_all(news_pairs(pays, buf, segs), sem)
    o_ref[...] = o_in[...]
    m_ref[...] = m_in[...]
    asked.wait()
    spread_heads(stage, q_ref)
    add_prefix(6, pre, pre_sem, q_ref, o_ref, m_ref, False)
    for v in copies:
        v.wait()
    own = y * 2 + c
    row = row_ref[1:2, :]
    mine = jnp.max(jnp.where(lax.broadcasted_iota(jnp.int32, (1, NQ), 1) == 0, row, -1.0))
    src = half_sources()
    begin = own * TD - count_same(segs, mine, [v < own for v in src])
    start = jnp.where(row == mine, begin, row_ref[0:1, :].astype(jnp.int32) + own * TD)
    lane = lax.broadcasted_iota(jnp.int32, (1, NQ), 1)
    last = own * TD + jnp.where(lane >= TD, lane - TD, lane)
    low = begin // TD
    whole = jnp.minimum((jnp.max(start) + TD - 1) // TD, own)
    add_suffix(low, whole, own, True, start, last, buf, q_ref, o_ref, m_ref)

    @pl.when(too_large(o_ref))
    def _():
        o_ref[...] = o_in[...]
        m_ref[...] = m_in[...]
        again_prefix(6, pre, q_ref, o_ref, m_ref)
        again_suffix(low, own + 1, start, last, buf, q_ref, o_ref, m_ref)

    out_ref[...] = o_ref[...]
    top_ref[...] = m_ref[...]


def own_call(ask, rows, state, parts, pays):
    return pl.pallas_call(
        own_kernel,
        in_specs=[HBM, VM, VM, VM] + [HBM] * 14,
        out_specs=[VM, VM],
        out_shape=STATE,
        scratch_shapes=ASK
        + [
            pltpu.VMEM((NV, NQ), F32),
            pltpu.VMEM((8, NQ), F32),
            pltpu.VMEM((6, PRE, 128), BF),
            pltpu.VMEM((8 * TD, 128), BF),
            pltpu.VMEM((8, 16, 128), BF),
            pltpu.SemaphoreType.DMA((17,)),
            pltpu.SemaphoreType.DMA((6,)),
        ],
        cost_estimate=price(9 * PRE),
        compiler_params=room(20),
        name="attend_own",
    )(ask, rows, state[0], state[1], *parts, *pays)


def join_kernel(o_ref, m_ref, msg_ref, out_ref):
    far = msg_ref[HD + 1 : HD + 2, :]
    near = m_ref[0:1, :]
    top = jnp.maximum(near, far)
    wa, wb = jnp.exp(near - top), jnp.exp(far - top)
    total = o_ref[: HD + 8, :] * wa + msg_ref[...] * wb
    mixed = total[:HD, :] / total[HD : HD + 1, :]
    both = jnp.concatenate([mixed[:, :TD], mixed[:, TD:]], axis=0)
    out_ref[...] = jnp.transpose(both).astype(BF)


def mix_kernel(
    att_ref, tok_hbm, gain_ref, route_ref, weight_ref, w0, w1, w2, w3, w4, res_ref, xi_ref, tok, sem
):
    tp = lax.axis_index("tp")
    fetch = pltpu.make_async_copy(
        tok_hbm.at[pl.ds(pl.multiple_of(tp * ROWS, ROWS), ROWS), :], tok, sem
    )
    fetch.start()
    q, z = tp // 4, lax.rem(tp, 4)
    side = 1 + 2 * place()[2]
    back = [0, side, 4 - side, 2]
    total = jnp.zeros((ROWS, 1024), F32)
    for j in range(4):
        row = lax.rem(z - back[j] + 4, 4)
        pair = jnp.concatenate([att_ref[q * 4 + row], att_ref[(1 - q) * 4 + row]], axis=1)
        w = jnp.concatenate([w0[0], w1[0]], axis=0) if j == 0 else (w2, w3, w4)[j - 1][...].reshape(256, 1024)
        total = total + jnp.dot(pair, w, preferred_element_type=F32)
    line = lax.broadcasted_iota(jnp.int32, (128, ROWS), 0)
    table = jnp.zeros((128, ROWS), F32)
    for k in range(8):
        expert = route_ref[k : k + 1, :]
        weight = weight_ref[k : k + 1, :]
        high = weight.astype(BF).astype(F32)
        table = table + jnp.where(line == expert, high, 0.0)
        table = table + jnp.where(line == expert + 32, weight - high, 0.0)
    gates = jnp.transpose(table).astype(BF)
    fetch.wait()
    total = tok[...].astype(F32) + total
    res_ref[...] = total
    xi = rms(total, gain_ref[...]).astype(BF)
    for j in range(8):
        xi_ref[j, :, :1024] = xi
        xi_ref[j, :, 1024:] = gates


def mix_call(att, tokens, gain, routes, weights, ws):
    return pl.pallas_call(
        mix_kernel,
        in_specs=[VM, HBM] + [VM] * 8,
        out_specs=[VM, VM],
        out_shape=[
            jax.ShapeDtypeStruct((ROWS, 1024), F32),
            jax.ShapeDtypeStruct((8, ROWS, 1152), BF),
        ],
        scratch_shapes=[pltpu.VMEM((ROWS, 1024), BF), pltpu.SemaphoreType.DMA],
        compiler_params=room(12),
        name="mix",
    )(att, tokens, gain, routes, weights, *ws)


def expert_kernel(x_ref, wi_own, wi_peer, wo_own, wo_peer, out_ref, acc):
    x, y, c = place()
    for e in range(4):
        wi, wo = ((wi_own, wo_own), (wi_peer, wo_peer))[e // 2]
        number = (x * 8 + y * 2 + (c if e < 2 else 1 - c)) * 2 + e % 2

        def half(h, _):
            rows = pl.ds(pl.multiple_of(h * 256, 256), 256)
            joined = jnp.dot(x_ref[rows, :1024], wi[e % 2], preferred_element_type=F32)
            g = joined[:, :512]
            hidden = (g / (1.0 + jnp.exp(-g)) * joined[:, 512:]).astype(BF)
            o = jnp.dot(hidden, wo[e % 2], preferred_element_type=F32).astype(BF).astype(F32)
            lane = lax.broadcasted_iota(jnp.int32, (256, 128), 1)
            hit = (lane == number) | (lane == number + 32)
            table = x_ref[rows, 1024:].astype(F32)
            gate = jnp.sum(jnp.where(hit, table, 0.0), axis=1, keepdims=True)
            o = o * gate
            if e:
                o = acc[rows, :] + o
            if e < 3:
                acc[rows, :] = o
            else:
                out_ref[rows, :] = o.astype(BF)
            return 0

        lax.fori_loop(0, 2, half, 0, unroll=2)


def expert_call(x, wi_own, wi_peer, wo_own, wo_peer):
    return pl.pallas_call(
        expert_kernel,
        in_specs=[VM] * 5,
        out_specs=VM,
        scratch_shapes=[pltpu.VMEM((512, 1024), F32)],
        out_shape=jax.ShapeDtypeStruct((512, 1024), BF),
        compiler_params=room(EXPERT_ROOM),
        name="experts",
    )(x, wi_own, wi_peer, wo_own, wo_peer)


EXPERT_ROOM = 30


def body(
    tokens,
    segment_ids,
    prefix_cache,
    norm1_gain,
    w_qkv,
    w_out,
    norm2_gain,
    expert_in,
    expert_out,
    routes,
    route_weights,
):
    tie = lax.optimization_barrier

    def swap(v):
        return lax.ppermute(v, "seq", CORE)

    def across(v):
        return lax.ppermute(v, "seq", ACROSS)

    def round_y(v):
        return [
            lax.ppermute(v, "seq", seq_perm(lambda a, b, d, k=k: (a, (b + k) % 4, d)))
            for k in TURNS
        ]

    pre = prefix_cache.reshape(PRE, 128)
    wx = lax.ppermute(w_out, "tp", tp_perm(lambda a, b: (1 - a, b)))
    far_pre = round_y(pre)
    near_pre = [swap(pre)]
    pay, ask, rows, new = pl.pallas_call(
        project_kernel,
        out_shape=[
            jax.ShapeDtypeStruct((PAY, 128), BF),
            jax.ShapeDtypeStruct((PAY, 128), BF),
            jax.ShapeDtypeStruct((8, NQ), F32),
            jax.ShapeDtypeStruct((TD, 128), BF),
        ],
        cost_estimate=pl.CostEstimate(flops=2 * TD * 1024 * 256, bytes_accessed=2 << 20, transcendentals=TD),
        compiler_params=room(12),
        name="project",
    )(tokens, norm1_gain[None, :], w_qkv.reshape(1024, 256), segment_ids.reshape(4, 128))
    asked = across(ask)
    first = begin_call(ask, [pre, near_pre[0]])

    far_pre, asked, first, pay = tie((far_pre, asked, first, pay))
    near_pre += [swap(v) for v in far_pre]
    near_new = [swap(pay)]
    near_new, pay = tie((near_new, pay))
    far_new = round_y(pay)
    wpair = jnp.concatenate([w_out, wx])
    side = lax.ppermute(wpair, ("seq", "tp"), SIDES)
    opposite = lax.ppermute(wpair, "tp", tp_perm(lambda a, b: (a, (b + 2) % 4)))
    shards = [v for p in zip([pre] + far_pre, near_pre) for v in p]
    second = begin_call(asked, shards)

    far_new, side, opposite, second = tie((far_new, side, opposite, second))
    near_new += [swap(v) for v in far_new]
    wz = [side, swap(side), opposite]
    pays = [v for p in zip([pay] + far_new, near_new) for v in p]
    message = partner_call(asked, second, pays)

    wz, near_new, message, expert_in_t, expert_out_t = tie(
        (wz, near_new, message, expert_in, expert_out)
    )
    returned = across(message)
    wi_peer = swap(expert_in_t)
    wo_peer = swap(expert_out_t)
    o, m = own_call(ask, rows, first, shards[2:], pays)
    attended = pl.pallas_call(
        join_kernel, out_shape=jax.ShapeDtypeStruct((TD, 128), BF), compiler_params=room(8), name="join"
    )(o, m, returned)

    spread = lax.all_to_all(attended.reshape(8, ROWS, 128), "tp", 0, 0, tiled=True)
    residual, copies = mix_call(
        spread,
        tokens,
        norm2_gain[None, :],
        jnp.transpose(routes),
        jnp.transpose(route_weights),
        [w_out, wx] + wz,
    )
    everyone = lax.all_to_all(copies, "seq", 0, 0, axis_index_groups=CHIP_GROUPS, tiled=True)
    partial = expert_call(
        everyone.reshape(512, 1152), expert_in, wi_peer, expert_out, wo_peer
    )
    back = lax.all_to_all(
        partial.reshape(8, ROWS, 1024), "seq", 0, 0, axis_index_groups=CHIP_GROUPS, tiled=True
    )
    hidden = (residual + jnp.sum(back.astype(F32), axis=0)).astype(BF)
    return hidden, new.reshape(TD, 1, 128)


def solution(mesh):
    in_specs = (
        P("seq", None),
        P("seq"),
        P("seq", "tp", None),
        P(),
        P(None, "tp", None),
        P("tp", None, None),
        P(),
        P("seq", None, None),
        P("seq", None, None),
        P(("seq", "tp"), None),
        P(("seq", "tp"), None),
    )
    out_specs = (P(("seq", "tp"), None), P("seq", "tp", None))
    return jax.shard_map(body, mesh=mesh, in_specs=in_specs, out_specs=out_specs, check_vma=False)
```

```python
import functools

import jax
import jax.numpy as jnp
from jax import lax
from jax.experimental import pallas as pl
from jax.experimental.pallas import tpu as pltpu
from jax.sharding import PartitionSpec as P

SCALE = 0.015625
EPS = 1e-06
HD = 64
NV = 80
TD = 512
PRE = 1024
ROWS = 64
TQ = 512
NQ = 2 * TD
SEG_AT = TD
PAY = SEG_AT + 16
MSG = 72
LIMIT = 1e26
NEG = -1e30
NT = (((1,), (1,)), ((), ()))
F32 = jnp.float32
BF = jnp.bfloat16


def seq_perm(move):
    return [
        (x * 8 + y * 2 + c, (lambda t: t[0] * 8 + t[1] * 2 + t[2])(move(x, y, c)))
        for x in range(2)
        for y in range(4)
        for c in range(2)
    ]


def tp_perm(move):
    return [(q * 4 + z, (lambda t: t[0] * 4 + t[1])(move(q, z))) for q in range(2) for z in range(4)]


CORE = seq_perm(lambda x, y, c: (x, y, 1 - c))
ACROSS = seq_perm(lambda x, y, c: (1 - x, y, c))
TURNS = (1, 3, 2)
SIDES = [
    (s * 8 + q * 4 + z, s * 8 + q * 4 + (z + (1 if s % 2 == 0 else 3)) % 4)
    for s in range(16)
    for q in range(2)
    for z in range(4)
]
CHIP_GROUPS = [[x * 8 + y * 2 + c for x in range(2) for y in range(4)] for c in range(2)]


def room(mib):
    return pltpu.CompilerParams(vmem_limit_bytes=mib << 20)


def rms(wide, gain):
    mean_square = jnp.mean(wide * wide, axis=-1, keepdims=True)
    return wide * lax.rsqrt(mean_square + EPS) * gain


def project_kernel(
    tok_hbm, gain_hbm, w_hbm, seg_hbm, pay_ref, ask_ref, row_ref, new_ref, tok, gain, w, seg_in, sem
):
    small = [
        pltpu.make_async_copy(w_hbm, w, sem.at[4]),
        pltpu.make_async_copy(gain_hbm, gain, sem.at[5]),
        pltpu.make_async_copy(seg_hbm, seg_in, sem.at[6]),
    ]
    large = [
        pltpu.make_async_copy(tok_hbm.at[pl.ds(i * 128, 128), :], tok.at[pl.ds(i * 128, 128), :], sem.at[i])
        for i in range(4)
    ]
    for v in [large[0]] + small + large[1:]:
        v.start()
    for v in small:
        v.wait()
    seg = seg_in[...].astype(F32)
    segs = jnp.concatenate([seg, jnp.full((12, 128), -1.0, F32)], axis=0).astype(BF)
    pay_ref[SEG_AT:, :] = segs
    ask_ref[SEG_AT:, :] = segs
    row = jnp.concatenate([seg[k : k + 1, :] for k in range(4)], axis=1)
    col = jnp.transpose(jnp.broadcast_to(row, (8, TD)))[:, 0:1]
    below = jnp.sum(jnp.where(col < row, 1.0, 0.0), axis=0, keepdims=True)
    row_ref[0:1, :] = jnp.concatenate([below, below], axis=1)
    row_ref[1:2, :] = jnp.concatenate([row, row], axis=1)
    for i in range(2):
        large[2 * i].wait()
        large[2 * i + 1].wait()
        rows = pl.ds(i * 256, 256)
        normed = rms(tok[rows, :].astype(F32), gain[...]).astype(BF)
        proj = jnp.dot(normed, w[...], preferred_element_type=F32)
        ask_ref[rows, :] = (proj[:, :128].astype(BF).astype(F32) * SCALE).astype(BF)
        new = proj[:, 128:].astype(BF)
        new_ref[rows, :] = new
        pay_ref[rows, :] = new


def values_t(kv):
    row = lax.broadcasted_iota(jnp.int32, (NV, 128), 0)
    col = lax.broadcasted_iota(jnp.int32, (NV, 128), 1)
    pick = jnp.where((col == row + HD) & (row < HD), 1.0, 0.0).astype(BF)
    vt = lax.dot_general(pick, kv, NT, preferred_element_type=F32)
    ones = lax.broadcasted_iota(jnp.int32, vt.shape, 0) >= HD
    return jnp.where(ones, 1.0, vt).astype(BF)


def online_step(q, kv, o_ref, m_ref, cols, mask):
    s = lax.dot_general(kv, q, NT, preferred_element_type=F32)
    if mask is not None:
        s = jnp.where(mask, s, NEG)
    m0 = m_ref[0:1, cols]
    m1 = jnp.maximum(m0, jnp.max(s, axis=0, keepdims=True))
    p = jnp.exp(s - m1).astype(BF)
    o_ref[:, cols] = o_ref[:, cols] * jnp.exp(m0 - m1) + jnp.dot(
        values_t(kv), p, preferred_element_type=F32
    )
    m_ref[0:1, cols] = m1


def spread_heads(stage, q_ref):
    wide = stage[...].astype(F32)
    low = lax.broadcasted_iota(jnp.int32, (TD, 128), 1) < HD
    q_ref[:TD, :] = jnp.where(low, wide, 0.0).astype(BF)
    q_ref[TD:, :] = jnp.where(low, pltpu.roll(wide, HD, 1), 0.0).astype(BF)


def fetch_all(pairs, sem):
    copies = [pltpu.make_async_copy(a, b, sem.at[i]) for i, (a, b) in enumerate(pairs)]
    for v in copies:
        v.start()
    return copies


def add_block(kv, q_ref, o_ref, m_ref, mask, level=0):
    vt = values_t(kv)
    for t in range(NQ // TQ):
        cols = pl.ds(t * TQ, TQ)
        s = lax.dot_general(kv, q_ref[cols, :], NT, preferred_element_type=F32)
        if mask is not None:
            s = jnp.where(mask(t * TQ, TQ), s, NEG)
        p = jnp.exp(s - m_ref[level : level + 1, cols]).astype(BF)
        o_ref[:, cols] = o_ref[:, cols] + jnp.dot(vt, p, preferred_element_type=F32)


def too_large(o_ref):
    return jnp.logical_not(jnp.max(o_ref[HD : HD + 1, :]) < LIMIT)


def add_prefix(count, buf, sem, q_ref, o_ref, m_ref, head):
    def wait(j):
        pltpu.make_async_copy(buf.at[0], buf.at[j], sem.at[j]).wait()

    def block(j, _):
        if head:
            pl.when(j > 0)(lambda: wait(j))
        else:
            wait(j)
        add_block(buf[j], q_ref, o_ref, m_ref, None)
        return 0

    lax.fori_loop(0, count, block, 0, unroll=2)


def again_prefix(count, buf, q_ref, o_ref, m_ref):
    def again(i, _):
        kv = buf[i // 4, pl.ds(pl.multiple_of(i % 4 * 256, 256), 256), :]
        for t in range(NQ // 256):
            cols = pl.ds(t * 256, 256)
            online_step(q_ref[cols, :], kv, o_ref, m_ref, cols, None)
        return 0

    lax.fori_loop(0, count * 4, again, 0)


def masker(start, last, at, size):
    def mask(t, width):
        key = at + lax.broadcasted_iota(jnp.int32, (size, width), 0)
        ok = key >= start[:, t : t + width]
        return ok if last is None else ok & (key <= last[:, t : t + width])

    return mask


def add_suffix(low, end, diagonal, start, last, reach, buf, q_ref, o_ref, m_ref):
    m_ref[1:2, :] = jnp.where(reach, m_ref[0:1, :], -NEG)

    def block(at, size, masked, level=0):
        at = pl.multiple_of(at, TD)
        bound = last if masked == "both" else None
        mask = masker(start, bound, at, size) if masked else None
        add_block(buf[pl.ds(at, size), :], q_ref, o_ref, m_ref, mask, level)

    pl.when(low < end)(lambda: block(low * TD, TD, "start"))
    if diagonal:
        block(end * TD, TD, "both")
    between = jnp.maximum(end - 1 - low, 0)
    split = lax.rem(between, 2)
    pl.when(split == 1)(lambda: block((low + 1) * TD, TD, None, 1))

    def fully(b, _):
        block((low + 1 + split + 2 * b) * TD, 2 * TD, None, 1)
        return 0

    lax.fori_loop(0, between // 2, fully, 0)


def again_suffix(low, end, start, last, buf, q_ref, o_ref, m_ref):
    def again(i, _):
        at = pl.multiple_of(i * 256, 256)
        kv = buf[pl.ds(at, 256), :]
        mask = masker(start, last, at, 256)
        for t in range(4):
            online_step(
                q_ref[pl.ds(t * 256, 256), :], kv, o_ref, m_ref, pl.ds(t * 256, 256), mask(t * 256, 256)
            )
        return 0

    lax.fori_loop(low * 2, end * 2, again, 0)


def place():
    seq = lax.axis_index("seq")
    return seq // 8, lax.rem(seq // 2, 4), lax.rem(seq, 2)


def half_sources():
    x, y, c = place()
    rows = [y] + [lax.rem(y - k + 4, 4) for k in TURNS]
    return [r * 2 + d for r in rows for d in (c, 1 - c)]


def news_pairs(pays, buf, segs):
    src = half_sources()
    out = [(pays[j].at[pl.ds(SEG_AT, 16), :], segs.at[j]) for j in range(8)]
    for j in range(8):
        at = pl.multiple_of(src[j] * TD, TD)
        out.append((pays[j].at[pl.ds(0, TD), :], buf.at[pl.ds(at, TD), :]))
    return out


def count_same(segs, number, keep):
    total = jnp.zeros((16, 128), F32)
    for j in range(8):
        hit = segs[j].astype(F32) == jnp.where(keep[j], number, -2.0)
        total = total + jnp.where(hit, 1.0, 0.0)
    return jnp.sum(total).astype(jnp.int32)


def begin_kernel(ask_hbm, *refs, count):
    parts = refs[:count]
    o_ref, m_ref, stage, q_ref, buf, sem = refs[count:]
    copies = fetch_all(
        [(parts[j], buf.at[j]) for j in range(count)] + [(ask_hbm.at[pl.ds(0, TD), :], stage)], sem
    )
    o_ref[...] = jnp.zeros_like(o_ref)
    copies[count].wait()
    spread_heads(stage, q_ref)
    copies[0].wait()
    s = lax.dot_general(buf[0, :256, :], q_ref[...], NT, preferred_element_type=F32)
    m_ref[...] = jnp.broadcast_to(jnp.max(s, axis=0, keepdims=True), m_ref.shape)
    add_prefix(count, buf, sem, q_ref, o_ref, m_ref, True)

    @pl.when(too_large(o_ref))
    def _():
        o_ref[...] = jnp.zeros_like(o_ref)
        m_ref[...] = jnp.full_like(m_ref, NEG)
        again_prefix(count, buf, q_ref, o_ref, m_ref)


VM = pl.BlockSpec(memory_space=pltpu.VMEM)
HBM = pl.BlockSpec(memory_space=pl.ANY)
FAR = pl.BlockSpec(memory_space=pltpu.HBM)
STATE = [jax.ShapeDtypeStruct((NV, NQ), F32), jax.ShapeDtypeStruct((8, NQ), F32)]
ASK = [pltpu.VMEM((TD, 128), BF), pltpu.VMEM((NQ, 128), BF)]


def price(keys):
    return pl.CostEstimate(
        flops=keys * NQ * 2 * 600, bytes_accessed=keys * 256, transcendentals=keys * NQ
    )


def begin_call(ask, parts):
    count = len(parts)
    return pl.pallas_call(
        functools.partial(begin_kernel, count=count),
        in_specs=[HBM, FAR] + [HBM] * (count - 1),
        out_specs=[VM, VM],
        out_shape=STATE,
        scratch_shapes=ASK
        + [pltpu.VMEM((count, PRE, 128), BF), pltpu.SemaphoreType.DMA((count + 1,))],
        cost_estimate=price(count * PRE),
        compiler_params=room(20),
        name="attend_prefix",
    )(ask, *parts)


def partner_kernel(ask_hbm, o_in, m_in, *refs):
    pays = refs[:8]
    out_ref, stage, marks, q_ref, o_ref, m_ref, buf, segs, sem = refs[8:]
    o_ref[...] = o_in[...]
    m_ref[...] = m_in[...]

    @pl.when(place()[0] == 0)
    def _():
        copies = fetch_all(
            news_pairs(pays, buf, segs)
            + [
                (ask_hbm.at[pl.ds(0, TD), :], stage),
                (ask_hbm.at[pl.ds(SEG_AT, 16), :], marks),
            ],
            sem,
        )
        for v in copies[:8] + copies[16:]:
            v.wait()
        spread_heads(stage, q_ref)
        newest = segs[0].astype(F32)
        for j in range(1, 8):
            newest = jnp.maximum(newest, segs[j].astype(F32))
        newest = jnp.max(newest)
        begin = 8 * TD - count_same(segs, newest, [True] * 8)
        seg = marks[...].astype(F32)
        row = jnp.concatenate([seg[k : k + 1, :] for k in range(4)], axis=1)
        row = jnp.concatenate([row, row], axis=1)
        start = jnp.where(row == newest, begin, 8 * TD)
        last = jnp.full((1, NQ), 8 * TD, jnp.int32)
        low = jnp.min(start) // TD
        for v in copies[8:16]:
            v.wait()
        add_suffix(low, 8, False, start, None, row == newest, buf, q_ref, o_ref, m_ref)

        @pl.when(too_large(o_ref))
        def _():
            o_ref[...] = o_in[...]
            m_ref[...] = m_in[...]
            again_suffix(low, 8, start, last, buf, q_ref, o_ref, m_ref)

    out_ref[:HD, :] = o_ref[:HD, :]
    first = lax.broadcasted_iota(jnp.int32, (8, NQ), 0) == 0
    out_ref[HD:, :] = jnp.where(first, o_ref[HD : HD + 1, :], m_ref[0:1, :])


def partner_call(ask, state, pays):
    return pl.pallas_call(
        partner_kernel,
        in_specs=[HBM, VM, VM] + [HBM] * 8,
        out_specs=VM,
        out_shape=jax.ShapeDtypeStruct((MSG, NQ), F32),
        scratch_shapes=[
            ASK[0],
            pltpu.VMEM((16, 128), BF),
            ASK[1],
            pltpu.VMEM((NV, NQ), F32),
            pltpu.VMEM((8, NQ), F32),
            pltpu.VMEM((8 * TD, 128), BF),
            pltpu.VMEM((8, 16, 128), BF),
            pltpu.SemaphoreType.DMA((18,)),
        ],
        cost_estimate=price(3 * TD),
        compiler_params=room(20),
        name="attend_partner",
    )(ask, state[0], state[1], *pays)


def own_kernel(ask_hbm, row_ref, o_in, m_in, *refs):
    parts = refs[:6]
    pays = refs[6:14]
    out_ref, top_ref, stage, q_ref, o_ref, m_ref, pre, buf, segs, sem, pre_sem = refs[14:]
    x, y, c = place()
    asked = pltpu.make_async_copy(ask_hbm.at[pl.ds(0, TD), :], stage, sem.at[16])
    asked.start()
    fetch_all([(parts[j], pre.at[j]) for j in range(6)], pre_sem)
    copies = fetch_all(news_pairs(pays, buf, segs), sem)
    o_ref[...] = o_in[...]
    m_ref[...] = m_in[...]
    asked.wait()
    spread_heads(stage, q_ref)
    add_prefix(6, pre, pre_sem, q_ref, o_ref, m_ref, False)
    for v in copies:
        v.wait()
    own = y * 2 + c
    row = row_ref[1:2, :]
    mine = jnp.max(jnp.where(lax.broadcasted_iota(jnp.int32, (1, NQ), 1) == 0, row, -1.0))
    src = half_sources()
    begin = own * TD - count_same(segs, mine, [v < own for v in src])
    start = jnp.where(row == mine, begin, row_ref[0:1, :].astype(jnp.int32) + own * TD)
    lane = lax.broadcasted_iota(jnp.int32, (1, NQ), 1)
    last = own * TD + jnp.where(lane >= TD, lane - TD, lane)
    low = begin // TD
    add_suffix(low, own, True, start, last, row == mine, buf, q_ref, o_ref, m_ref)

    @pl.when(too_large(o_ref))
    def _():
        o_ref[...] = o_in[...]
        m_ref[...] = m_in[...]
        again_prefix(6, pre, q_ref, o_ref, m_ref)
        again_suffix(low, own + 1, start, last, buf, q_ref, o_ref, m_ref)

    out_ref[...] = o_ref[...]
    top_ref[...] = m_ref[...]


def own_call(ask, rows, state, parts, pays):
    return pl.pallas_call(
        own_kernel,
        in_specs=[HBM, VM, VM, VM] + [HBM] * 14,
        out_specs=[VM, VM],
        out_shape=STATE,
        scratch_shapes=ASK
        + [
            pltpu.VMEM((NV, NQ), F32),
            pltpu.VMEM((8, NQ), F32),
            pltpu.VMEM((6, PRE, 128), BF),
            pltpu.VMEM((8 * TD, 128), BF),
            pltpu.VMEM((8, 16, 128), BF),
            pltpu.SemaphoreType.DMA((17,)),
            pltpu.SemaphoreType.DMA((6,)),
        ],
        cost_estimate=price(9 * PRE),
        compiler_params=room(20),
        name="attend_own",
    )(ask, rows, state[0], state[1], *parts, *pays)


def join_kernel(o_ref, m_ref, msg_ref, out_ref):
    far = msg_ref[HD + 1 : HD + 2, :]
    near = m_ref[0:1, :]
    top = jnp.maximum(near, far)
    wa, wb = jnp.exp(near - top), jnp.exp(far - top)
    total = o_ref[: HD + 8, :] * wa + msg_ref[...] * wb
    mixed = total[:HD, :] / total[HD : HD + 1, :]
    both = jnp.concatenate([mixed[:, :TD], mixed[:, TD:]], axis=0)
    out_ref[...] = jnp.transpose(both).astype(BF)


def mix_kernel(
    att_ref, tok_hbm, gain_ref, route_ref, weight_ref, w0, w1, w2, w3, w4, res_ref, xi_ref, tok, sem
):
    tp = lax.axis_index("tp")
    fetch = pltpu.make_async_copy(
        tok_hbm.at[pl.ds(pl.multiple_of(tp * ROWS, ROWS), ROWS), :], tok, sem
    )
    fetch.start()
    q, z = tp // 4, lax.rem(tp, 4)
    side = 1 + 2 * place()[2]
    back = [0, side, 4 - side, 2]
    total = jnp.zeros((ROWS, 1024), F32)
    for j in range(4):
        row = lax.rem(z - back[j] + 4, 4)
        pair = jnp.concatenate([att_ref[q * 4 + row], att_ref[(1 - q) * 4 + row]], axis=1)
        w = jnp.concatenate([w0[0], w1[0]], axis=0) if j == 0 else (w2, w3, w4)[j - 1][...].reshape(256, 1024)
        total = total + jnp.dot(pair, w, preferred_element_type=F32)
    line = lax.broadcasted_iota(jnp.int32, (128, ROWS), 0)
    table = jnp.zeros((128, ROWS), F32)
    for k in range(8):
        expert = route_ref[k : k + 1, :]
        weight = weight_ref[k : k + 1, :]
        high = weight.astype(BF).astype(F32)
        table = table + jnp.where(line == expert, high, 0.0)
        table = table + jnp.where(line == expert + 32, weight - high, 0.0)
    gates = jnp.transpose(table).astype(BF)
    fetch.wait()
    total = tok[...].astype(F32) + total
    res_ref[...] = total
    xi = rms(total, gain_ref[...]).astype(BF)
    for j in range(8):
        xi_ref[j, :, :1024] = xi
        xi_ref[j, :, 1024:] = gates


def mix_call(att, tokens, gain, routes, weights, ws):
    return pl.pallas_call(
        mix_kernel,
        in_specs=[VM, HBM] + [VM] * 8,
        out_specs=[VM, VM],
        out_shape=[
            jax.ShapeDtypeStruct((ROWS, 1024), F32),
            jax.ShapeDtypeStruct((8, ROWS, 1152), BF),
        ],
        scratch_shapes=[pltpu.VMEM((ROWS, 1024), BF), pltpu.SemaphoreType.DMA],
        compiler_params=room(12),
        name="mix",
    )(att, tokens, gain, routes, weights, *ws)


def expert_kernel(x_ref, wi_own, wi_peer, wo_own, wo_peer, out_ref, acc):
    x, y, c = place()
    for e in range(4):
        wi, wo = ((wi_own, wo_own), (wi_peer, wo_peer))[e // 2]
        number = (x * 8 + y * 2 + (c if e < 2 else 1 - c)) * 2 + e % 2

        def half(h, _):
            rows = pl.ds(pl.multiple_of(h * 256, 256), 256)
            joined = jnp.dot(x_ref[rows, :1024], wi[e % 2], preferred_element_type=F32)
            g = joined[:, :512]
            hidden = (g / (1.0 + jnp.exp(-g)) * joined[:, 512:]).astype(BF)
            o = jnp.dot(hidden, wo[e % 2], preferred_element_type=F32).astype(BF).astype(F32)
            lane = lax.broadcasted_iota(jnp.int32, (256, 128), 1)
            hit = (lane == number) | (lane == number + 32)
            table = x_ref[rows, 1024:].astype(F32)
            gate = jnp.sum(jnp.where(hit, table, 0.0), axis=1, keepdims=True)
            o = o * gate
            if e:
                o = acc[rows, :] + o
            if e < 3:
                acc[rows, :] = o
            else:
                out_ref[rows, :] = o.astype(BF)
            return 0

        lax.fori_loop(0, 2, half, 0, unroll=2)


def expert_call(x, wi_own, wi_peer, wo_own, wo_peer):
    return pl.pallas_call(
        expert_kernel,
        in_specs=[VM] * 5,
        out_specs=VM,
        scratch_shapes=[pltpu.VMEM((512, 1024), F32)],
        out_shape=jax.ShapeDtypeStruct((512, 1024), BF),
        compiler_params=room(EXPERT_ROOM),
        name="experts",
    )(x, wi_own, wi_peer, wo_own, wo_peer)


EXPERT_ROOM = 30


def body(
    tokens,
    segment_ids,
    prefix_cache,
    norm1_gain,
    w_qkv,
    w_out,
    norm2_gain,
    expert_in,
    expert_out,
    routes,
    route_weights,
):
    tie = lax.optimization_barrier

    def swap(v):
        return lax.ppermute(v, "seq", CORE)

    def across(v):
        return lax.ppermute(v, "seq", ACROSS)

    def round_y(v):
        return [
            lax.ppermute(v, "seq", seq_perm(lambda a, b, d, k=k: (a, (b + k) % 4, d)))
            for k in TURNS
        ]

    pre = prefix_cache.reshape(PRE, 128)
    wx = lax.ppermute(w_out, "tp", tp_perm(lambda a, b: (1 - a, b)))
    far_pre = round_y(pre)
    near_pre = [swap(pre)]
    pay, ask, rows, new = pl.pallas_call(
        project_kernel,
        out_shape=[
            jax.ShapeDtypeStruct((PAY, 128), BF),
            jax.ShapeDtypeStruct((PAY, 128), BF),
            jax.ShapeDtypeStruct((8, NQ), F32),
            jax.ShapeDtypeStruct((TD, 128), BF),
        ],
        in_specs=[FAR] * 4,
        scratch_shapes=[
            pltpu.VMEM((TD, 1024), BF),
            pltpu.VMEM((1, 1024), F32),
            pltpu.VMEM((1024, 256), BF),
            pltpu.VMEM((4, 128), jnp.int32),
            pltpu.SemaphoreType.DMA((7,)),
        ],
        cost_estimate=pl.CostEstimate(
            flops=2 * TD * 1024 * 256, bytes_accessed=2 << 20, transcendentals=TD
        ),
        name="project",
    )(tokens, norm1_gain[None, :], w_qkv.reshape(1024, 256), segment_ids.reshape(4, 128))
    asked = across(ask)
    first = begin_call(ask, [pre, near_pre[0]])

    far_pre, asked, first, pay = tie((far_pre, asked, first, pay))
    near_pre += [swap(v) for v in far_pre]
    near_new = [swap(pay)]
    near_new, pay = tie((near_new, pay))
    far_new = round_y(pay)
    wpair = jnp.concatenate([w_out, wx])
    side = lax.ppermute(wpair, ("seq", "tp"), SIDES)
    opposite = lax.ppermute(wpair, "tp", tp_perm(lambda a, b: (a, (b + 2) % 4)))
    shards = [v for p in zip([pre] + far_pre, near_pre) for v in p]
    second = begin_call(asked, shards)

    far_new, second = tie((far_new, second))
    near_new += [swap(v) for v in far_new]
    pays = [v for p in zip([pay] + far_new, near_new) for v in p]
    message = partner_call(asked, second, pays)

    side, opposite, near_new, message, expert_in_t, expert_out_t = tie(
        (side, opposite, near_new, message, expert_in, expert_out)
    )
    wz = [side, swap(side), opposite]
    returned = across(message)
    wi_peer = swap(expert_in_t)
    wo_peer = swap(expert_out_t)
    o, m = own_call(ask, rows, first, shards[2:], pays)
    attended = pl.pallas_call(
        join_kernel, out_shape=jax.ShapeDtypeStruct((TD, 128), BF), compiler_params=room(8), name="join"
    )(o, m, returned)

    spread = lax.all_to_all(attended.reshape(8, ROWS, 128), "tp", 0, 0, tiled=True)
    residual, copies = mix_call(
        spread,
        tokens,
        norm2_gain[None, :],
        jnp.transpose(routes),
        jnp.transpose(route_weights),
        [w_out, wx] + wz,
    )
    everyone = lax.all_to_all(copies, "seq", 0, 0, axis_index_groups=CHIP_GROUPS, tiled=True)
    partial = expert_call(
        everyone.reshape(512, 1152), expert_in, wi_peer, expert_out, wo_peer
    )
    back = lax.all_to_all(
        partial.reshape(8, ROWS, 1024), "seq", 0, 0, axis_index_groups=CHIP_GROUPS, tiled=True
    )
    hidden = (residual + jnp.sum(back.astype(F32), axis=0)).astype(BF)
    return hidden, new.reshape(TD, 1, 128)


def solution(mesh):
    in_specs = (
        P("seq", None),
        P("seq"),
        P("seq", "tp", None),
        P(),
        P(None, "tp", None),
        P("tp", None, None),
        P(),
        P("seq", None, None),
        P("seq", None, None),
        P(("seq", "tp"), None),
        P(("seq", "tp"), None),
    )
    out_specs = (P(("seq", "tp"), None), P("seq", "tp", None))
    return jax.shard_map(body, mesh=mesh, in_specs=in_specs, out_specs=out_specs, check_vma=False)
```

```python
import functools

import jax
import jax.numpy as jnp
from jax import lax
from jax.experimental import pallas as pl
from jax.experimental.pallas import tpu as pltpu
from jax.sharding import PartitionSpec as P

SCALE = 0.015625
EPS = 1e-06
HD = 64
NV = 80
TD = 512
PRE = 1024
ROWS = 64
TQ = 512
NQ = 2 * TD
SEG_AT = TD
PAY = SEG_AT + 16
MSG = 72
LIMIT = 1e26
NEG = -1e30
NT = (((1,), (1,)), ((), ()))
F32 = jnp.float32
BF = jnp.bfloat16


def seq_perm(move):
    return [
        (x * 8 + y * 2 + c, (lambda t: t[0] * 8 + t[1] * 2 + t[2])(move(x, y, c)))
        for x in range(2)
        for y in range(4)
        for c in range(2)
    ]


def tp_perm(move):
    return [(q * 4 + z, (lambda t: t[0] * 4 + t[1])(move(q, z))) for q in range(2) for z in range(4)]


CORE = seq_perm(lambda x, y, c: (x, y, 1 - c))
ACROSS = seq_perm(lambda x, y, c: (1 - x, y, c))
TURNS = (1, 3, 2)
SIDES = [
    (s * 8 + q * 4 + z, s * 8 + q * 4 + (z + (1 if s % 2 == 0 else 3)) % 4)
    for s in range(16)
    for q in range(2)
    for z in range(4)
]
CHIP_GROUPS = [[x * 8 + y * 2 + c for x in range(2) for y in range(4)] for c in range(2)]


def room(mib):
    return pltpu.CompilerParams(vmem_limit_bytes=mib << 20)


def rms(wide, gain):
    mean_square = jnp.mean(wide * wide, axis=-1, keepdims=True)
    return wide * lax.rsqrt(mean_square + EPS) * gain


def project_kernel(
    tok_hbm, gain_hbm, w_hbm, seg_hbm, pay_ref, ask_ref, row_ref, new_ref, tok, gain, w, seg_in, sem
):
    small = [
        pltpu.make_async_copy(w_hbm, w, sem.at[4]),
        pltpu.make_async_copy(gain_hbm, gain, sem.at[5]),
        pltpu.make_async_copy(seg_hbm, seg_in, sem.at[6]),
    ]
    large = [
        pltpu.make_async_copy(tok_hbm.at[pl.ds(i * 128, 128), :], tok.at[pl.ds(i * 128, 128), :], sem.at[i])
        for i in range(4)
    ]
    for v in [large[0]] + small + large[1:]:
        v.start()
    for v in small:
        v.wait()
    seg = seg_in[...].astype(F32)
    segs = jnp.concatenate([seg, jnp.full((12, 128), -1.0, F32)], axis=0).astype(BF)
    pay_ref[SEG_AT:, :] = segs
    ask_ref[SEG_AT:, :] = segs
    row = jnp.concatenate([seg[k : k + 1, :] for k in range(4)], axis=1)
    col = jnp.transpose(jnp.broadcast_to(row, (8, TD)))[:, 0:1]
    below = jnp.sum(jnp.where(col < row, 1.0, 0.0), axis=0, keepdims=True)
    row_ref[0:1, :] = jnp.concatenate([below, below], axis=1)
    row_ref[1:2, :] = jnp.concatenate([row, row], axis=1)
    for i in range(2):
        large[2 * i].wait()
        large[2 * i + 1].wait()
        rows = pl.ds(i * 256, 256)
        normed = rms(tok[rows, :].astype(F32), gain[...]).astype(BF)
        proj = jnp.dot(normed, w[...], preferred_element_type=F32)
        ask_ref[rows, :] = (proj[:, :128].astype(BF).astype(F32) * SCALE).astype(BF)
        new = proj[:, 128:].astype(BF)
        new_ref[rows, :] = new
        pay_ref[rows, :] = new


def values_t(kv):
    row = lax.broadcasted_iota(jnp.int32, (NV, 128), 0)
    col = lax.broadcasted_iota(jnp.int32, (NV, 128), 1)
    pick = jnp.where((col == row + HD) & (row < HD), 1.0, 0.0).astype(BF)
    vt = lax.dot_general(pick, kv, NT, preferred_element_type=F32)
    ones = lax.broadcasted_iota(jnp.int32, vt.shape, 0) >= HD
    return jnp.where(ones, 1.0, vt).astype(BF)


def online_step(q, kv, o_ref, m_ref, cols, mask):
    s = lax.dot_general(kv, q, NT, preferred_element_type=F32)
    if mask is not None:
        s = jnp.where(mask, s, NEG)
    m0 = m_ref[0:1, cols]
    m1 = jnp.maximum(m0, jnp.max(s, axis=0, keepdims=True))
    p = jnp.exp(s - m1).astype(BF)
    o_ref[:, cols] = o_ref[:, cols] * jnp.exp(m0 - m1) + jnp.dot(
        values_t(kv), p, preferred_element_type=F32
    )
    m_ref[0:1, cols] = m1


def spread_heads(stage, q_ref):
    wide = stage[...].astype(F32)
    low = lax.broadcasted_iota(jnp.int32, (TD, 128), 1) < HD
    q_ref[:TD, :] = jnp.where(low, wide, 0.0).astype(BF)
    q_ref[TD:, :] = jnp.where(low, pltpu.roll(wide, HD, 1), 0.0).astype(BF)


def fetch_all(pairs, sem):
    copies = [pltpu.make_async_copy(a, b, sem.at[i]) for i, (a, b) in enumerate(pairs)]
    for v in copies:
        v.start()
    return copies


def add_block(kv, q_ref, o_ref, m_ref, mask, level=0):
    vt = values_t(kv)
    for t in range(NQ // TQ):
        cols = pl.ds(t * TQ, TQ)
        s = lax.dot_general(kv, q_ref[cols, :], NT, preferred_element_type=F32)
        if mask is not None:
            s = jnp.where(mask(t * TQ, TQ), s, NEG)
        p = jnp.exp(s - m_ref[level : level + 1, cols]).astype(BF)
        o_ref[:, cols] = o_ref[:, cols] + jnp.dot(vt, p, preferred_element_type=F32)


def too_large(o_ref):
    return jnp.logical_not(jnp.max(o_ref[HD : HD + 1, :]) < LIMIT)


def add_prefix(count, buf, sem, q_ref, o_ref, m_ref, head):
    def wait(j):
        pltpu.make_async_copy(buf.at[0], buf.at[j], sem.at[j]).wait()

    def block(j, _):
        if head:
            pl.when(j > 0)(lambda: wait(j))
        else:
            wait(j)
        add_block(buf[j], q_ref, o_ref, m_ref, None)
        return 0

    lax.fori_loop(0, count, block, 0, unroll=2)


def again_prefix(count, buf, q_ref, o_ref, m_ref):
    def again(i, _):
        kv = buf[i // 4, pl.ds(pl.multiple_of(i % 4 * 256, 256), 256), :]
        for t in range(NQ // 256):
            cols = pl.ds(t * 256, 256)
            online_step(q_ref[cols, :], kv, o_ref, m_ref, cols, None)
        return 0

    lax.fori_loop(0, count * 4, again, 0)


def masker(start, last, at, size):
    def mask(t, width):
        key = at + lax.broadcasted_iota(jnp.int32, (size, width), 0)
        ok = key >= start[:, t : t + width]
        return ok if last is None else ok & (key <= last[:, t : t + width])

    return mask


def add_suffix(low, end, diagonal, start, last, reach, buf, q_ref, o_ref, m_ref):
    m_ref[1:2, :] = jnp.where(reach, m_ref[0:1, :], -NEG)

    def block(at, size, masked, level=0):
        at = pl.multiple_of(at, TD)
        bound = last if masked == "both" else None
        mask = masker(start, bound, at, size) if masked else None
        add_block(buf[pl.ds(at, size), :], q_ref, o_ref, m_ref, mask, level)

    pl.when(low < end)(lambda: block(low * TD, TD, "start"))
    pl.when(diagonal)(lambda: block(end * TD, TD, "both"))
    between = jnp.maximum(end - 1 - low, 0)
    split = lax.rem(between, 2)
    pl.when(split == 1)(lambda: block((low + 1) * TD, TD, None, 1))

    def fully(b, _):
        block((low + 1 + split + 2 * b) * TD, 2 * TD, None, 1)
        return 0

    lax.fori_loop(0, between // 2, fully, 0)


def again_suffix(low, end, start, last, buf, q_ref, o_ref, m_ref):
    def again(i, _):
        at = pl.multiple_of(i * 256, 256)
        kv = buf[pl.ds(at, 256), :]
        mask = masker(start, last, at, 256)
        for t in range(4):
            online_step(
                q_ref[pl.ds(t * 256, 256), :], kv, o_ref, m_ref, pl.ds(t * 256, 256), mask(t * 256, 256)
            )
        return 0

    lax.fori_loop(low * 2, end * 2, again, 0)


def place():
    seq = lax.axis_index("seq")
    return seq // 8, lax.rem(seq // 2, 4), lax.rem(seq, 2)


def half_sources():
    x, y, c = place()
    rows = [y] + [lax.rem(y - k + 4, 4) for k in TURNS]
    return [r * 2 + d for r in rows for d in (c, 1 - c)]


def news_pairs(pays, buf, segs):
    src = half_sources()
    out = [(pays[j].at[pl.ds(SEG_AT, 16), :], segs.at[j]) for j in range(8)]
    for j in range(8):
        at = pl.multiple_of(src[j] * TD, TD)
        out.append((pays[j].at[pl.ds(0, TD), :], buf.at[pl.ds(at, TD), :]))
    return out


def count_same(segs, number, keep):
    total = jnp.zeros((16, 128), F32)
    for j in range(8):
        hit = segs[j].astype(F32) == jnp.where(keep[j], number, -2.0)
        total = total + jnp.where(hit, 1.0, 0.0)
    return jnp.sum(total).astype(jnp.int32)


def begin_kernel(ask_hbm, *refs, count):
    parts = refs[:count]
    o_ref, m_ref, stage, q_ref, buf, sem = refs[count:]
    copies = fetch_all(
        [(parts[j], buf.at[j]) for j in range(count)] + [(ask_hbm.at[pl.ds(0, TD), :], stage)], sem
    )
    o_ref[...] = jnp.zeros_like(o_ref)
    copies[count].wait()
    spread_heads(stage, q_ref)
    copies[0].wait()
    s = lax.dot_general(buf[0, :256, :], q_ref[...], NT, preferred_element_type=F32)
    m_ref[...] = jnp.broadcast_to(jnp.max(s, axis=0, keepdims=True), m_ref.shape)
    add_prefix(count, buf, sem, q_ref, o_ref, m_ref, True)

    @pl.when(too_large(o_ref))
    def _():
        o_ref[...] = jnp.zeros_like(o_ref)
        m_ref[...] = jnp.full_like(m_ref, NEG)
        again_prefix(count, buf, q_ref, o_ref, m_ref)


VM = pl.BlockSpec(memory_space=pltpu.VMEM)
HBM = pl.BlockSpec(memory_space=pl.ANY)
FAR = pl.BlockSpec(memory_space=pltpu.HBM)
STATE = [jax.ShapeDtypeStruct((NV, NQ), F32), jax.ShapeDtypeStruct((8, NQ), F32)]
ASK = [pltpu.VMEM((TD, 128), BF), pltpu.VMEM((NQ, 128), BF)]


def price(keys):
    return pl.CostEstimate(
        flops=keys * NQ * 2 * 600, bytes_accessed=keys * 256, transcendentals=keys * NQ
    )


def begin_call(ask, parts):
    count = len(parts)
    return pl.pallas_call(
        functools.partial(begin_kernel, count=count),
        in_specs=[HBM, FAR] + [HBM] * (count - 1),
        out_specs=[VM, VM],
        out_shape=STATE,
        scratch_shapes=ASK
        + [pltpu.VMEM((count, PRE, 128), BF), pltpu.SemaphoreType.DMA((count + 1,))],
        cost_estimate=price(count * PRE),
        compiler_params=room(20),
        name="attend_prefix",
    )(ask, *parts)


def own_terms(row_ref, segs, own):
    row = row_ref[1:2, :]
    mine = jnp.max(jnp.where(lax.broadcasted_iota(jnp.int32, (1, NQ), 1) == 0, row, -1.0))
    begin = own * TD - count_same(segs, mine, [v < own for v in half_sources()])
    start = jnp.where(row == mine, begin, row_ref[0:1, :].astype(jnp.int32) + own * TD)
    lane = lax.broadcasted_iota(jnp.int32, (1, NQ), 1)
    last = own * TD + jnp.where(lane >= TD, lane - TD, lane)
    return start, last, jnp.where(row == mine, 1, 0), begin // TD


def partner_terms(marks, segs):
    newest = segs[0].astype(F32)
    for j in range(1, 8):
        newest = jnp.maximum(newest, segs[j].astype(F32))
    newest = jnp.max(newest)
    begin = 8 * TD - count_same(segs, newest, [True] * 8)
    seg = marks[...].astype(F32)
    row = jnp.concatenate([seg[k : k + 1, :] for k in range(4)], axis=1)
    row = jnp.concatenate([row, row], axis=1)
    start = jnp.where(row == newest, begin, 8 * TD)
    last = jnp.full((1, NQ), 8 * TD, jnp.int32)
    return start, last, jnp.where(row == newest, 1, 0), jnp.min(start) // TD


def partner_kernel(ask_hbm, own_hbm, row_ref, o_in, m_in, o_own, m_own, *refs):
    pays = refs[:8]
    out_ref, o_out, m_out, stage, marks, q_ref, o_ref, m_ref, buf, segs, sem = refs[8:]
    x, y, c = place()
    own = y * 2 + c
    early = x == 0
    asked = pltpu.make_async_copy(ask_hbm.at[pl.ds(0, TD), :], stage, sem.at[17])
    mine = pltpu.make_async_copy(own_hbm.at[pl.ds(0, TD), :], stage, sem.at[17])
    pl.when(early)(lambda: asked.start())
    pl.when(jnp.logical_not(early))(lambda: mine.start())
    copies = fetch_all(
        news_pairs(pays, buf, segs) + [(ask_hbm.at[pl.ds(SEG_AT, 16), :], marks)], sem
    )

    def load():
        @pl.when(early)
        def _():
            o_ref[...] = o_in[...]
            m_ref[...] = m_in[...]

        @pl.when(jnp.logical_not(early))
        def _():
            o_ref[...] = o_own[...]
            m_ref[...] = m_own[...]

    load()
    for v in copies[:8] + copies[16:]:
        v.wait()
    asked.wait()
    spread_heads(stage, q_ref)
    theirs, ours = partner_terms(marks, segs), own_terms(row_ref, segs, own)
    start, last, reach, low = [jnp.where(early, a, b) for a, b in zip(theirs, ours)]
    end = jnp.where(early, 8, own)
    for v in copies[8:16]:
        v.wait()
    add_suffix(low, end, x == 1, start, last, reach == 1, buf, q_ref, o_ref, m_ref)

    @pl.when(too_large(o_ref))
    def _():
        load()
        again_suffix(low, end + x, start, last, buf, q_ref, o_ref, m_ref)

    first = lax.broadcasted_iota(jnp.int32, (8, NQ), 0) == 0

    def tell(o, m):
        out_ref[:HD, :] = o[:HD, :]
        out_ref[HD:, :] = jnp.where(first, o[HD : HD + 1, :], m[0:1, :])

    @pl.when(early)
    def _():
        tell(o_ref, m_ref)
        o_out[...] = o_own[...]
        m_out[...] = m_own[...]

    @pl.when(jnp.logical_not(early))
    def _():
        tell(o_in, m_in)
        o_out[...] = o_ref[...]
        m_out[...] = m_ref[...]


def partner_call(ask, own_ask, rows, state, own_state, pays):
    return pl.pallas_call(
        partner_kernel,
        in_specs=[HBM, HBM] + [VM] * 5 + [HBM] * 8,
        out_specs=[VM] * 3,
        out_shape=[jax.ShapeDtypeStruct((MSG, NQ), F32)] + STATE,
        scratch_shapes=[
            ASK[0],
            pltpu.VMEM((16, 128), BF),
            ASK[1],
            pltpu.VMEM((NV, NQ), F32),
            pltpu.VMEM((8, NQ), F32),
            pltpu.VMEM((8 * TD, 128), BF),
            pltpu.VMEM((8, 16, 128), BF),
            pltpu.SemaphoreType.DMA((18,)),
        ],
        cost_estimate=price(3 * TD),
        compiler_params=room(20),
        name="attend_partner",
    )(ask, own_ask, rows, *state, *own_state, *pays)


def own_kernel(ask_hbm, row_ref, o_in, m_in, *refs):
    parts = refs[:6]
    pays = refs[6:14]
    out_ref, top_ref, stage, q_ref, o_ref, m_ref, pre, buf, segs, sem, pre_sem = refs[14:]
    x, y, c = place()
    own = y * 2 + c
    asked = pltpu.make_async_copy(ask_hbm.at[pl.ds(0, TD), :], stage, sem.at[16])
    asked.start()
    fetch_all([(parts[j], pre.at[j]) for j in range(6)], pre_sem)
    copies = [
        pltpu.make_async_copy(a, b, sem.at[i])
        for i, (a, b) in enumerate(news_pairs(pays, buf, segs))
    ]

    @pl.when(x == 0)
    def _():
        for v in copies:
            v.start()

    o_ref[...] = o_in[...]
    m_ref[...] = m_in[...]
    asked.wait()
    spread_heads(stage, q_ref)
    add_prefix(6, pre, pre_sem, q_ref, o_ref, m_ref, False)

    @pl.when(x == 0)
    def _():
        for v in copies:
            v.wait()
        start, last, reach, low = own_terms(row_ref, segs, own)
        add_suffix(low, own, x == 0, start, last, reach == 1, buf, q_ref, o_ref, m_ref)

    @pl.when(too_large(o_ref))
    def _():
        o_ref[...] = o_in[...]
        m_ref[...] = m_in[...]
        again_prefix(6, pre, q_ref, o_ref, m_ref)

        @pl.when(x == 0)
        def _():
            start, last, reach, low = own_terms(row_ref, segs, own)
            again_suffix(low, own + 1, start, last, buf, q_ref, o_ref, m_ref)

    out_ref[...] = o_ref[...]
    top_ref[...] = m_ref[...]


def own_call(ask, rows, state, parts, pays):
    return pl.pallas_call(
        own_kernel,
        in_specs=[HBM, VM, VM, VM] + [HBM] * 14,
        out_specs=[VM, VM],
        out_shape=STATE,
        scratch_shapes=ASK
        + [
            pltpu.VMEM((NV, NQ), F32),
            pltpu.VMEM((8, NQ), F32),
            pltpu.VMEM((6, PRE, 128), BF),
            pltpu.VMEM((8 * TD, 128), BF),
            pltpu.VMEM((8, 16, 128), BF),
            pltpu.SemaphoreType.DMA((17,)),
            pltpu.SemaphoreType.DMA((6,)),
        ],
        cost_estimate=price(9 * PRE),
        compiler_params=room(20),
        name="attend_own",
    )(ask, rows, state[0], state[1], *parts, *pays)


def join_kernel(o_ref, m_ref, msg_ref, out_ref):
    far = msg_ref[HD + 1 : HD + 2, :]
    near = m_ref[0:1, :]
    top = jnp.maximum(near, far)
    wa, wb = jnp.exp(near - top), jnp.exp(far - top)
    total = o_ref[: HD + 8, :] * wa + msg_ref[...] * wb
    mixed = total[:HD, :] / total[HD : HD + 1, :]
    both = jnp.concatenate([mixed[:, :TD], mixed[:, TD:]], axis=0)
    out_ref[...] = jnp.transpose(both).astype(BF)


def mix_kernel(
    att_ref, tok_hbm, gain_ref, route_ref, weight_ref, w0, w1, w2, w3, w4, res_ref, xi_ref, tok, sem
):
    tp = lax.axis_index("tp")
    fetch = pltpu.make_async_copy(
        tok_hbm.at[pl.ds(pl.multiple_of(tp * ROWS, ROWS), ROWS), :], tok, sem
    )
    fetch.start()
    q, z = tp // 4, lax.rem(tp, 4)
    side = 1 + 2 * place()[2]
    back = [0, side, 4 - side, 2]
    total = jnp.zeros((ROWS, 1024), F32)
    for j in range(4):
        row = lax.rem(z - back[j] + 4, 4)
        pair = jnp.concatenate([att_ref[q * 4 + row], att_ref[(1 - q) * 4 + row]], axis=1)
        w = jnp.concatenate([w0[0], w1[0]], axis=0) if j == 0 else (w2, w3, w4)[j - 1][...].reshape(256, 1024)
        total = total + jnp.dot(pair, w, preferred_element_type=F32)
    line = lax.broadcasted_iota(jnp.int32, (128, ROWS), 0)
    table = jnp.zeros((128, ROWS), F32)
    for k in range(8):
        expert = route_ref[k : k + 1, :]
        weight = weight_ref[k : k + 1, :]
        high = weight.astype(BF).astype(F32)
        table = table + jnp.where(line == expert, high, 0.0)
        table = table + jnp.where(line == expert + 32, weight - high, 0.0)
    gates = jnp.transpose(table).astype(BF)
    fetch.wait()
    total = tok[...].astype(F32) + total
    res_ref[...] = total
    xi = rms(total, gain_ref[...]).astype(BF)
    for j in range(8):
        xi_ref[j, :, :1024] = xi
        xi_ref[j, :, 1024:] = gates


def mix_call(att, tokens, gain, routes, weights, ws):
    return pl.pallas_call(
        mix_kernel,
        in_specs=[VM, HBM] + [VM] * 8,
        out_specs=[VM, VM],
        out_shape=[
            jax.ShapeDtypeStruct((ROWS, 1024), F32),
            jax.ShapeDtypeStruct((8, ROWS, 1152), BF),
        ],
        scratch_shapes=[pltpu.VMEM((ROWS, 1024), BF), pltpu.SemaphoreType.DMA],
        compiler_params=room(12),
        name="mix",
    )(att, tokens, gain, routes, weights, *ws)


def expert_kernel(x_ref, wi_own, wi_peer, wo_own, wo_peer, out_ref, acc):
    x, y, c = place()
    for e in range(4):
        wi, wo = ((wi_own, wo_own), (wi_peer, wo_peer))[e // 2]
        number = (x * 8 + y * 2 + (c if e < 2 else 1 - c)) * 2 + e % 2

        def half(h, _):
            rows = pl.ds(pl.multiple_of(h * 256, 256), 256)
            joined = jnp.dot(x_ref[rows, :1024], wi[e % 2], preferred_element_type=F32)
            g = joined[:, :512]
            hidden = (g / (1.0 + jnp.exp(-g)) * joined[:, 512:]).astype(BF)
            o = jnp.dot(hidden, wo[e % 2], preferred_element_type=F32).astype(BF).astype(F32)
            lane = lax.broadcasted_iota(jnp.int32, (256, 128), 1)
            hit = (lane == number) | (lane == number + 32)
            table = x_ref[rows, 1024:].astype(F32)
            gate = jnp.sum(jnp.where(hit, table, 0.0), axis=1, keepdims=True)
            o = o * gate
            if e:
                o = acc[rows, :] + o
            if e < 3:
                acc[rows, :] = o
            else:
                out_ref[rows, :] = o.astype(BF)
            return 0

        lax.fori_loop(0, 2, half, 0, unroll=2)


def expert_call(x, wi_own, wi_peer, wo_own, wo_peer):
    return pl.pallas_call(
        expert_kernel,
        in_specs=[VM] * 5,
        out_specs=VM,
        scratch_shapes=[pltpu.VMEM((512, 1024), F32)],
        out_shape=jax.ShapeDtypeStruct((512, 1024), BF),
        compiler_params=room(EXPERT_ROOM),
        name="experts",
    )(x, wi_own, wi_peer, wo_own, wo_peer)


EXPERT_ROOM = 30


def body(
    tokens,
    segment_ids,
    prefix_cache,
    norm1_gain,
    w_qkv,
    w_out,
    norm2_gain,
    expert_in,
    expert_out,
    routes,
    route_weights,
):
    tie = lax.optimization_barrier

    def swap(v):
        return lax.ppermute(v, "seq", CORE)

    def across(v):
        return lax.ppermute(v, "seq", ACROSS)

    def round_y(v):
        return [
            lax.ppermute(v, "seq", seq_perm(lambda a, b, d, k=k: (a, (b + k) % 4, d)))
            for k in TURNS
        ]

    pre = prefix_cache.reshape(PRE, 128)
    wx = lax.ppermute(w_out, "tp", tp_perm(lambda a, b: (1 - a, b)))
    far_pre = round_y(pre)
    near_pre = [swap(pre)]
    pay, ask, rows, new = pl.pallas_call(
        project_kernel,
        out_shape=[
            jax.ShapeDtypeStruct((PAY, 128), BF),
            jax.ShapeDtypeStruct((PAY, 128), BF),
            jax.ShapeDtypeStruct((8, NQ), F32),
            jax.ShapeDtypeStruct((TD, 128), BF),
        ],
        in_specs=[FAR] * 4,
        scratch_shapes=[
            pltpu.VMEM((TD, 1024), BF),
            pltpu.VMEM((1, 1024), F32),
            pltpu.VMEM((1024, 256), BF),
            pltpu.VMEM((4, 128), jnp.int32),
            pltpu.SemaphoreType.DMA((7,)),
        ],
        cost_estimate=pl.CostEstimate(
            flops=2 * TD * 1024 * 256, bytes_accessed=2 << 20, transcendentals=TD
        ),
        name="project",
    )(tokens, norm1_gain[None, :], w_qkv.reshape(1024, 256), segment_ids.reshape(4, 128))
    asked = across(ask)
    first = begin_call(ask, [pre, near_pre[0]])

    far_pre, asked, first, pay = tie((far_pre, asked, first, pay))
    near_pre += [swap(v) for v in far_pre]
    near_new = [swap(pay)]
    near_new, pay = tie((near_new, pay))
    far_new = round_y(pay)
    wpair = jnp.concatenate([w_out, wx])
    side = lax.ppermute(wpair, ("seq", "tp"), SIDES)
    opposite = lax.ppermute(wpair, "tp", tp_perm(lambda a, b: (a, (b + 2) % 4)))
    shards = [v for p in zip([pre] + far_pre, near_pre) for v in p]
    second = begin_call(asked, shards)

    far_new, second = tie((far_new, second))
    near_new += [swap(v) for v in far_new]
    pays = [v for p in zip([pay] + far_new, near_new) for v in p]
    message, *first = partner_call(asked, ask, rows, second, first, pays)

    side, opposite, near_new, message, first, expert_in_t, expert_out_t = tie(
        (side, opposite, near_new, message, first, expert_in, expert_out)
    )
    wz = [side, swap(side), opposite]
    returned = across(message)
    wi_peer = swap(expert_in_t)
    wo_peer = swap(expert_out_t)
    o, m = own_call(ask, rows, first, shards[2:], pays)
    attended = pl.pallas_call(
        join_kernel, out_shape=jax.ShapeDtypeStruct((TD, 128), BF), compiler_params=room(8), name="join"
    )(o, m, returned)

    spread = lax.all_to_all(attended.reshape(8, ROWS, 128), "tp", 0, 0, tiled=True)
    residual, copies = mix_call(
        spread,
        tokens,
        norm2_gain[None, :],
        jnp.transpose(routes),
        jnp.transpose(route_weights),
        [w_out, wx] + wz,
    )
    everyone = lax.all_to_all(copies, "seq", 0, 0, axis_index_groups=CHIP_GROUPS, tiled=True)
    partial = expert_call(
        everyone.reshape(512, 1152), expert_in, wi_peer, expert_out, wo_peer
    )
    back = lax.all_to_all(
        partial.reshape(8, ROWS, 1024), "seq", 0, 0, axis_index_groups=CHIP_GROUPS, tiled=True
    )
    hidden = (residual + jnp.sum(back.astype(F32), axis=0)).astype(BF)
    return hidden, new.reshape(TD, 1, 128)


def solution(mesh):
    in_specs = (
        P("seq", None),
        P("seq"),
        P("seq", "tp", None),
        P(),
        P(None, "tp", None),
        P("tp", None, None),
        P(),
        P("seq", None, None),
        P("seq", None, None),
        P(("seq", "tp"), None),
        P(("seq", "tp"), None),
    )
    out_specs = (P(("seq", "tp"), None), P("seq", "tp", None))
    return jax.shard_map(body, mesh=mesh, in_specs=in_specs, out_specs=out_specs, check_vma=False)
```

```python
import functools

import jax
import jax.numpy as jnp
from jax import lax
from jax.experimental import pallas as pl
from jax.experimental.pallas import tpu as pltpu
from jax.sharding import PartitionSpec as P

SCALE = 0.015625
EPS = 1e-06
HD = 64
NV = 80
TD = 512
PRE = 1024
ROWS = 64
TQ = 1024
NQ = 2 * TD
SEG_AT = TD
PAY = SEG_AT + 16
MSG = 72
LIMIT = 1e26
NEG = -1e30
NT = (((1,), (1,)), ((), ()))
F32 = jnp.float32
BF = jnp.bfloat16


def seq_perm(move):
    return [
        (x * 8 + y * 2 + c, (lambda t: t[0] * 8 + t[1] * 2 + t[2])(move(x, y, c)))
        for x in range(2)
        for y in range(4)
        for c in range(2)
    ]


def tp_perm(move):
    return [(q * 4 + z, (lambda t: t[0] * 4 + t[1])(move(q, z))) for q in range(2) for z in range(4)]


CORE = seq_perm(lambda x, y, c: (x, y, 1 - c))
ACROSS = seq_perm(lambda x, y, c: (1 - x, y, c))
TURNS = (1, 3, 2)
SIDES = [
    (s * 8 + q * 4 + z, s * 8 + q * 4 + (z + (1 if s % 2 == 0 else 3)) % 4)
    for s in range(16)
    for q in range(2)
    for z in range(4)
]
CHIP_GROUPS = [[x * 8 + y * 2 + c for x in range(2) for y in range(4)] for c in range(2)]


def room(mib):
    return pltpu.CompilerParams(vmem_limit_bytes=mib << 20)


def rms(wide, gain):
    mean_square = jnp.mean(wide * wide, axis=-1, keepdims=True)
    return wide * lax.rsqrt(mean_square + EPS) * gain


def project_kernel(
    tok_hbm, gain_hbm, w_hbm, seg_hbm, pay_ref, ask_ref, row_ref, new_ref, tok, gain, w, seg_in, sem
):
    small = [
        pltpu.make_async_copy(w_hbm, w, sem.at[4]),
        pltpu.make_async_copy(gain_hbm, gain, sem.at[5]),
        pltpu.make_async_copy(seg_hbm, seg_in, sem.at[6]),
    ]
    large = [
        pltpu.make_async_copy(tok_hbm.at[pl.ds(i * 128, 128), :], tok.at[pl.ds(i * 128, 128), :], sem.at[i])
        for i in range(4)
    ]
    for v in [large[0]] + small + large[1:]:
        v.start()
    for v in small:
        v.wait()
    seg = seg_in[...].astype(F32)
    segs = jnp.concatenate([seg, jnp.full((12, 128), -1.0, F32)], axis=0).astype(BF)
    pay_ref[SEG_AT:, :] = segs
    ask_ref[SEG_AT:, :] = segs
    row = jnp.concatenate([seg[k : k + 1, :] for k in range(4)], axis=1)
    col = jnp.transpose(jnp.broadcast_to(row, (8, TD)))[:, 0:1]
    below = jnp.sum(jnp.where(col < row, 1.0, 0.0), axis=0, keepdims=True)
    row_ref[0:1, :] = jnp.concatenate([below, below], axis=1)
    row_ref[1:2, :] = jnp.concatenate([row, row], axis=1)
    for i in range(2):
        large[2 * i].wait()
        large[2 * i + 1].wait()
        rows = pl.ds(i * 256, 256)
        normed = rms(tok[rows, :].astype(F32), gain[...]).astype(BF)
        proj = jnp.dot(normed, w[...], preferred_element_type=F32)
        ask_ref[rows, :] = (proj[:, :128].astype(BF).astype(F32) * SCALE).astype(BF)
        new = proj[:, 128:].astype(BF)
        new_ref[rows, :] = new
        pay_ref[rows, :] = new


def values_t(kv):
    row = lax.broadcasted_iota(jnp.int32, (NV, 128), 0)
    col = lax.broadcasted_iota(jnp.int32, (NV, 128), 1)
    pick = jnp.where((col == row + HD) & (row < HD), 1.0, 0.0).astype(BF)
    vt = lax.dot_general(pick, kv, NT, preferred_element_type=F32)
    ones = lax.broadcasted_iota(jnp.int32, vt.shape, 0) >= HD
    return jnp.where(ones, 1.0, vt).astype(BF)


def online_step(q, kv, o_ref, m_ref, cols, mask):
    s = lax.dot_general(kv, q, NT, preferred_element_type=F32)
    if mask is not None:
        s = jnp.where(mask, s, NEG)
    m0 = m_ref[0:1, cols]
    m1 = jnp.maximum(m0, jnp.max(s, axis=0, keepdims=True))
    p = jnp.exp(s - m1).astype(BF)
    o_ref[:, cols] = o_ref[:, cols] * jnp.exp(m0 - m1) + jnp.dot(
        values_t(kv), p, preferred_element_type=F32
    )
    m_ref[0:1, cols] = m1


def spread_heads(stage, q_ref):
    wide = stage[...].astype(F32)
    low = lax.broadcasted_iota(jnp.int32, (TD, 128), 1) < HD
    q_ref[:TD, :] = jnp.where(low, wide, 0.0).astype(BF)
    q_ref[TD:, :] = jnp.where(low, pltpu.roll(wide, HD, 1), 0.0).astype(BF)


def fetch_all(pairs, sem):
    copies = [pltpu.make_async_copy(a, b, sem.at[i]) for i, (a, b) in enumerate(pairs)]
    for v in copies:
        v.start()
    return copies


def add_block(kv, q_ref, o_ref, m_ref, mask, level=0):
    vt = values_t(kv)
    for t in range(NQ // TQ):
        cols = pl.ds(t * TQ, TQ)
        s = lax.dot_general(kv, q_ref[cols, :], NT, preferred_element_type=F32)
        if mask is not None:
            s = jnp.where(mask(t * TQ, TQ), s, NEG)
        p = jnp.exp(s - m_ref[level : level + 1, cols]).astype(BF)
        o_ref[:, cols] = o_ref[:, cols] + jnp.dot(vt, p, preferred_element_type=F32)


def too_large(o_ref):
    return jnp.logical_not(jnp.max(o_ref[HD : HD + 1, :]) < LIMIT)


def add_prefix(count, buf, sem, q_ref, o_ref, m_ref, head):
    def wait(j):
        pltpu.make_async_copy(buf.at[0], buf.at[j], sem.at[j]).wait()

    def block(j, _):
        if head:
            pl.when(j > 0)(lambda: wait(j))
        else:
            wait(j)
        add_block(buf[j], q_ref, o_ref, m_ref, None)
        return 0

    lax.fori_loop(0, count, block, 0, unroll=2)


def again_prefix(count, buf, q_ref, o_ref, m_ref):
    def again(i, _):
        kv = buf[i // 4, pl.ds(pl.multiple_of(i % 4 * 256, 256), 256), :]
        for t in range(NQ // 256):
            cols = pl.ds(t * 256, 256)
            online_step(q_ref[cols, :], kv, o_ref, m_ref, cols, None)
        return 0

    lax.fori_loop(0, count * 4, again, 0)


def masker(start, last, at, size):
    def mask(t, width):
        key = at + lax.broadcasted_iota(jnp.int32, (size, width), 0)
        ok = key >= start[:, t : t + width]
        return ok if last is None else ok & (key <= last[:, t : t + width])

    return mask


def add_suffix(low, end, diagonal, start, last, reach, buf, q_ref, o_ref, m_ref):
    m_ref[1:2, :] = jnp.where(reach, m_ref[0:1, :], -NEG)

    def block(at, size, masked, level=0):
        at = pl.multiple_of(at, TD)
        bound = last if masked == "both" else None
        mask = masker(start, bound, at, size) if masked else None
        add_block(buf[pl.ds(at, size), :], q_ref, o_ref, m_ref, mask, level)

    pl.when(low < end)(lambda: block(low * TD, TD, "start"))
    pl.when(diagonal)(lambda: block(end * TD, TD, "both"))
    between = jnp.maximum(end - 1 - low, 0)
    split = lax.rem(between, 2)
    pl.when(split == 1)(lambda: block((low + 1) * TD, TD, None, 1))

    def fully(b, _):
        block((low + 1 + split + 2 * b) * TD, 2 * TD, None, 1)
        return 0

    lax.fori_loop(0, between // 2, fully, 0)


def again_suffix(low, end, start, last, buf, q_ref, o_ref, m_ref):
    def again(i, _):
        at = pl.multiple_of(i * 256, 256)
        kv = buf[pl.ds(at, 256), :]
        mask = masker(start, last, at, 256)
        for t in range(4):
            online_step(
                q_ref[pl.ds(t * 256, 256), :], kv, o_ref, m_ref, pl.ds(t * 256, 256), mask(t * 256, 256)
            )
        return 0

    lax.fori_loop(low * 2, end * 2, again, 0)


def place():
    seq = lax.axis_index("seq")
    return seq // 8, lax.rem(seq // 2, 4), lax.rem(seq, 2)


def half_sources():
    x, y, c = place()
    rows = [y] + [lax.rem(y - k + 4, 4) for k in TURNS]
    return [r * 2 + d for r in rows for d in (c, 1 - c)]


def news_pairs(pays, buf, segs):
    src = half_sources()
    out = [(pays[j].at[pl.ds(SEG_AT, 16), :], segs.at[j]) for j in range(8)]
    for j in range(8):
        at = pl.multiple_of(src[j] * TD, TD)
        out.append((pays[j].at[pl.ds(0, TD), :], buf.at[pl.ds(at, TD), :]))
    return out


def count_same(segs, number, keep):
    total = jnp.zeros((16, 128), F32)
    for j in range(8):
        hit = segs[j].astype(F32) == jnp.where(keep[j], number, -2.0)
        total = total + jnp.where(hit, 1.0, 0.0)
    return jnp.sum(total).astype(jnp.int32)


def begin_kernel(ask_hbm, *refs, count):
    parts = refs[:count]
    o_ref, m_ref, stage, q_ref, buf, sem = refs[count:]
    copies = fetch_all(
        [(parts[j], buf.at[j]) for j in range(count)] + [(ask_hbm.at[pl.ds(0, TD), :], stage)], sem
    )
    o_ref[...] = jnp.zeros_like(o_ref)
    copies[count].wait()
    spread_heads(stage, q_ref)
    copies[0].wait()
    s = lax.dot_general(buf[0, :256, :], q_ref[...], NT, preferred_element_type=F32)
    m_ref[...] = jnp.broadcast_to(jnp.max(s, axis=0, keepdims=True), m_ref.shape)
    add_prefix(count, buf, sem, q_ref, o_ref, m_ref, True)

    @pl.when(too_large(o_ref))
    def _():
        o_ref[...] = jnp.zeros_like(o_ref)
        m_ref[...] = jnp.full_like(m_ref, NEG)
        again_prefix(count, buf, q_ref, o_ref, m_ref)


VM = pl.BlockSpec(memory_space=pltpu.VMEM)
HBM = pl.BlockSpec(memory_space=pl.ANY)
FAR = pl.BlockSpec(memory_space=pltpu.HBM)
STATE = [jax.ShapeDtypeStruct((NV, NQ), F32), jax.ShapeDtypeStruct((8, NQ), F32)]
ASK = [pltpu.VMEM((TD, 128), BF), pltpu.VMEM((NQ, 128), BF)]


def price(keys):
    return pl.CostEstimate(
        flops=keys * NQ * 2 * 600, bytes_accessed=keys * 256, transcendentals=keys * NQ
    )


def begin_call(ask, parts):
    count = len(parts)
    return pl.pallas_call(
        functools.partial(begin_kernel, count=count),
        in_specs=[HBM, FAR] + [HBM] * (count - 1),
        out_specs=[VM, VM],
        out_shape=STATE,
        scratch_shapes=ASK
        + [pltpu.VMEM((count, PRE, 128), BF), pltpu.SemaphoreType.DMA((count + 1,))],
        cost_estimate=price(count * PRE),
        compiler_params=room(20),
        name="attend_prefix",
    )(ask, *parts)


def own_terms(row_ref, segs, own):
    row = row_ref[1:2, :]
    mine = jnp.max(jnp.where(lax.broadcasted_iota(jnp.int32, (1, NQ), 1) == 0, row, -1.0))
    begin = own * TD - count_same(segs, mine, [v < own for v in half_sources()])
    start = jnp.where(row == mine, begin, row_ref[0:1, :].astype(jnp.int32) + own * TD)
    lane = lax.broadcasted_iota(jnp.int32, (1, NQ), 1)
    last = own * TD + jnp.where(lane >= TD, lane - TD, lane)
    return start, last, jnp.where(row == mine, 1, 0), begin // TD


def partner_terms(marks, segs):
    newest = segs[0].astype(F32)
    for j in range(1, 8):
        newest = jnp.maximum(newest, segs[j].astype(F32))
    newest = jnp.max(newest)
    begin = 8 * TD - count_same(segs, newest, [True] * 8)
    seg = marks[...].astype(F32)
    row = jnp.concatenate([seg[k : k + 1, :] for k in range(4)], axis=1)
    row = jnp.concatenate([row, row], axis=1)
    start = jnp.where(row == newest, begin, 8 * TD)
    last = jnp.full((1, NQ), 8 * TD, jnp.int32)
    return start, last, jnp.where(row == newest, 1, 0), jnp.min(start) // TD


def partner_kernel(ask_hbm, own_hbm, row_ref, o_in, m_in, o_own, m_own, *refs):
    pays = refs[:8]
    out_ref, o_out, m_out, stage, marks, q_ref, o_ref, m_ref, buf, segs, sem = refs[8:]
    x, y, c = place()
    own = y * 2 + c
    early = x == 0
    asked = pltpu.make_async_copy(ask_hbm.at[pl.ds(0, TD), :], stage, sem.at[17])
    mine = pltpu.make_async_copy(own_hbm.at[pl.ds(0, TD), :], stage, sem.at[17])
    pl.when(early)(lambda: asked.start())
    pl.when(jnp.logical_not(early))(lambda: mine.start())
    copies = fetch_all(
        news_pairs(pays, buf, segs) + [(ask_hbm.at[pl.ds(SEG_AT, 16), :], marks)], sem
    )

    def load():
        @pl.when(early)
        def _():
            o_ref[...] = o_in[...]
            m_ref[...] = m_in[...]

        @pl.when(jnp.logical_not(early))
        def _():
            o_ref[...] = o_own[...]
            m_ref[...] = m_own[...]

    load()
    for v in copies[:8] + copies[16:]:
        v.wait()
    asked.wait()
    spread_heads(stage, q_ref)
    theirs, ours = partner_terms(marks, segs), own_terms(row_ref, segs, own)
    start, last, reach, low = [jnp.where(early, a, b) for a, b in zip(theirs, ours)]
    end = jnp.where(early, 8, own)
    for v in copies[8:16]:
        v.wait()
    add_suffix(low, end, x == 1, start, last, reach == 1, buf, q_ref, o_ref, m_ref)

    @pl.when(too_large(o_ref))
    def _():
        load()
        again_suffix(low, end + x, start, last, buf, q_ref, o_ref, m_ref)

    first = lax.broadcasted_iota(jnp.int32, (8, NQ), 0) == 0

    def tell(o, m):
        out_ref[:HD, :] = o[:HD, :]
        out_ref[HD:, :] = jnp.where(first, o[HD : HD + 1, :], m[0:1, :])

    @pl.when(early)
    def _():
        tell(o_ref, m_ref)
        o_out[...] = o_own[...]
        m_out[...] = m_own[...]

    @pl.when(jnp.logical_not(early))
    def _():
        tell(o_in, m_in)
        o_out[...] = o_ref[...]
        m_out[...] = m_ref[...]


def partner_call(ask, own_ask, rows, state, own_state, pays):
    return pl.pallas_call(
        partner_kernel,
        in_specs=[HBM, HBM] + [VM] * 5 + [HBM] * 8,
        out_specs=[VM] * 3,
        out_shape=[jax.ShapeDtypeStruct((MSG, NQ), F32)] + STATE,
        scratch_shapes=[
            ASK[0],
            pltpu.VMEM((16, 128), BF),
            ASK[1],
            pltpu.VMEM((NV, NQ), F32),
            pltpu.VMEM((8, NQ), F32),
            pltpu.VMEM((8 * TD, 128), BF),
            pltpu.VMEM((8, 16, 128), BF),
            pltpu.SemaphoreType.DMA((18,)),
        ],
        cost_estimate=price(3 * TD),
        compiler_params=room(20),
        name="attend_partner",
    )(ask, own_ask, rows, *state, *own_state, *pays)


def own_kernel(ask_hbm, row_ref, o_in, m_in, *refs):
    parts = refs[:6]
    pays = refs[6:14]
    out_ref, top_ref, stage, q_ref, o_ref, m_ref, pre, buf, segs, sem, pre_sem = refs[14:]
    x, y, c = place()
    own = y * 2 + c
    asked = pltpu.make_async_copy(ask_hbm.at[pl.ds(0, TD), :], stage, sem.at[16])
    asked.start()
    fetch_all([(parts[j], pre.at[j]) for j in range(6)], pre_sem)
    copies = [
        pltpu.make_async_copy(a, b, sem.at[i])
        for i, (a, b) in enumerate(news_pairs(pays, buf, segs))
    ]

    @pl.when(x == 0)
    def _():
        for v in copies:
            v.start()

    o_ref[...] = o_in[...]
    m_ref[...] = m_in[...]
    asked.wait()
    spread_heads(stage, q_ref)
    add_prefix(6, pre, pre_sem, q_ref, o_ref, m_ref, False)

    @pl.when(x == 0)
    def _():
        for v in copies:
            v.wait()
        start, last, reach, low = own_terms(row_ref, segs, own)
        add_suffix(low, own, x == 0, start, last, reach == 1, buf, q_ref, o_ref, m_ref)

    @pl.when(too_large(o_ref))
    def _():
        o_ref[...] = o_in[...]
        m_ref[...] = m_in[...]
        again_prefix(6, pre, q_ref, o_ref, m_ref)

        @pl.when(x == 0)
        def _():
            start, last, reach, low = own_terms(row_ref, segs, own)
            again_suffix(low, own + 1, start, last, buf, q_ref, o_ref, m_ref)

    out_ref[...] = o_ref[...]
    top_ref[...] = m_ref[...]


def own_call(ask, rows, state, parts, pays):
    return pl.pallas_call(
        own_kernel,
        in_specs=[HBM, VM, VM, VM] + [HBM] * 14,
        out_specs=[VM, VM],
        out_shape=STATE,
        scratch_shapes=ASK
        + [
            pltpu.VMEM((NV, NQ), F32),
            pltpu.VMEM((8, NQ), F32),
            pltpu.VMEM((6, PRE, 128), BF),
            pltpu.VMEM((8 * TD, 128), BF),
            pltpu.VMEM((8, 16, 128), BF),
            pltpu.SemaphoreType.DMA((17,)),
            pltpu.SemaphoreType.DMA((6,)),
        ],
        cost_estimate=price(9 * PRE),
        compiler_params=room(20),
        name="attend_own",
    )(ask, rows, state[0], state[1], *parts, *pays)


def join_kernel(o_ref, m_ref, msg_ref, out_ref):
    far = msg_ref[HD + 1 : HD + 2, :]
    near = m_ref[0:1, :]
    top = jnp.maximum(near, far)
    wa, wb = jnp.exp(near - top), jnp.exp(far - top)
    total = o_ref[: HD + 8, :] * wa + msg_ref[...] * wb
    mixed = total[:HD, :] / total[HD : HD + 1, :]
    both = jnp.concatenate([mixed[:, :TD], mixed[:, TD:]], axis=0)
    out_ref[...] = jnp.transpose(both).astype(BF)


def mix_kernel(
    att_ref, tok_hbm, gain_ref, route_ref, weight_ref, w0, w1, w2, w3, w4, res_ref, xi_ref, tok, sem
):
    tp = lax.axis_index("tp")
    fetch = pltpu.make_async_copy(
        tok_hbm.at[pl.ds(pl.multiple_of(tp * ROWS, ROWS), ROWS), :], tok, sem
    )
    fetch.start()
    q, z = tp // 4, lax.rem(tp, 4)
    side = 1 + 2 * place()[2]
    back = [0, side, 4 - side, 2]
    total = jnp.zeros((ROWS, 1024), F32)
    for j in range(4):
        row = lax.rem(z - back[j] + 4, 4)
        pair = jnp.concatenate([att_ref[q * 4 + row], att_ref[(1 - q) * 4 + row]], axis=1)
        w = jnp.concatenate([w0[0], w1[0]], axis=0) if j == 0 else (w2, w3, w4)[j - 1][...].reshape(256, 1024)
        total = total + jnp.dot(pair, w, preferred_element_type=F32)
    line = lax.broadcasted_iota(jnp.int32, (128, ROWS), 0)
    table = jnp.zeros((128, ROWS), F32)
    for k in range(8):
        expert = route_ref[k : k + 1, :]
        weight = weight_ref[k : k + 1, :]
        high = weight.astype(BF).astype(F32)
        table = table + jnp.where(line == expert, high, 0.0)
        table = table + jnp.where(line == expert + 32, weight - high, 0.0)
    gates = jnp.transpose(table).astype(BF)
    fetch.wait()
    total = tok[...].astype(F32) + total
    res_ref[...] = total
    xi = rms(total, gain_ref[...]).astype(BF)
    for j in range(8):
        xi_ref[j, :, :1024] = xi
        xi_ref[j, :, 1024:] = gates


def mix_call(att, tokens, gain, routes, weights, ws):
    return pl.pallas_call(
        mix_kernel,
        in_specs=[VM, HBM] + [VM] * 8,
        out_specs=[VM, VM],
        out_shape=[
            jax.ShapeDtypeStruct((ROWS, 1024), F32),
            jax.ShapeDtypeStruct((8, ROWS, 1152), BF),
        ],
        scratch_shapes=[pltpu.VMEM((ROWS, 1024), BF), pltpu.SemaphoreType.DMA],
        compiler_params=room(12),
        name="mix",
    )(att, tokens, gain, routes, weights, *ws)


def expert_kernel(x_ref, wi_own, wi_peer, wo_own, wo_peer, out_ref, acc):
    x, y, c = place()
    for e in range(4):
        wi, wo = ((wi_own, wo_own), (wi_peer, wo_peer))[e // 2]
        number = (x * 8 + y * 2 + (c if e < 2 else 1 - c)) * 2 + e % 2

        def half(h, _):
            rows = pl.ds(h * 512, 512)
            joined = jnp.dot(x_ref[rows, :1024], wi[e % 2], preferred_element_type=F32)
            g = joined[:, :512]
            hidden = (g / (1.0 + jnp.exp(-g)) * joined[:, 512:]).astype(BF)
            o = jnp.dot(hidden, wo[e % 2], preferred_element_type=F32).astype(BF).astype(F32)
            lane = lax.broadcasted_iota(jnp.int32, (512, 128), 1)
            hit = (lane == number) | (lane == number + 32)
            table = x_ref[rows, 1024:].astype(F32)
            gate = jnp.sum(jnp.where(hit, table, 0.0), axis=1, keepdims=True)
            o = o * gate
            if e:
                o = acc[rows, :] + o
            if e < 3:
                acc[rows, :] = o
            else:
                out_ref[rows, :] = o.astype(BF)
            return 0

        half(0, 0)


def expert_call(x, wi_own, wi_peer, wo_own, wo_peer):
    return pl.pallas_call(
        expert_kernel,
        in_specs=[VM] * 5,
        out_specs=VM,
        scratch_shapes=[pltpu.VMEM((512, 1024), F32)],
        out_shape=jax.ShapeDtypeStruct((512, 1024), BF),
        compiler_params=room(EXPERT_ROOM),
        name="experts",
    )(x, wi_own, wi_peer, wo_own, wo_peer)


EXPERT_ROOM = 30


def body(
    tokens,
    segment_ids,
    prefix_cache,
    norm1_gain,
    w_qkv,
    w_out,
    norm2_gain,
    expert_in,
    expert_out,
    routes,
    route_weights,
):
    tie = lax.optimization_barrier

    def swap(v):
        return lax.ppermute(v, "seq", CORE)

    def across(v):
        return lax.ppermute(v, "seq", ACROSS)

    def round_y(v):
        return [
            lax.ppermute(v, "seq", seq_perm(lambda a, b, d, k=k: (a, (b + k) % 4, d)))
            for k in TURNS
        ]

    pre = prefix_cache.reshape(PRE, 128)
    wx = lax.ppermute(w_out, "tp", tp_perm(lambda a, b: (1 - a, b)))
    far_pre = round_y(pre)
    near_pre = [swap(pre)]
    pay, ask, rows, new = pl.pallas_call(
        project_kernel,
        out_shape=[
            jax.ShapeDtypeStruct((PAY, 128), BF),
            jax.ShapeDtypeStruct((PAY, 128), BF),
            jax.ShapeDtypeStruct((8, NQ), F32),
            jax.ShapeDtypeStruct((TD, 128), BF),
        ],
        in_specs=[FAR] * 4,
        scratch_shapes=[
            pltpu.VMEM((TD, 1024), BF),
            pltpu.VMEM((1, 1024), F32),
            pltpu.VMEM((1024, 256), BF),
            pltpu.VMEM((4, 128), jnp.int32),
            pltpu.SemaphoreType.DMA((7,)),
        ],
        cost_estimate=pl.CostEstimate(
            flops=2 * TD * 1024 * 256, bytes_accessed=2 << 20, transcendentals=TD
        ),
        name="project",
    )(tokens, norm1_gain[None, :], w_qkv.reshape(1024, 256), segment_ids.reshape(4, 128))
    asked = across(ask)
    first = begin_call(ask, [pre, near_pre[0]])

    far_pre, asked, first, pay = tie((far_pre, asked, first, pay))
    near_pre += [swap(v) for v in far_pre]
    near_new = [swap(pay)]
    near_new, pay = tie((near_new, pay))
    far_new = round_y(pay)
    wpair = jnp.concatenate([w_out, wx])
    side = lax.ppermute(wpair, ("seq", "tp"), SIDES)
    opposite = lax.ppermute(wpair, "tp", tp_perm(lambda a, b: (a, (b + 2) % 4)))
    shards = [v for p in zip([pre] + far_pre, near_pre) for v in p]
    second = begin_call(asked, shards)

    far_new, second = tie((far_new, second))
    near_new += [swap(v) for v in far_new]
    pays = [v for p in zip([pay] + far_new, near_new) for v in p]
    message, *first = partner_call(asked, ask, rows, second, first, pays)

    side, opposite, near_new, message, first, expert_in_t, expert_out_t = tie(
        (side, opposite, near_new, message, first, expert_in, expert_out)
    )
    wz = [side, swap(side), opposite]
    returned = across(message)
    wi_peer = swap(expert_in_t)
    wo_peer = swap(expert_out_t)
    o, m = own_call(ask, rows, first, shards[2:], pays)
    attended = pl.pallas_call(
        join_kernel, out_shape=jax.ShapeDtypeStruct((TD, 128), BF), compiler_params=room(8), name="join"
    )(o, m, returned)

    spread = lax.all_to_all(attended.reshape(8, ROWS, 128), "tp", 0, 0, tiled=True)
    residual, copies = mix_call(
        spread,
        tokens,
        norm2_gain[None, :],
        jnp.transpose(routes),
        jnp.transpose(route_weights),
        [w_out, wx] + wz,
    )
    everyone = lax.all_to_all(copies, "seq", 0, 0, axis_index_groups=CHIP_GROUPS, tiled=True)
    partial = expert_call(
        everyone.reshape(512, 1152), expert_in, wi_peer, expert_out, wo_peer
    )
    back = lax.all_to_all(
        partial.reshape(8, ROWS, 1024), "seq", 0, 0, axis_index_groups=CHIP_GROUPS, tiled=True
    )
    hidden = (residual + jnp.sum(back.astype(F32), axis=0)).astype(BF)
    return hidden, new.reshape(TD, 1, 128)


def solution(mesh):
    in_specs = (
        P("seq", None),
        P("seq"),
        P("seq", "tp", None),
        P(),
        P(None, "tp", None),
        P("tp", None, None),
        P(),
        P("seq", None, None),
        P("seq", None, None),
        P(("seq", "tp"), None),
        P(("seq", "tp"), None),
    )
    out_specs = (P(("seq", "tp"), None), P("seq", "tp", None))
    return jax.shard_map(body, mesh=mesh, in_specs=in_specs, out_specs=out_specs, check_vma=False)
```

```python
import functools

import jax
import jax.numpy as jnp
from jax import lax
from jax.experimental import pallas as pl
from jax.experimental.pallas import tpu as pltpu
from jax.sharding import PartitionSpec as P

SCALE = 0.015625
EPS = 1e-06
HD = 64
NV = 80
TD = 512
PRE = 1024
ROWS = 64
TQ = 1024
NQ = 2 * TD
SEG_AT = TD
PAY = SEG_AT + 16
MSG = 72
LIMIT = 1e26
NEG = -1e30
NT = (((1,), (1,)), ((), ()))
F32 = jnp.float32
BF = jnp.bfloat16


def seq_perm(move):
    return [
        (x * 8 + y * 2 + c, (lambda t: t[0] * 8 + t[1] * 2 + t[2])(move(x, y, c)))
        for x in range(2)
        for y in range(4)
        for c in range(2)
    ]


def tp_perm(move):
    return [(q * 4 + z, (lambda t: t[0] * 4 + t[1])(move(q, z))) for q in range(2) for z in range(4)]


CORE = seq_perm(lambda x, y, c: (x, y, 1 - c))
ACROSS = seq_perm(lambda x, y, c: (1 - x, y, c))
TURNS = (1, 3, 2)
SIDES = [
    (s * 8 + q * 4 + z, s * 8 + q * 4 + (z + (1 if s % 2 == 0 else 3)) % 4)
    for s in range(16)
    for q in range(2)
    for z in range(4)
]
CHIP_GROUPS = [[x * 8 + y * 2 + c for x in range(2) for y in range(4)] for c in range(2)]


def room(mib):
    return pltpu.CompilerParams(vmem_limit_bytes=mib << 20)


def rms(wide, gain):
    mean_square = jnp.mean(wide * wide, axis=-1, keepdims=True)
    return wide * lax.rsqrt(mean_square + EPS) * gain


def project_kernel(
    tok_hbm, gain_hbm, w_hbm, seg_hbm, pay_ref, ask_ref, row_ref, new_ref, tok, gain, w, seg_in, sem
):
    small = [
        pltpu.make_async_copy(w_hbm, w, sem.at[4]),
        pltpu.make_async_copy(gain_hbm, gain, sem.at[5]),
        pltpu.make_async_copy(seg_hbm, seg_in, sem.at[6]),
    ]
    large = [
        pltpu.make_async_copy(tok_hbm.at[pl.ds(i * 128, 128), :], tok.at[pl.ds(i * 128, 128), :], sem.at[i])
        for i in range(4)
    ]
    for v in [large[0]] + small + large[1:]:
        v.start()
    for v in small:
        v.wait()
    seg = seg_in[...].astype(F32)
    segs = jnp.concatenate([seg, jnp.full((12, 128), -1.0, F32)], axis=0).astype(BF)
    pay_ref[SEG_AT:, :] = segs
    ask_ref[SEG_AT:, :] = segs
    row = jnp.concatenate([seg[k : k + 1, :] for k in range(4)], axis=1)
    col = jnp.transpose(jnp.broadcast_to(row, (8, TD)))[:, 0:1]
    below = jnp.sum(jnp.where(col < row, 1.0, 0.0), axis=0, keepdims=True)
    row_ref[0:1, :] = jnp.concatenate([below, below], axis=1)
    row_ref[1:2, :] = jnp.concatenate([row, row], axis=1)
    for i in range(2):
        large[2 * i].wait()
        large[2 * i + 1].wait()
        rows = pl.ds(i * 256, 256)
        normed = rms(tok[rows, :].astype(F32), gain[...]).astype(BF)
        proj = jnp.dot(normed, w[...], preferred_element_type=F32)
        ask_ref[rows, :] = (proj[:, :128].astype(BF).astype(F32) * SCALE).astype(BF)
        new = proj[:, 128:].astype(BF)
        new_ref[rows, :] = new
        pay_ref[rows, :] = new


def values_t(kv):
    row = lax.broadcasted_iota(jnp.int32, (NV, 128), 0)
    col = lax.broadcasted_iota(jnp.int32, (NV, 128), 1)
    pick = jnp.where((col == row + HD) & (row < HD), 1.0, 0.0).astype(BF)
    vt = lax.dot_general(pick, kv, NT, preferred_element_type=F32)
    ones = lax.broadcasted_iota(jnp.int32, vt.shape, 0) >= HD
    return jnp.where(ones, 1.0, vt).astype(BF)


def online_step(q, kv, o_ref, m_ref, cols, mask):
    s = lax.dot_general(kv, q, NT, preferred_element_type=F32)
    if mask is not None:
        s = jnp.where(mask, s, NEG)
    m0 = m_ref[0:1, cols]
    m1 = jnp.maximum(m0, jnp.max(s, axis=0, keepdims=True))
    p = jnp.exp(s - m1).astype(BF)
    o_ref[:, cols] = o_ref[:, cols] * jnp.exp(m0 - m1) + jnp.dot(
        values_t(kv), p, preferred_element_type=F32
    )
    m_ref[0:1, cols] = m1


def spread_heads(stage, q_ref):
    wide = stage[...].astype(F32)
    low = lax.broadcasted_iota(jnp.int32, (TD, 128), 1) < HD
    q_ref[:TD, :] = jnp.where(low, wide, 0.0).astype(BF)
    q_ref[TD:, :] = jnp.where(low, pltpu.roll(wide, HD, 1), 0.0).astype(BF)


def fetch_all(pairs, sem):
    copies = [pltpu.make_async_copy(a, b, sem.at[i]) for i, (a, b) in enumerate(pairs)]
    for v in copies:
        v.start()
    return copies


def add_block(kv, q_ref, o_ref, m_ref, mask, level=0):
    vt = values_t(kv)
    for t in range(NQ // TQ):
        cols = pl.ds(t * TQ, TQ)
        s = lax.dot_general(kv, q_ref[cols, :], NT, preferred_element_type=F32)
        if mask is not None:
            s = jnp.where(mask(t * TQ, TQ), s, NEG)
        p = jnp.exp(s - m_ref[level : level + 1, cols]).astype(BF)
        o_ref[:, cols] = o_ref[:, cols] + jnp.dot(vt, p, preferred_element_type=F32)


def too_large(o_ref):
    return jnp.logical_not(jnp.max(o_ref[HD : HD + 1, :]) < LIMIT)


def add_prefix(count, buf, sem, q_ref, o_ref, m_ref, head):
    def wait(j):
        pltpu.make_async_copy(buf.at[0], buf.at[j], sem.at[j]).wait()

    def block(j, _):
        if head:
            pl.when(j > 0)(lambda: wait(j))
        else:
            wait(j)
        add_block(buf[j], q_ref, o_ref, m_ref, None)
        return 0

    lax.fori_loop(0, count, block, 0, unroll=4 if count == 8 else 2)


def again_prefix(count, buf, q_ref, o_ref, m_ref):
    def again(i, _):
        kv = buf[i // 4, pl.ds(pl.multiple_of(i % 4 * 256, 256), 256), :]
        for t in range(NQ // 256):
            cols = pl.ds(t * 256, 256)
            online_step(q_ref[cols, :], kv, o_ref, m_ref, cols, None)
        return 0

    lax.fori_loop(0, count * 4, again, 0)


def masker(start, last, at, size):
    def mask(t, width):
        key = at + lax.broadcasted_iota(jnp.int32, (size, width), 0)
        ok = key >= start[:, t : t + width]
        return ok if last is None else ok & (key <= last[:, t : t + width])

    return mask


def add_suffix(low, end, diagonal, start, last, reach, buf, q_ref, o_ref, m_ref):
    m_ref[1:2, :] = jnp.where(reach, m_ref[0:1, :], -NEG)

    def block(at, size, masked, level=0):
        at = pl.multiple_of(at, TD)
        bound = last if masked == "both" else None
        mask = masker(start, bound, at, size) if masked else None
        add_block(buf[pl.ds(at, size), :], q_ref, o_ref, m_ref, mask, level)

    pl.when(low < end)(lambda: block(low * TD, TD, "start"))
    pl.when(diagonal)(lambda: block(end * TD, TD, "both"))
    between = jnp.maximum(end - 1 - low, 0)
    split = lax.rem(between, 2)
    pl.when(split == 1)(lambda: block((low + 1) * TD, TD, None, 1))

    def fully(b, _):
        block((low + 1 + split + 2 * b) * TD, 2 * TD, None, 1)
        return 0

    lax.fori_loop(0, between // 2, fully, 0)


def again_suffix(low, end, start, last, buf, q_ref, o_ref, m_ref):
    def again(i, _):
        at = pl.multiple_of(i * 256, 256)
        kv = buf[pl.ds(at, 256), :]
        mask = masker(start, last, at, 256)
        for t in range(4):
            online_step(
                q_ref[pl.ds(t * 256, 256), :], kv, o_ref, m_ref, pl.ds(t * 256, 256), mask(t * 256, 256)
            )
        return 0

    lax.fori_loop(low * 2, end * 2, again, 0)


def place():
    seq = lax.axis_index("seq")
    return seq // 8, lax.rem(seq // 2, 4), lax.rem(seq, 2)


def half_sources():
    x, y, c = place()
    rows = [y] + [lax.rem(y - k + 4, 4) for k in TURNS]
    return [r * 2 + d for r in rows for d in (c, 1 - c)]


def news_pairs(pays, buf, segs):
    src = half_sources()
    out = [(pays[j].at[pl.ds(SEG_AT, 16), :], segs.at[j]) for j in range(8)]
    for j in range(8):
        at = pl.multiple_of(src[j] * TD, TD)
        out.append((pays[j].at[pl.ds(0, TD), :], buf.at[pl.ds(at, TD), :]))
    return out


def count_same(segs, number, keep):
    total = jnp.zeros((16, 128), F32)
    for j in range(8):
        hit = segs[j].astype(F32) == jnp.where(keep[j], number, -2.0)
        total = total + jnp.where(hit, 1.0, 0.0)
    return jnp.sum(total).astype(jnp.int32)


def begin_kernel(ask_hbm, *refs, count):
    parts = refs[:count]
    o_ref, m_ref, stage, q_ref, buf, sem = refs[count:]
    copies = fetch_all(
        [(parts[j], buf.at[j]) for j in range(count)] + [(ask_hbm.at[pl.ds(0, TD), :], stage)], sem
    )
    o_ref[...] = jnp.zeros_like(o_ref)
    copies[count].wait()
    spread_heads(stage, q_ref)
    copies[0].wait()
    s = lax.dot_general(buf[0, :256, :], q_ref[...], NT, preferred_element_type=F32)
    m_ref[...] = jnp.broadcast_to(jnp.max(s, axis=0, keepdims=True), m_ref.shape)
    add_prefix(count, buf, sem, q_ref, o_ref, m_ref, True)

    @pl.when(too_large(o_ref))
    def _():
        o_ref[...] = jnp.zeros_like(o_ref)
        m_ref[...] = jnp.full_like(m_ref, NEG)
        again_prefix(count, buf, q_ref, o_ref, m_ref)


VM = pl.BlockSpec(memory_space=pltpu.VMEM)
HBM = pl.BlockSpec(memory_space=pl.ANY)
FAR = pl.BlockSpec(memory_space=pltpu.HBM)
STATE = [jax.ShapeDtypeStruct((NV, NQ), F32), jax.ShapeDtypeStruct((8, NQ), F32)]
ASK = [pltpu.VMEM((TD, 128), BF), pltpu.VMEM((NQ, 128), BF)]


def price(keys):
    return pl.CostEstimate(
        flops=keys * NQ * 2 * 600, bytes_accessed=keys * 256, transcendentals=keys * NQ
    )


def begin_call(ask, parts):
    count = len(parts)
    return pl.pallas_call(
        functools.partial(begin_kernel, count=count),
        in_specs=[HBM, FAR] + [HBM] * (count - 1),
        out_specs=[VM, VM],
        out_shape=STATE,
        scratch_shapes=ASK
        + [pltpu.VMEM((count, PRE, 128), BF), pltpu.SemaphoreType.DMA((count + 1,))],
        cost_estimate=price(count * PRE),
        compiler_params=room(20),
        name="attend_prefix",
    )(ask, *parts)


def own_terms(row_ref, segs, own):
    row = row_ref[1:2, :]
    mine = jnp.max(jnp.where(lax.broadcasted_iota(jnp.int32, (1, NQ), 1) == 0, row, -1.0))
    begin = own * TD - count_same(segs, mine, [v < own for v in half_sources()])
    start = jnp.where(row == mine, begin, row_ref[0:1, :].astype(jnp.int32) + own * TD)
    lane = lax.broadcasted_iota(jnp.int32, (1, NQ), 1)
    last = own * TD + jnp.where(lane >= TD, lane - TD, lane)
    return start, last, jnp.where(row == mine, 1, 0), begin // TD


def partner_terms(marks, segs):
    newest = segs[0].astype(F32)
    for j in range(1, 8):
        newest = jnp.maximum(newest, segs[j].astype(F32))
    newest = jnp.max(newest)
    begin = 8 * TD - count_same(segs, newest, [True] * 8)
    seg = marks[...].astype(F32)
    row = jnp.concatenate([seg[k : k + 1, :] for k in range(4)], axis=1)
    row = jnp.concatenate([row, row], axis=1)
    start = jnp.where(row == newest, begin, 8 * TD)
    last = jnp.full((1, NQ), 8 * TD, jnp.int32)
    return start, last, jnp.where(row == newest, 1, 0), jnp.min(start) // TD


def partner_kernel(ask_hbm, own_hbm, row_ref, o_in, m_in, o_own, m_own, *refs):
    pays = refs[:8]
    out_ref, o_out, m_out, stage, marks, q_ref, o_ref, m_ref, buf, segs, sem = refs[8:]
    x, y, c = place()
    own = y * 2 + c
    early = x == 0
    asked = pltpu.make_async_copy(ask_hbm.at[pl.ds(0, TD), :], stage, sem.at[17])
    mine = pltpu.make_async_copy(own_hbm.at[pl.ds(0, TD), :], stage, sem.at[17])
    pl.when(early)(lambda: asked.start())
    pl.when(jnp.logical_not(early))(lambda: mine.start())
    copies = fetch_all(
        news_pairs(pays, buf, segs) + [(ask_hbm.at[pl.ds(SEG_AT, 16), :], marks)], sem
    )

    def load():
        @pl.when(early)
        def _():
            o_ref[...] = o_in[...]
            m_ref[...] = m_in[...]

        @pl.when(jnp.logical_not(early))
        def _():
            o_ref[...] = o_own[...]
            m_ref[...] = m_own[...]

    load()
    for v in copies[:8] + copies[16:]:
        v.wait()
    asked.wait()
    spread_heads(stage, q_ref)
    theirs, ours = partner_terms(marks, segs), own_terms(row_ref, segs, own)
    start, last, reach, low = [jnp.where(early, a, b) for a, b in zip(theirs, ours)]
    end = jnp.where(early, 8, own)
    for v in copies[8:16]:
        v.wait()
    add_suffix(low, end, x == 1, start, last, reach == 1, buf, q_ref, o_ref, m_ref)

    @pl.when(too_large(o_ref))
    def _():
        load()
        again_suffix(low, end + x, start, last, buf, q_ref, o_ref, m_ref)

    first = lax.broadcasted_iota(jnp.int32, (8, NQ), 0) == 0

    def tell(o, m):
        out_ref[:HD, :] = o[:HD, :]
        out_ref[HD:, :] = jnp.where(first, o[HD : HD + 1, :], m[0:1, :])

    @pl.when(early)
    def _():
        tell(o_ref, m_ref)
        o_out[...] = o_own[...]
        m_out[...] = m_own[...]

    @pl.when(jnp.logical_not(early))
    def _():
        tell(o_in, m_in)
        o_out[...] = o_ref[...]
        m_out[...] = m_ref[...]


def partner_call(ask, own_ask, rows, state, own_state, pays):
    return pl.pallas_call(
        partner_kernel,
        in_specs=[HBM, HBM] + [VM] * 5 + [HBM] * 8,
        out_specs=[VM] * 3,
        out_shape=[jax.ShapeDtypeStruct((MSG, NQ), F32)] + STATE,
        scratch_shapes=[
            ASK[0],
            pltpu.VMEM((16, 128), BF),
            ASK[1],
            pltpu.VMEM((NV, NQ), F32),
            pltpu.VMEM((8, NQ), F32),
            pltpu.VMEM((8 * TD, 128), BF),
            pltpu.VMEM((8, 16, 128), BF),
            pltpu.SemaphoreType.DMA((18,)),
        ],
        cost_estimate=price(3 * TD),
        compiler_params=room(20),
        name="attend_partner",
    )(ask, own_ask, rows, *state, *own_state, *pays)


def own_kernel(ask_hbm, row_ref, o_in, m_in, *refs):
    parts = refs[:6]
    pays = refs[6:14]
    out_ref, top_ref, stage, q_ref, o_ref, m_ref, pre, buf, segs, sem, pre_sem = refs[14:]
    x, y, c = place()
    own = y * 2 + c
    asked = pltpu.make_async_copy(ask_hbm.at[pl.ds(0, TD), :], stage, sem.at[16])
    asked.start()
    fetch_all([(parts[j], pre.at[j]) for j in range(6)], pre_sem)
    copies = [
        pltpu.make_async_copy(a, b, sem.at[i])
        for i, (a, b) in enumerate(news_pairs(pays, buf, segs))
    ]

    @pl.when(x == 0)
    def _():
        for v in copies:
            v.start()

    o_ref[...] = o_in[...]
    m_ref[...] = m_in[...]
    asked.wait()
    spread_heads(stage, q_ref)
    add_prefix(6, pre, pre_sem, q_ref, o_ref, m_ref, False)

    @pl.when(x == 0)
    def _():
        for v in copies:
            v.wait()
        start, last, reach, low = own_terms(row_ref, segs, own)
        add_suffix(low, own, x == 0, start, last, reach == 1, buf, q_ref, o_ref, m_ref)

    @pl.when(too_large(o_ref))
    def _():
        o_ref[...] = o_in[...]
        m_ref[...] = m_in[...]
        again_prefix(6, pre, q_ref, o_ref, m_ref)

        @pl.when(x == 0)
        def _():
            start, last, reach, low = own_terms(row_ref, segs, own)
            again_suffix(low, own + 1, start, last, buf, q_ref, o_ref, m_ref)

    out_ref[...] = o_ref[...]
    top_ref[...] = m_ref[...]


def own_call(ask, rows, state, parts, pays):
    return pl.pallas_call(
        own_kernel,
        in_specs=[HBM, VM, VM, VM] + [HBM] * 14,
        out_specs=[VM, VM],
        out_shape=STATE,
        scratch_shapes=ASK
        + [
            pltpu.VMEM((NV, NQ), F32),
            pltpu.VMEM((8, NQ), F32),
            pltpu.VMEM((6, PRE, 128), BF),
            pltpu.VMEM((8 * TD, 128), BF),
            pltpu.VMEM((8, 16, 128), BF),
            pltpu.SemaphoreType.DMA((17,)),
            pltpu.SemaphoreType.DMA((6,)),
        ],
        cost_estimate=price(9 * PRE),
        compiler_params=room(20),
        name="attend_own",
    )(ask, rows, state[0], state[1], *parts, *pays)


def join_kernel(o_ref, m_ref, msg_ref, out_ref):
    far = msg_ref[HD + 1 : HD + 2, :]
    near = m_ref[0:1, :]
    top = jnp.maximum(near, far)
    wa, wb = jnp.exp(near - top), jnp.exp(far - top)
    total = o_ref[: HD + 8, :] * wa + msg_ref[...] * wb
    mixed = total[:HD, :] / total[HD : HD + 1, :]
    both = jnp.concatenate([mixed[:, :TD], mixed[:, TD:]], axis=0)
    out_ref[...] = jnp.transpose(both).astype(BF)


def mix_kernel(
    att_ref, tok_hbm, gain_ref, route_ref, weight_ref, w0, w1, w2, w3, w4, res_ref, xi_ref, tok, sem
):
    tp = lax.axis_index("tp")
    fetch = pltpu.make_async_copy(
        tok_hbm.at[pl.ds(pl.multiple_of(tp * ROWS, ROWS), ROWS), :], tok, sem
    )
    fetch.start()
    q, z = tp // 4, lax.rem(tp, 4)
    side = 1 + 2 * place()[2]
    back = [0, side, 4 - side, 2]
    total = jnp.zeros((ROWS, 1024), F32)
    for j in range(4):
        row = lax.rem(z - back[j] + 4, 4)
        pair = jnp.concatenate([att_ref[q * 4 + row], att_ref[(1 - q) * 4 + row]], axis=1)
        w = jnp.concatenate([w0[0], w1[0]], axis=0) if j == 0 else (w2, w3, w4)[j - 1][...].reshape(256, 1024)
        total = total + jnp.dot(pair, w, preferred_element_type=F32)
    line = lax.broadcasted_iota(jnp.int32, (128, ROWS), 0)
    table = jnp.zeros((128, ROWS), F32)
    for k in range(8):
        expert = route_ref[k : k + 1, :]
        weight = weight_ref[k : k + 1, :]
        high = weight.astype(BF).astype(F32)
        table = table + jnp.where(line == expert, high, 0.0)
        table = table + jnp.where(line == expert + 32, weight - high, 0.0)
    gates = jnp.transpose(table).astype(BF)
    fetch.wait()
    total = tok[...].astype(F32) + total
    res_ref[...] = total
    xi = rms(total, gain_ref[...]).astype(BF)
    for j in range(8):
        xi_ref[j, :, :1024] = xi
        xi_ref[j, :, 1024:] = gates


def mix_call(att, tokens, gain, routes, weights, ws):
    return pl.pallas_call(
        mix_kernel,
        in_specs=[VM, HBM] + [VM] * 8,
        out_specs=[VM, VM],
        out_shape=[
            jax.ShapeDtypeStruct((ROWS, 1024), F32),
            jax.ShapeDtypeStruct((8, ROWS, 1152), BF),
        ],
        scratch_shapes=[pltpu.VMEM((ROWS, 1024), BF), pltpu.SemaphoreType.DMA],
        compiler_params=room(12),
        name="mix",
    )(att, tokens, gain, routes, weights, *ws)


def expert_kernel(x_ref, wi_own, wi_peer, wo_own, wo_peer, out_ref, acc):
    x, y, c = place()
    for e in range(4):
        wi, wo = ((wi_own, wo_own), (wi_peer, wo_peer))[e // 2]
        number = (x * 8 + y * 2 + (c if e < 2 else 1 - c)) * 2 + e % 2

        def half(h, _):
            rows = pl.ds(h * 512, 512)
            joined = jnp.dot(x_ref[rows, :1024], wi[e % 2], preferred_element_type=F32)
            g = joined[:, :512]
            hidden = (g / (1.0 + jnp.exp(-g)) * joined[:, 512:]).astype(BF)
            o = jnp.dot(hidden, wo[e % 2], preferred_element_type=F32).astype(BF).astype(F32)
            lane = lax.broadcasted_iota(jnp.int32, (512, 128), 1)
            hit = (lane == number) | (lane == number + 32)
            table = x_ref[rows, 1024:].astype(F32)
            gate = jnp.sum(jnp.where(hit, table, 0.0), axis=1, keepdims=True)
            o = o * gate
            if e:
                o = acc[rows, :] + o
            if e < 3:
                acc[rows, :] = o
            else:
                out_ref[rows, :] = o.astype(BF)
            return 0

        half(0, 0)


def expert_call(x, wi_own, wi_peer, wo_own, wo_peer):
    return pl.pallas_call(
        expert_kernel,
        in_specs=[VM] * 5,
        out_specs=VM,
        scratch_shapes=[pltpu.VMEM((512, 1024), F32)],
        out_shape=jax.ShapeDtypeStruct((512, 1024), BF),
        compiler_params=room(EXPERT_ROOM),
        name="experts",
    )(x, wi_own, wi_peer, wo_own, wo_peer)


EXPERT_ROOM = 30


def body(
    tokens,
    segment_ids,
    prefix_cache,
    norm1_gain,
    w_qkv,
    w_out,
    norm2_gain,
    expert_in,
    expert_out,
    routes,
    route_weights,
):
    tie = lax.optimization_barrier

    def swap(v):
        return lax.ppermute(v, "seq", CORE)

    def across(v):
        return lax.ppermute(v, "seq", ACROSS)

    def round_y(v):
        return [
            lax.ppermute(v, "seq", seq_perm(lambda a, b, d, k=k: (a, (b + k) % 4, d)))
            for k in TURNS
        ]

    pre = prefix_cache.reshape(PRE, 128)
    wx = lax.ppermute(w_out, "tp", tp_perm(lambda a, b: (1 - a, b)))
    far_pre = round_y(pre)
    near_pre = [swap(pre)]
    pay, ask, rows, new = pl.pallas_call(
        project_kernel,
        out_shape=[
            jax.ShapeDtypeStruct((PAY, 128), BF),
            jax.ShapeDtypeStruct((PAY, 128), BF),
            jax.ShapeDtypeStruct((8, NQ), F32),
            jax.ShapeDtypeStruct((TD, 128), BF),
        ],
        in_specs=[FAR] * 4,
        scratch_shapes=[
            pltpu.VMEM((TD, 1024), BF),
            pltpu.VMEM((1, 1024), F32),
            pltpu.VMEM((1024, 256), BF),
            pltpu.VMEM((4, 128), jnp.int32),
            pltpu.SemaphoreType.DMA((7,)),
        ],
        cost_estimate=pl.CostEstimate(
            flops=2 * TD * 1024 * 256, bytes_accessed=2 << 20, transcendentals=TD
        ),
        name="project",
    )(tokens, norm1_gain[None, :], w_qkv.reshape(1024, 256), segment_ids.reshape(4, 128))
    asked = across(ask)
    first = begin_call(ask, [pre, near_pre[0]])

    far_pre, asked, first, pay = tie((far_pre, asked, first, pay))
    near_pre += [swap(v) for v in far_pre]
    near_new = [swap(pay)]
    near_new, pay = tie((near_new, pay))
    far_new = round_y(pay)
    wpair = jnp.concatenate([w_out, wx])
    side = lax.ppermute(wpair, ("seq", "tp"), SIDES)
    opposite = lax.ppermute(wpair, "tp", tp_perm(lambda a, b: (a, (b + 2) % 4)))
    shards = [v for p in zip([pre] + far_pre, near_pre) for v in p]
    second = begin_call(asked, shards)

    far_new, second = tie((far_new, second))
    near_new += [swap(v) for v in far_new]
    pays = [v for p in zip([pay] + far_new, near_new) for v in p]
    message, *first = partner_call(asked, ask, rows, second, first, pays)

    side, opposite, near_new, message, first, expert_in_t, expert_out_t = tie(
        (side, opposite, near_new, message, first, expert_in, expert_out)
    )
    wz = [side, swap(side), opposite]
    returned = across(message)
    wi_peer = swap(expert_in_t)
    wo_peer = swap(expert_out_t)
    o, m = own_call(ask, rows, first, shards[2:], pays)
    attended = pl.pallas_call(
        join_kernel, out_shape=jax.ShapeDtypeStruct((TD, 128), BF), compiler_params=room(8), name="join"
    )(o, m, returned)

    spread = lax.all_to_all(attended.reshape(8, ROWS, 128), "tp", 0, 0, tiled=True)
    residual, copies = mix_call(
        spread,
        tokens,
        norm2_gain[None, :],
        jnp.transpose(routes),
        jnp.transpose(route_weights),
        [w_out, wx] + wz,
    )
    everyone = lax.all_to_all(copies, "seq", 0, 0, axis_index_groups=CHIP_GROUPS, tiled=True)
    partial = expert_call(
        everyone.reshape(512, 1152), expert_in, wi_peer, expert_out, wo_peer
    )
    back = lax.all_to_all(
        partial.reshape(8, ROWS, 1024), "seq", 0, 0, axis_index_groups=CHIP_GROUPS, tiled=True
    )
    hidden = (residual + jnp.sum(back.astype(F32), axis=0)).astype(BF)
    return hidden, new.reshape(TD, 1, 128)


def solution(mesh):
    in_specs = (
        P("seq", None),
        P("seq"),
        P("seq", "tp", None),
        P(),
        P(None, "tp", None),
        P("tp", None, None),
        P(),
        P("seq", None, None),
        P("seq", None, None),
        P(("seq", "tp"), None),
        P(("seq", "tp"), None),
    )
    out_specs = (P(("seq", "tp"), None), P("seq", "tp", None))
    return jax.shard_map(body, mesh=mesh, in_specs=in_specs, out_specs=out_specs, check_vma=False)
```
